128 devices in a mesh: row: 16 (over y, x), col: 8 (over z, core).
Axes of the slice: x: 4, y: 4, z: 4, core: 2. Of those that a mesh axis runs over, the one named last changes fastest.
Arguments:
- embeddings: bfloat16 [65536, 1024], P('row'), may hold values from -6 to 6
- vectors: bfloat16 [64, 65536], P(None, ('row', 'col')), may hold values from -6 to 6
- block_pairs: int32 [3968, 2], replicated, may hold values from 0 to 127, as said below
Outputs:
- new_basis: float32 [64, 65536], P(None, ('row', 'col'))
The draws below stay inside these ranges and needn't reach their ends.
Inputs may be any that keep to these rules, and one draw needn't show every extreme that they name: `block_pairs`: no pair is listed twice, no pair has equal blocks, and every block occurs as a row block at least once.
All inputs are finite; a program needn't handle non-finite values.
Results may differ from the reference program's by a relative error of at most 0.0032.
Values may be sent and summed in bfloat16 or wider, within the bound.
No kernel may reach another device: no remote copies, remote signals or barrier semaphores. Data moves between devices by JAX's collectives and lax.ppermute only.
A program may use at most 128 MiB of HBM per device.

```python
import math
import jax
import jax.numpy as jnp
from jax import lax

BLOCK = 512
WIDTH = 1024
EIGS = 64
NBLOCKS = 128
NROWS = 65536
NPAIRS = 3968


def draw_block_pairs(key, part):
    total = NBLOCKS * NBLOCKS
    index = jnp.arange(total, dtype=jnp.int32)
    row_of = index // NBLOCKS
    col_of = index % NBLOCKS
    level = jnp.arange(NBLOCKS, dtype=jnp.int32) * 4 // NBLOCKS
    noise = jax.random.randint(key, (total,), 0, 4096, dtype=jnp.int32)
    score = noise * (1 + level[row_of] + level[col_of])
    forced = (col_of == (row_of + 1) % NBLOCKS) | (col_of == (row_of + NBLOCKS // 2) % NBLOCKS)
    score = jnp.where(forced, 65535, score)
    score = jnp.where(row_of == col_of, -1, score)
    keyed = score * total + index
    chosen = lax.top_k(keyed, NPAIRS)[1]
    return jnp.stack([row_of[chosen], col_of[chosen]], axis=1).astype(jnp.int32)


def shard_levels(own_key, shape, shards, low, high):
    factor_of, own = 1.0, jax.random.fold_in(own_key, 6)
    for axis_at, parts in shards:
        heights = jnp.exp(jax.random.uniform(jax.random.fold_in(own, axis_at), (parts,), jnp.float32, low / len(shards), high / len(shards)))
        factor_of = factor_of * jnp.repeat(heights, shape[axis_at] // parts).reshape([-1 if axis == axis_at else 1 for axis in range(len(shape))])
    return factor_of


def gaussian(stream_key, extent, spread, limit, pieces=(), held_as=jnp.bfloat16):
    factor_of = shard_levels(stream_key, extent, pieces, -0.22, 0.18) if pieces else 1.0
    result = jax.random.normal(stream_key, extent, jnp.float32) * spread * factor_of
    return jnp.minimum(jnp.maximum(result, -limit), limit).astype(held_as)


def setup_inputs(seed: int = 0) -> dict:
    key_list = jax.random.split(jax.random.key(seed), 4)
    return {
        "embeddings": gaussian(key_list[0], (NROWS, WIDTH), 1.0, 6.0, ((0, 16),)),
        "vectors": gaussian(key_list[1], (EIGS, NROWS), 1.0, 6.0, ((1, 128),)),
        "block_pairs": draw_block_pairs(jax.random.fold_in(key_list[3], 71), 0),
    }


def reference(embeddings, vectors, block_pairs):
    row_norms = lax.rsqrt(lax.optimization_barrier(jnp.mean(jnp.square(embeddings.astype(jnp.float32)), axis=1)) + 1e-06)

    def one_tile(running, pair_now):
        partial_sums, degree = running
        row_start = (pair_now[0] * BLOCK).astype(jnp.int32)
        col_start = (pair_now[1] * BLOCK).astype(jnp.int32)
        rows_x = lax.dynamic_slice_in_dim(embeddings, row_start, BLOCK, 0)
        cols_x = lax.dynamic_slice_in_dim(embeddings, col_start, BLOCK, 0)
        norm_rows = lax.dynamic_slice_in_dim(row_norms, row_start, BLOCK, 0)
        norm_cols = lax.dynamic_slice_in_dim(row_norms, col_start, BLOCK, 0)
        scores = jnp.dot(rows_x.astype(jnp.float32), cols_x.T.astype(jnp.float32), preferred_element_type=jnp.float32)
        affinity = jnp.exp(scores * norm_rows[:, None] * norm_cols[None, :] / math.sqrt(WIDTH))
        rounded = affinity.astype(jnp.bfloat16)
        cols_v = lax.dynamic_slice_in_dim(vectors, col_start, BLOCK, 1)
        contrib = jnp.dot(cols_v.astype(jnp.float32), rounded.T.astype(jnp.float32), preferred_element_type=jnp.float32)
        old_sums = lax.dynamic_slice_in_dim(partial_sums, row_start, BLOCK, 1)
        partial_sums = lax.dynamic_update_slice_in_dim(partial_sums, old_sums + contrib, row_start, 1)
        old_degree = lax.dynamic_slice_in_dim(degree, row_start, BLOCK, 0)
        degree = lax.dynamic_update_slice_in_dim(degree, old_degree + lax.optimization_barrier(jnp.sum(affinity, axis=1)), row_start, 0)
        return ((partial_sums, degree), None)
    start_sums = jnp.zeros((EIGS, NROWS), jnp.float32)
    start_degree = jnp.zeros((NROWS,), jnp.float32)
    (partial_sums, degree), unused = lax.scan(one_tile, (start_sums, start_degree), block_pairs)
    smoothed = partial_sums / degree[None, :]
    gram_matrix = jnp.dot(smoothed.astype(jnp.float32), smoothed.T.astype(jnp.float32), precision=lax.Precision.HIGHEST, preferred_element_type=jnp.float32) / NROWS
    factor = jnp.linalg.cholesky(gram_matrix)
    return lax.linalg.triangular_solve(factor, smoothed, left_side=True, lower=True)
```

```python
import functools
import math

import jax
import jax.numpy as jnp
from jax import lax
from jax.experimental import pallas as pl
from jax.experimental.pallas import tpu as pltpu
from jax.sharding import PartitionSpec as P

BLOCK = 512
WIDTH = 1024
EIGS = 64
NBLOCKS = 128
SIDE = 4
COLS = 8
CORES = 2
VROWS = BLOCK + EIGS // 2
PAYLOAD = VROWS + 16
ACC = EIGS + 8
SCALE = math.log2(math.e) / math.sqrt(WIDTH)
NT = (((1,), (1,)), ((), ()))


def shift(dy, dx, keep=None):
    pairs = []
    for y in range(SIDE):
        for x in range(SIDE):
            to_y, to_x = (y + dy) % SIDE, (x + dx) % SIDE
            if keep is None or keep(to_y, to_x):
                pairs.append((y * SIDE + x, to_y * SIDE + to_x))
    return pairs


def left_half(y, x):
    return x < SIDE // 2


def top_half(y, x):
    return y < SIDE // 2


STAGES = {
    "own": ((0, 0), None),
    "a": ((0, 1), None),
    "b": ((1, 0), None),
    "c": ((-1, -1), None),
    "d": ((-1, 1), None),
    "e": ((-1, -2), None),
    "g": ((0, 2), left_half),
    "h": ((2, 0), top_half),
    "f": ((2, 1), None),
    "k": ((2, 2), top_half),
}


def row_norm(x):
    return lax.rsqrt(jnp.sum(x * x, axis=1, keepdims=True) * (1.0 / WIDTH) + 1e-06)


def payload_kernel(index_ref, x_ref, v_ref, out_ref):
    x = x_ref[0]
    out_ref[0:BLOCK, :] = x
    half = EIGS // 2
    out_ref[BLOCK:VROWS, 0:BLOCK] = v_ref[0:half, :]
    out_ref[BLOCK:VROWS, BLOCK : 2 * BLOCK] = v_ref[half:EIGS, :]
    norms = jnp.broadcast_to(row_norm(x.astype(jnp.float32)) * SCALE, (BLOCK, 128))
    rows = norms.T[0:16, :]
    high = rows.astype(jnp.bfloat16)
    low = (rows - high.astype(jnp.float32)).astype(jnp.bfloat16)
    out_ref[VROWS:PAYLOAD, 0:BLOCK] = high
    out_ref[VROWS:PAYLOAD, BLOCK : 2 * BLOCK] = low


def make_payload(here_col, blocks, vectors):
    return pl.pallas_call(
        payload_kernel,
        out_shape=jax.ShapeDtypeStruct((PAYLOAD, WIDTH), jnp.bfloat16),
        grid_spec=pltpu.PrefetchScalarGridSpec(
            num_scalar_prefetch=1,
            grid=(1,),
            in_specs=[
                pl.BlockSpec((1, BLOCK, WIDTH), lambda g, index: (index[0], 0, 0)),
                pl.BlockSpec((EIGS, BLOCK), lambda g, index: (0, 0)),
            ],
            out_specs=pl.BlockSpec((PAYLOAD, WIDTH), lambda g, index: (0, 0)),
        ),
        name="payload",
    )(here_col, blocks, vectors)


def norms_kernel(x_ref, out_ref):
    out_ref[0] = jnp.broadcast_to(row_norm(x_ref[0].astype(jnp.float32)), (BLOCK, 128))


def local_norms(blocks):
    return pl.pallas_call(
        norms_kernel,
        out_shape=jax.ShapeDtypeStruct((COLS, BLOCK, 128), jnp.float32),
        grid=(COLS,),
        in_specs=[pl.BlockSpec((1, BLOCK, WIDTH), lambda g: (g, 0, 0))],
        out_specs=pl.BlockSpec((1, BLOCK, 128), lambda g: (g, 0, 0)),
        name="norms",
    )(blocks)


def cells_kernel(order_ref, flags_ref, x_ref, far_ref, v_ref, norm_ref, old_ref, new_ref, far_sums_ref, p_ref):
    step = pl.program_id(0)
    flag = flags_ref[step]
    ones = jnp.ones((16, BLOCK), jnp.bfloat16)

    @pl.when(step == 0)
    def _():
        far_sums_ref[...] = jnp.zeros_like(far_sums_ref)

    new_ref[...] = old_ref[...]

    @pl.when(flag > 0)
    def _():
        near = norm_ref[0]
        near = jnp.concatenate([near, near], axis=1)
        for at in range(0, BLOCK, 256):
            scores = lax.dot_general(
                x_ref[0], far_ref[at : at + 256, :], NT, preferred_element_type=jnp.float32
            )
            far = far_ref[VROWS : VROWS + 1, at : at + 256].astype(jnp.float32)
            far = far + far_ref[VROWS : VROWS + 1, BLOCK + at : BLOCK + at + 256].astype(jnp.float32)
            p_ref[:, at : at + 256] = jnp.exp2(scores * near * far).astype(jnp.bfloat16)

    @pl.when(flag % 2 == 1)
    def _():
        far_v = jnp.concatenate(
            [far_ref[BLOCK:VROWS, 0:BLOCK], far_ref[BLOCK:VROWS, BLOCK : 2 * BLOCK], ones], axis=0
        )
        part = lax.dot_general(far_v, p_ref[...], NT, preferred_element_type=jnp.float32)
        new_ref[0] += part[0:ACC, :]

    @pl.when(flag >= 2)
    def _():
        near_v = jnp.concatenate([v_ref[0], ones], axis=0)
        part = jnp.dot(near_v, p_ref[...], preferred_element_type=jnp.float32)
        far_sums_ref[...] += part[0:ACC, :]


def cells(order, flags, blocks, far, near_v, norms, sums):
    near = lambda g, order, flags: (order[g], 0, 0)
    whole = lambda g, order, flags: (0, 0)
    return pl.pallas_call(
        cells_kernel,
        out_shape=(
            jax.ShapeDtypeStruct((COLS, ACC, BLOCK), jnp.float32),
            jax.ShapeDtypeStruct((ACC, BLOCK), jnp.float32),
        ),
        grid_spec=pltpu.PrefetchScalarGridSpec(
            num_scalar_prefetch=2,
            grid=(COLS,),
            in_specs=[
                pl.BlockSpec((1, BLOCK, WIDTH), near),
                pl.BlockSpec((PAYLOAD, WIDTH), whole),
                pl.BlockSpec((1, EIGS, BLOCK), lambda g, order, flags: (g, 0, 0)),
                pl.BlockSpec((1, BLOCK, 128), near),
                pl.BlockSpec((1, ACC, BLOCK), near),
            ],
            out_specs=(
                pl.BlockSpec((1, ACC, BLOCK), near),
                pl.BlockSpec((ACC, BLOCK), whole),
            ),
            scratch_shapes=[pltpu.VMEM((BLOCK, BLOCK), jnp.bfloat16)],
        ),
        input_output_aliases={6: 0},
        compiler_params=pltpu.CompilerParams(vmem_limit_bytes=32 << 20),
        cost_estimate=pl.CostEstimate(
            flops=4 * 2 * BLOCK * BLOCK * WIDTH, bytes_accessed=12 << 20, transcendentals=4 * BLOCK * BLOCK
        ),
        name="cells",
    )(order, flags, blocks, far, near_v, norms, sums)


def solve_kernel(gram_ref, smoothed_ref, out_ref):
    rows = lax.broadcasted_iota(jnp.int32, (EIGS, 2 * EIGS), 0)
    lanes = lax.broadcasted_iota(jnp.int32, (EIGS, 2 * EIGS), 1)
    eye = jnp.where(rows + EIGS == lanes, 1.0, 0.0)[:, EIGS:]
    work = jnp.concatenate([gram_ref[...], eye], axis=1)
    pivots = jnp.ones((EIGS, 1), jnp.float32)
    below = rows[:, 0:1]
    for j in range(EIGS):
        row = work[j : j + 1, :]
        pivot = work[j : j + 1, j : j + 1]
        column = work[:, j : j + 1]
        pivots = jnp.where(below == j, pivot, pivots)
        factor = jnp.where(below > j, column / pivot, 0.0)
        work = work - factor * row
    inverse = work[:, EIGS:] * lax.rsqrt(pivots)
    out_ref[...] = jnp.dot(
        inverse, smoothed_ref[...], precision=lax.Precision.HIGHEST, preferred_element_type=jnp.float32
    )


def solve(gram, smoothed):
    return pl.pallas_call(
        solve_kernel,
        out_shape=jax.ShapeDtypeStruct(smoothed.shape, jnp.float32),
        in_specs=[pl.BlockSpec(memory_space=pltpu.VMEM)] * 2,
        out_specs=pl.BlockSpec(memory_space=pltpu.VMEM),
        name="solve",
    )(gram, smoothed)


def per_device(embeddings, vectors, block_pairs):
    here_row = lax.axis_index("row")
    here_col = lax.axis_index("col")
    here_y, here_x = here_row // SIDE, here_row % SIDE
    blocks = embeddings.reshape(COLS, BLOCK, WIDTH)

    def move(array, dy, dx, keep=None):
        return lax.ppermute(array, "row", shift(dy, dx, keep))

    def turn(array, by):
        return lax.ppermute(array, "col", [(i, (i + by * CORES) % COLS) for i in range(COLS)])

    def swap(array):
        return lax.ppermute(array, "col", [(i, i ^ 1) for i in range(COLS)])

    far = {"own": make_payload(here_col[None], blocks, vectors)}
    far["a"] = move(far["own"], 0, 1)
    far["b"] = move(far["own"], 1, 0)
    far["c"] = move(far["own"], -1, -1)
    far["d"] = move(far["a"], -1, 0)
    far["e"] = move(far["c"], 0, -1)
    far["g"] = move(far["a"], 0, 1, left_half)
    far["h"] = move(far["b"], 1, 0)
    far["f"] = move(far["h"], 0, 1)
    far["k"] = move(far["e"], -1, 0, top_half)

    pair_v = jnp.stack([vectors, swap(vectors)])
    near_v = jnp.concatenate([pair_v] + [turn(pair_v, k) for k in range(1, SIDE)], axis=0)
    order = jnp.stack([(here_col - CORES * k) % COLS ^ core for k in range(SIDE) for core in range(CORES)])
    norms = local_norms(blocks)

    far_ids, works = [], []
    ahead = (order - here_col) % COLS
    for name, ((dy, dx), keep) in STAGES.items():
        from_row = (here_y - dy) % SIDE * SIDE + (here_x - dx) % SIDE
        far_ids.append(from_row * COLS + here_col)
        if name == "own":
            half = COLS // 2
            works.append((ahead > 0) & ((ahead < half) | ((ahead == half) & (here_col < half))))
        else:
            works.append(jnp.broadcast_to(True if keep is None else keep(here_y, here_x), (COLS,)))
    far_ids = jnp.stack(far_ids)[:, None]
    near_ids = (here_row * COLS + order)[None, :]
    wanted = jnp.stack([near_ids * NBLOCKS + far_ids, far_ids * NBLOCKS + near_ids])
    listed = block_pairs[:, 0] * NBLOCKS + block_pairs[:, 1]
    found = jnp.any(wanted[..., None] == listed, axis=-1)
    flags = jnp.where(jnp.stack(works), found[0] + 2 * found[1], 0).astype(jnp.int32)

    sums = jnp.zeros((COLS, ACC, BLOCK), jnp.float32)
    owned = None
    for at, (name, ((dy, dx), keep)) in enumerate(STAGES.items()):
        sums, far_sums = cells(order, flags[at], blocks, far[name], near_v, norms, sums)
        if name == "own":
            owned = far_sums
        else:
            back = [(to, source) for source, to in shift(dy, dx, keep)]
            owned = owned + lax.ppermute(far_sums, "row", back)
    owned = owned + jnp.sum(lax.all_to_all(sums, "col", 0, 0), axis=0)

    smoothed = owned[0:EIGS] / owned[EIGS : EIGS + 1]
    gram = jnp.dot(
        smoothed, smoothed.T, precision=lax.Precision.HIGHEST, preferred_element_type=jnp.float32
    ) / (BLOCK * NBLOCKS)
    gram = gram + swap(gram)
    gram = gram + (turn(gram, 1) + turn(gram, 2) + turn(gram, 3))
    gram = gram + (move(gram, 0, 1) + move(gram, 0, 2) + move(gram, 0, 3))
    gram = gram + (move(gram, 1, 0) + move(gram, 2, 0) + move(gram, 3, 0))
    return solve(gram, smoothed)


def solution(mesh):
    return jax.shard_map(
        per_device,
        mesh=mesh,
        in_specs=(P("row", None), P(None, ("row", "col")), P()),
        out_specs=P(None, ("row", "col")),
        check_vma=False,
    )
```

```python
import functools
import math

import jax
import jax.numpy as jnp
from jax import lax
from jax.experimental import pallas as pl
from jax.experimental.pallas import tpu as pltpu
from jax.sharding import PartitionSpec as P

BLOCK = 512
WIDTH = 1024
EIGS = 64
NBLOCKS = 128
SIDE = 4
COLS = 8
CORES = 2
VROWS = BLOCK + EIGS // 2
PAYLOAD = VROWS + 16
ACC = EIGS + 8
SCALE = math.sqrt(math.log2(math.e) / math.sqrt(WIDTH))
COST = 8
NT = (((1,), (1,)), ((), ()))


def shift(dy, dx, keep=None):
    pairs = []
    for y in range(SIDE):
        for x in range(SIDE):
            to_y, to_x = (y + dy) % SIDE, (x + dx) % SIDE
            if keep is None or keep(to_y, to_x):
                pairs.append((y * SIDE + x, to_y * SIDE + to_x))
    return pairs


def left_half(y, x):
    return x < SIDE // 2


def top_half(y, x):
    return y < SIDE // 2


STAGES = {
    "own": ((0, 0), None),
    "a": ((0, 1), None),
    "b": ((1, 0), None),
    "c": ((-1, -1), None),
    "d": ((-1, 1), None),
    "e": ((-1, -2), None),
    "g": ((0, 2), left_half),
    "h": ((2, 0), top_half),
    "f": ((2, 1), None),
    "k": ((2, 2), top_half),
}


def row_norm(x):
    return lax.rsqrt(jnp.sum(x * x, axis=1, keepdims=True) * (1.0 / WIDTH) + 1e-06)


def payload_kernel(index_ref, x_ref, v_ref, out_ref):
    x = x_ref[0]
    out_ref[0:BLOCK, :] = x
    half = EIGS // 2
    out_ref[BLOCK:VROWS, 0:BLOCK] = v_ref[0:half, :]
    out_ref[BLOCK:VROWS, BLOCK : 2 * BLOCK] = v_ref[half:EIGS, :]
    norms = jnp.broadcast_to(row_norm(x.astype(jnp.float32)) * SCALE, (BLOCK, 128))
    rows = norms.T[0:16, :]
    high = rows.astype(jnp.bfloat16)
    low = (rows - high.astype(jnp.float32)).astype(jnp.bfloat16)
    out_ref[VROWS:PAYLOAD, 0:BLOCK] = high
    out_ref[VROWS:PAYLOAD, BLOCK : 2 * BLOCK] = low


def make_payload(here_col, blocks, vectors):
    return pl.pallas_call(
        payload_kernel,
        out_shape=jax.ShapeDtypeStruct((PAYLOAD, WIDTH), jnp.bfloat16),
        grid_spec=pltpu.PrefetchScalarGridSpec(
            num_scalar_prefetch=1,
            grid=(1,),
            in_specs=[
                pl.BlockSpec((1, BLOCK, WIDTH), lambda g, index: (index[0], 0, 0)),
                pl.BlockSpec((EIGS, BLOCK), lambda g, index: (0, 0)),
            ],
            out_specs=pl.BlockSpec((PAYLOAD, WIDTH), lambda g, index: (0, 0)),
        ),
        name="payload",
    )(here_col, blocks, vectors)


def side_vectors(side):
    half = EIGS // 2
    ones = jnp.ones((16, BLOCK), jnp.bfloat16)
    return jnp.concatenate([side[0:half, 0:BLOCK], side[0:half, BLOCK : 2 * BLOCK], ones], axis=0)


def side_norms(side):
    row = side[EIGS // 2 : EIGS // 2 + 1, :].astype(jnp.float32)
    return row[:, 0:BLOCK] + row[:, BLOCK : 2 * BLOCK]


def cells_kernel(count, first, order_ref, flags_ref, x_ref, side_ref, *refs):
    far_refs, refs = refs[:count], refs[count:]
    if first:
        new_ref, norm_ref, refs = refs[0], refs[1], refs[2:]
    else:
        norm_ref, old_ref, new_ref, refs = refs[0], refs[1], refs[2], refs[3:]
    far_sums_refs, token_ref, p_ref = refs[:count], refs[count], refs[count + 1]
    step = pl.program_id(0)

    @pl.when(step == 0)
    def _():
        for far_sums_ref in far_sums_refs:
            far_sums_ref[...] = jnp.zeros_like(far_sums_ref)
        token_ref[...] = jnp.zeros_like(token_ref)

    if first:
        new_ref[...] = jnp.zeros_like(new_ref)
        norm_ref[0] = jnp.broadcast_to(side_norms(side_ref[0, 0]), (128, BLOCK)).T
    else:
        new_ref[...] = old_ref[...]

    def score(far_ref):
        near = norm_ref[0]
        near = jnp.concatenate([near, near], axis=1)
        far = side_norms(far_ref[BLOCK:PAYLOAD, :])
        for at in range(0, BLOCK, 256):
            scores = lax.dot_general(
                x_ref[0], far_ref[at : at + 256, :], NT, preferred_element_type=jnp.float32
            )
            p_ref[:, at : at + 256] = jnp.exp2(scores * near * far[:, at : at + 256]).astype(jnp.bfloat16)

    def forward(far_ref):
        vectors = side_vectors(far_ref[BLOCK:PAYLOAD, :])
        part = lax.dot_general(vectors, p_ref[...], NT, preferred_element_type=jnp.float32)
        new_ref[0] += part[0:ACC, :]

    def backward(far_sums_ref):
        vectors = side_vectors(side_ref[0, 0])
        part = jnp.dot(vectors, p_ref[...], preferred_element_type=jnp.float32)
        far_sums_ref[...] += part[0:ACC, :]

    for at in range(count):
        flag = flags_ref[at * COLS + step]
        pl.when(flag > 0)(functools.partial(score, far_refs[at]))
        pl.when(flag % 2 == 1)(functools.partial(forward, far_refs[at]))
        pl.when(flag >= 2)(functools.partial(backward, far_sums_refs[at]))


def tie_kernel(*refs):
    pass


def tie(arrays, token):
    return pl.pallas_call(
        tie_kernel,
        out_shape=[jax.ShapeDtypeStruct(array.shape, array.dtype) for array in arrays],
        in_specs=[pl.BlockSpec(memory_space=pl.ANY)] * (len(arrays) + 1),
        out_specs=[pl.BlockSpec(memory_space=pl.ANY)] * len(arrays),
        input_output_aliases={at: at for at in range(len(arrays))},
        name="tie",
    )(*arrays, token)


def cells(order, flags, blocks, sides, fars, norms=None, sums=None):
    count, first = len(fars), sums is None
    near = lambda g, order, flags: (order[g], 0, 0)
    step = lambda g, order, flags: (g, 0, 0)
    whole = lambda g, order, flags: (0, 0)
    norm_spec, norm_shape = pl.BlockSpec((1, BLOCK, 128), step), (COLS, BLOCK, 128)
    sums_spec, sums_shape = pl.BlockSpec((1, ACC, BLOCK), step), (COLS, ACC, BLOCK)
    far_sums = [(pl.BlockSpec((ACC, BLOCK), whole), (ACC, BLOCK))] * count
    outs = [(sums_spec, sums_shape)] + ([(norm_spec, norm_shape)] if first else []) + far_sums
    outs += [(pl.BlockSpec((8, 128), whole), (8, 128))]
    result = pl.pallas_call(
        functools.partial(cells_kernel, count, first),
        out_shape=[jax.ShapeDtypeStruct(shape, jnp.float32) for _, shape in outs],
        grid_spec=pltpu.PrefetchScalarGridSpec(
            num_scalar_prefetch=2,
            grid=(COLS,),
            in_specs=[
                pl.BlockSpec((1, BLOCK, WIDTH), near),
                pl.BlockSpec((1, 1, PAYLOAD - BLOCK, WIDTH), lambda g, order, flags: (g % SIDE, g // SIDE, 0, 0)),
            ]
            + [pl.BlockSpec((PAYLOAD, WIDTH), whole)] * count
            + ([] if first else [norm_spec, sums_spec]),
            out_specs=[spec for spec, _ in outs],
            scratch_shapes=[pltpu.VMEM((BLOCK, BLOCK), jnp.bfloat16)],
        ),
        input_output_aliases={} if first else {5 + count: 0},
        compiler_params=pltpu.CompilerParams(vmem_limit_bytes=56 << 20),
        cost_estimate=pl.CostEstimate(
            flops=count * COST * BLOCK * BLOCK * WIDTH,
            bytes_accessed=(12 + count) << 20,
            transcendentals=count * 4 * BLOCK * BLOCK,
        ),
        name="cells",
    )(order, flags, blocks, sides, *fars, *([] if first else [norms, sums]))
    if first:
        return result[0], result[1], result[2:-1], result[-1]
    return result[0], norms, result[1:-1], result[-1]


def solve_kernel(gram_ref, smoothed_ref, out_ref):
    rows = lax.broadcasted_iota(jnp.int32, (EIGS, 2 * EIGS), 0)
    lanes = lax.broadcasted_iota(jnp.int32, (EIGS, 2 * EIGS), 1)
    eye = jnp.where(rows + EIGS == lanes, 1.0, 0.0)[:, EIGS:]
    work = jnp.concatenate([gram_ref[...], eye], axis=1)
    pivots = jnp.ones((EIGS, 1), jnp.float32)
    below = rows[:, 0:1]
    for j in range(EIGS):
        row = work[j : j + 1, :]
        pivot = work[j : j + 1, j : j + 1]
        column = work[:, j : j + 1]
        pivots = jnp.where(below == j, pivot, pivots)
        factor = jnp.where(below > j, column / pivot, 0.0)
        work = work - factor * row
    inverse = work[:, EIGS:] * lax.rsqrt(pivots)
    out_ref[...] = jnp.dot(
        inverse, smoothed_ref[...], precision=lax.Precision.HIGHEST, preferred_element_type=jnp.float32
    )


def solve(gram, smoothed):
    return pl.pallas_call(
        solve_kernel,
        out_shape=jax.ShapeDtypeStruct(smoothed.shape, jnp.float32),
        in_specs=[pl.BlockSpec(memory_space=pltpu.VMEM)] * 2,
        out_specs=pl.BlockSpec(memory_space=pltpu.VMEM),
        name="solve",
    )(gram, smoothed)


def per_device(embeddings, vectors, block_pairs):
    here_row = lax.axis_index("row")
    here_col = lax.axis_index("col")
    here_y, here_x = here_row // SIDE, here_row % SIDE
    blocks = embeddings.reshape(COLS, BLOCK, WIDTH)

    def move(array, dy, dx, keep=None):
        return lax.ppermute(array, "row", shift(dy, dx, keep))

    def turn(array, by):
        return lax.ppermute(array, "col", [(i, (i + by * CORES) % COLS) for i in range(COLS)])

    def swap(array):
        return lax.ppermute(array, "col", [(i, i ^ 1) for i in range(COLS)])

    far = {"own": make_payload(here_col[None], blocks, vectors)}
    far["a"] = move(far["own"], 0, 1)
    far["b"] = move(far["own"], 1, 0)
    far["c"] = move(far["own"], -1, -1)
    side = far["own"][BLOCK:PAYLOAD]
    pair = jnp.stack([side, swap(side)])
    sides = jnp.stack([pair] + [turn(pair, k) for k in range(1, SIDE)])
    order = jnp.stack([(here_col - CORES * k) % COLS ^ core for core in range(CORES) for k in range(SIDE)])

    far_ids, works = [], []
    ahead = (order - here_col) % COLS
    for name, ((dy, dx), keep) in STAGES.items():
        from_row = (here_y - dy) % SIDE * SIDE + (here_x - dx) % SIDE
        far_ids.append(from_row * COLS + here_col)
        if name == "own":
            half = COLS // 2
            works.append((ahead > 0) & ((ahead < half) | ((ahead == half) & (here_col < half))))
        else:
            works.append(jnp.broadcast_to(True if keep is None else keep(here_y, here_x), (COLS,)))
    far_ids = jnp.stack(far_ids)[:, None]
    near_ids = (here_row * COLS + order)[None, :]
    wanted = jnp.stack([near_ids * NBLOCKS + far_ids, far_ids * NBLOCKS + near_ids])
    listed = block_pairs[:, 0] * NBLOCKS + block_pairs[:, 1]
    found = jnp.any(wanted[..., None] == listed, axis=-1)
    flags = jnp.where(jnp.stack(works), found[0] + 2 * found[1], 0).astype(jnp.int32)

    starts = {name: at for at, name in enumerate(STAGES)}

    def work(group, norms=None, sums=None):
        at = starts[group[0]]
        return cells(
            order, flags[at : at + len(group)].reshape(-1), blocks, sides, [far[name] for name in group], norms, sums
        )

    def give_back(group, parts):
        moved = []
        for name, part in zip(group, parts):
            (dy, dx), keep = STAGES[name]
            moved.append(lax.ppermute(part, "row", [(to, source) for source, to in shift(dy, dx, keep)]))
        return moved

    sums, norms, returned, token = work(("own",))
    far["a"], far["b"], far["c"] = tie([far["a"], far["b"], far["c"]], token)
    far["d"] = move(far["a"], -1, 0)
    far["e"] = move(far["c"], 0, -1)
    far["g"] = move(far["a"], 0, 1, left_half)
    far["h"] = move(far["b"], 1, 0)

    group = ("a", "b", "c")
    sums, norms, parts, token = work(group, norms, sums)
    far["h"], far["e"] = tie([far["h"], far["e"]], token)
    early = sum(give_back(group, parts)) + returned[0]
    far["f"] = move(far["h"], 0, 1)
    far["k"] = move(far["e"], -1, 0, top_half)

    group = ("d", "e", "g", "h")
    sums, norms, parts, token = work(group, norms, sums)
    returned = give_back(group, parts)

    far["f"], far["k"] = tie([far["f"], far["k"]], early[0:8, 0:128])
    group = ("f", "k")
    sums, norms, parts, token = work(group, norms, sums)
    returned = [early] + returned + give_back(group, parts)

    kept = sums[:SIDE] + swap(sums[SIDE:])
    returned += [kept[0]] + [turn(kept[k], SIDE - k) for k in range(1, SIDE)]
    owned = sum(returned)

    smoothed = owned[0:EIGS] / owned[EIGS : EIGS + 1]
    gram = jnp.dot(
        smoothed, smoothed.T, precision=lax.Precision.HIGHEST, preferred_element_type=jnp.float32
    ) / (BLOCK * NBLOCKS)
    gram = gram + swap(gram)
    gram = gram + (turn(gram, 1) + turn(gram, 2) + turn(gram, 3))
    gram = gram + (move(gram, 0, 1) + move(gram, 0, 2) + move(gram, 0, 3))
    gram = gram + (move(gram, 1, 0) + move(gram, 2, 0) + move(gram, 3, 0))
    return solve(gram, smoothed)


def solution(mesh):
    return jax.shard_map(
        per_device,
        mesh=mesh,
        in_specs=(P("row", None), P(None, ("row", "col")), P()),
        out_specs=P(None, ("row", "col")),
        check_vma=False,
    )
```

```python
import functools
import math

import jax
import jax.numpy as jnp
from jax import lax
from jax.experimental import pallas as pl
from jax.experimental.pallas import tpu as pltpu
from jax.sharding import PartitionSpec as P

BLOCK = 512
WIDTH = 1024
EIGS = 64
NBLOCKS = 128
SIDE = 4
COLS = 8
CORES = 2
VROWS = BLOCK + EIGS // 2
PAYLOAD = VROWS + 16
ACC = EIGS + 8
SCALE = math.sqrt(math.log2(math.e) / math.sqrt(WIDTH))
COST = 8
NT = (((1,), (1,)), ((), ()))


def shift(dy, dx, keep=None):
    pairs = []
    for y in range(SIDE):
        for x in range(SIDE):
            to_y, to_x = (y + dy) % SIDE, (x + dx) % SIDE
            if keep is None or keep(to_y, to_x):
                pairs.append((y * SIDE + x, to_y * SIDE + to_x))
    return pairs


def left_half(y, x):
    return x < SIDE // 2


def top_half(y, x):
    return y < SIDE // 2


STAGES = {
    "own": ((0, 0), None),
    "a": ((0, 1), None),
    "b": ((1, 0), None),
    "c": ((-1, -1), None),
    "d": ((-1, 1), None),
    "e": ((-1, -2), None),
    "g": ((0, 2), left_half),
    "h": ((2, 0), top_half),
    "f": ((2, 1), None),
    "k": ((2, 2), top_half),
}


def row_norm(x):
    return lax.rsqrt(jnp.sum(x * x, axis=1, keepdims=True) * (1.0 / WIDTH) + 1e-06)


def payload_kernel(index_ref, x_ref, v_ref, out_ref):
    x = x_ref[0]
    out_ref[0:BLOCK, :] = x
    half = EIGS // 2
    out_ref[BLOCK:VROWS, 0:BLOCK] = v_ref[0:half, :]
    out_ref[BLOCK:VROWS, BLOCK : 2 * BLOCK] = v_ref[half:EIGS, :]
    norms = jnp.broadcast_to(row_norm(x.astype(jnp.float32)) * SCALE, (BLOCK, 128))
    rows = norms.T[0:16, :]
    high = rows.astype(jnp.bfloat16)
    low = (rows - high.astype(jnp.float32)).astype(jnp.bfloat16)
    out_ref[VROWS:PAYLOAD, 0:BLOCK] = high
    out_ref[VROWS:PAYLOAD, BLOCK : 2 * BLOCK] = low


def make_payload(here_col, blocks, vectors):
    return pl.pallas_call(
        payload_kernel,
        out_shape=jax.ShapeDtypeStruct((PAYLOAD, WIDTH), jnp.bfloat16),
        grid_spec=pltpu.PrefetchScalarGridSpec(
            num_scalar_prefetch=1,
            grid=(1,),
            in_specs=[
                pl.BlockSpec((1, BLOCK, WIDTH), lambda g, index: (index[0], 0, 0)),
                pl.BlockSpec((EIGS, BLOCK), lambda g, index: (0, 0)),
            ],
            out_specs=pl.BlockSpec((PAYLOAD, WIDTH), lambda g, index: (0, 0)),
        ),
        name="payload",
    )(here_col, blocks, vectors)


def side_vectors(side):
    half = EIGS // 2
    ones = jnp.ones((16, BLOCK), jnp.bfloat16)
    return jnp.concatenate([side[0:half, 0:BLOCK], side[0:half, BLOCK : 2 * BLOCK], ones], axis=0)


def side_norms(side):
    row = side[EIGS // 2 : EIGS // 2 + 1, :].astype(jnp.float32)
    return row[:, 0:BLOCK] + row[:, BLOCK : 2 * BLOCK]


def double(columns):
    return jnp.concatenate([columns, columns], axis=1)


def own_kernel(order_ref, flags_ref, x_ref, far_ref, new_ref, norm_ref, token_ref, p_ref):
    step = pl.program_id(0)
    new_ref[...] = jnp.zeros_like(new_ref)
    token_ref[...] = jnp.zeros_like(token_ref)
    norm_ref[0] = jnp.broadcast_to(row_norm(x_ref[0].astype(jnp.float32)) * SCALE, (BLOCK, 128))

    @pl.when(flags_ref[step] > 0)
    def _():
        side = far_ref[BLOCK:PAYLOAD, :]
        near, far = double(norm_ref[0]), side_norms(side)
        for at in range(0, BLOCK, 256):
            scores = lax.dot_general(
                x_ref[0], far_ref[at : at + 256, :], NT, preferred_element_type=jnp.float32
            )
            p_ref[:, at : at + 256] = jnp.exp2(scores * near * far[:, at : at + 256]).astype(jnp.bfloat16)
        part = lax.dot_general(side_vectors(side), p_ref[...], NT, preferred_element_type=jnp.float32)
        new_ref[0] = part[0:ACC, :]


def cells_kernel(count, order_ref, flags_ref, x_ref, side_ref, *refs):
    far_refs, refs = refs[:count], refs[count:]
    norm_ref, old_ref, new_ref, refs = refs[0], refs[1], refs[2], refs[3:]
    far_sums_refs, token_ref, p_ref, column_ref = refs[:count], refs[count], refs[count + 1], refs[count + 2]
    step = pl.program_id(0)

    @pl.when(step == 0)
    def _():
        token_ref[...] = jnp.zeros_like(token_ref)
        for at in range(count):
            far_sums_refs[at][...] = jnp.zeros_like(far_sums_refs[at])
            column_ref[at] = jnp.broadcast_to(side_norms(far_refs[at][BLOCK:PAYLOAD, :]), (128, BLOCK)).T

    new_ref[...] = old_ref[...]

    def forward_only(at):
        far_ref = far_refs[at]
        near, far = side_norms(side_ref[0, 0]), double(column_ref[at])
        for to in range(0, BLOCK, 256):
            scores = lax.dot_general(
                far_ref[0:BLOCK, :], x_ref[0, to : to + 256, :], NT, preferred_element_type=jnp.float32
            )
            p_ref[:, to : to + 256] = jnp.exp2(scores * near[:, to : to + 256] * far).astype(jnp.bfloat16)
        part = jnp.dot(side_vectors(far_ref[BLOCK:PAYLOAD, :]), p_ref[...], preferred_element_type=jnp.float32)
        new_ref[0] += part[0:ACC, :]

    def backward(at, both):
        far_ref = far_refs[at]
        side = far_ref[BLOCK:PAYLOAD, :]
        near, far = double(norm_ref[0]), side_norms(side)
        for to in range(0, BLOCK, 256):
            scores = lax.dot_general(
                x_ref[0], far_ref[to : to + 256, :], NT, preferred_element_type=jnp.float32
            )
            p_ref[:, to : to + 256] = jnp.exp2(scores * near * far[:, to : to + 256]).astype(jnp.bfloat16)
        part = jnp.dot(side_vectors(side_ref[0, 0]), p_ref[...], preferred_element_type=jnp.float32)
        far_sums_refs[at][...] += part[0:ACC, :]
        if both:
            part = lax.dot_general(side_vectors(side), p_ref[...], NT, preferred_element_type=jnp.float32)
            new_ref[0] += part[0:ACC, :]

    for at in range(count):
        flag = flags_ref[at * COLS + step]
        pl.when(flag == 1)(functools.partial(forward_only, at))
        pl.when(flag == 2)(functools.partial(backward, at, False))
        pl.when(flag == 3)(functools.partial(backward, at, True))


NEAR = lambda g, order, flags: (order[g], 0, 0)
STEP = lambda g, order, flags: (g, 0, 0)
WHOLE = lambda g, order, flags: (0, 0)
X_SPEC = pl.BlockSpec((1, BLOCK, WIDTH), NEAR)
FAR_SPEC = pl.BlockSpec((PAYLOAD, WIDTH), WHOLE)
NORM = (pl.BlockSpec((1, BLOCK, 128), STEP), (COLS, BLOCK, 128))
SUMS = (pl.BlockSpec((1, ACC, BLOCK), STEP), (COLS, ACC, BLOCK))
PART = (pl.BlockSpec((ACC, BLOCK), WHOLE), (ACC, BLOCK))
TOKEN = (pl.BlockSpec((8, 128), WHOLE), (8, 128))


def cells_call(kernel, count, ins, outs, scratch, aliases, name, args):
    return pl.pallas_call(
        kernel,
        out_shape=[jax.ShapeDtypeStruct(shape, jnp.float32) for _, shape in outs],
        grid_spec=pltpu.PrefetchScalarGridSpec(
            num_scalar_prefetch=2, grid=(COLS,), in_specs=ins, out_specs=[spec for spec, _ in outs], scratch_shapes=scratch
        ),
        input_output_aliases=aliases,
        compiler_params=pltpu.CompilerParams(vmem_limit_bytes=56 << 20),
        cost_estimate=pl.CostEstimate(
            flops=count * COST * BLOCK * BLOCK * WIDTH,
            bytes_accessed=(12 + count) << 20,
            transcendentals=count * 4 * BLOCK * BLOCK,
        ),
        name=name,
    )(*args)


SCORES = pltpu.VMEM((BLOCK, BLOCK), jnp.bfloat16)


def own_cells(order, flags, blocks, far):
    ins, outs = [X_SPEC, FAR_SPEC], [SUMS, NORM, TOKEN]
    return cells_call(own_kernel, 1, ins, outs, [SCORES], {}, "cells_own", (order, flags, blocks, far))


def cells(order, flags, blocks, sides, fars, norms, sums):
    count = len(fars)
    side = pl.BlockSpec((1, 1, PAYLOAD - BLOCK, WIDTH), lambda g, order, flags: (g % SIDE, g // SIDE, 0, 0))
    ins = [X_SPEC, side] + [FAR_SPEC] * count + [NORM[0], SUMS[0]]
    outs = [SUMS] + [PART] * count + [TOKEN]
    scratch = [SCORES, pltpu.VMEM((count, BLOCK, 128), jnp.float32)]
    args = (order, flags, blocks, sides, *fars, norms, sums)
    kernel = functools.partial(cells_kernel, count)
    result = cells_call(kernel, count, ins, outs, scratch, {5 + count: 0}, "cells", args)
    return result[0], result[1:-1], result[-1]


def tie_kernel(*refs):
    pass


def tie(arrays, *tokens):
    return pl.pallas_call(
        tie_kernel,
        out_shape=[jax.ShapeDtypeStruct(array.shape, array.dtype) for array in arrays],
        in_specs=[pl.BlockSpec(memory_space=pl.ANY)] * (len(arrays) + len(tokens)),
        out_specs=[pl.BlockSpec(memory_space=pl.ANY)] * len(arrays),
        input_output_aliases={at: at for at in range(len(arrays))},
        name="tie",
    )(*arrays, *tokens)


def solve_kernel(gram_ref, smoothed_ref, out_ref):
    rows = lax.broadcasted_iota(jnp.int32, (EIGS, 2 * EIGS), 0)
    lanes = lax.broadcasted_iota(jnp.int32, (EIGS, 2 * EIGS), 1)
    eye = jnp.where(rows + EIGS == lanes, 1.0, 0.0)[:, EIGS:]
    work = jnp.concatenate([gram_ref[...], eye], axis=1)
    pivots = jnp.ones((EIGS, 1), jnp.float32)
    below = rows[:, 0:1]
    for j in range(EIGS):
        row = work[j : j + 1, :]
        pivot = work[j : j + 1, j : j + 1]
        column = work[:, j : j + 1]
        pivots = jnp.where(below == j, pivot, pivots)
        factor = jnp.where(below > j, column / pivot, 0.0)
        work = work - factor * row
    inverse = work[:, EIGS:] * lax.rsqrt(pivots)
    out_ref[...] = jnp.dot(
        inverse, smoothed_ref[...], precision=lax.Precision.HIGHEST, preferred_element_type=jnp.float32
    )


def solve(gram, smoothed):
    return pl.pallas_call(
        solve_kernel,
        out_shape=jax.ShapeDtypeStruct(smoothed.shape, jnp.float32),
        in_specs=[pl.BlockSpec(memory_space=pltpu.VMEM)] * 2,
        out_specs=pl.BlockSpec(memory_space=pltpu.VMEM),
        name="solve",
    )(gram, smoothed)


def per_device(embeddings, vectors, block_pairs):
    here_row = lax.axis_index("row")
    here_col = lax.axis_index("col")
    here_y, here_x = here_row // SIDE, here_row % SIDE
    blocks = embeddings.reshape(COLS, BLOCK, WIDTH)

    def move(array, dy, dx, keep=None):
        return lax.ppermute(array, "row", shift(dy, dx, keep))

    def turn(array, by):
        return lax.ppermute(array, "col", [(i, (i + by * CORES) % COLS) for i in range(COLS)])

    def swap(array):
        return lax.ppermute(array, "col", [(i, i ^ 1) for i in range(COLS)])

    far = {"own": make_payload(here_col[None], blocks, vectors)}
    far["a"] = move(far["own"], 0, 1)
    far["b"] = move(far["own"], 1, 0)
    far["c"] = move(far["own"], -1, -1)
    side = far["own"][BLOCK:PAYLOAD]
    pair = jnp.stack([side, swap(side)])
    sides = jnp.stack([pair] + [turn(pair, k) for k in range(1, SIDE)])
    order = jnp.stack([(here_col - CORES * k) % COLS ^ core for core in range(CORES) for k in range(SIDE)])

    far_ids, works = [], []
    for name, ((dy, dx), keep) in STAGES.items():
        from_row = (here_y - dy) % SIDE * SIDE + (here_x - dx) % SIDE
        far_ids.append(from_row * COLS + here_col)
        works.append(jnp.broadcast_to(True if keep is None else keep(here_y, here_x), (COLS,)))
    far_ids = jnp.stack(far_ids)[:, None]
    near_ids = (here_row * COLS + order)[None, :]
    wanted = jnp.stack([near_ids * NBLOCKS + far_ids, far_ids * NBLOCKS + near_ids])
    listed = block_pairs[:, 0] * NBLOCKS + block_pairs[:, 1]
    found = jnp.any(wanted[..., None] == listed, axis=-1)
    both_ways = (jnp.arange(len(STAGES)) > 0)[:, None]
    flags = jnp.where(jnp.stack(works), found[0] + 2 * (found[1] & both_ways), 0).astype(jnp.int32)

    starts = {name: at for at, name in enumerate(STAGES)}

    def work(group, sums):
        at = starts[group[0]]
        return cells(
            order, flags[at : at + len(group)].reshape(-1), blocks, sides, [far[name] for name in group], norms, sums
        )

    def give_back(group, parts):
        moved = []
        for name, part in zip(group, parts):
            (dy, dx), keep = STAGES[name]
            moved.append(lax.ppermute(part, "row", [(to, source) for source, to in shift(dy, dx, keep)]))
        return moved

    sums, norms, token = own_cells(order, flags[0], blocks, far["own"])
    far["a"], far["b"], far["c"] = tie([far["a"], far["b"], far["c"]], token, sides)
    far["d"] = move(far["a"], -1, 0)
    far["e"] = move(far["c"], 0, -1)
    far["g"] = move(far["a"], 0, 1, left_half)
    far["h"] = move(far["b"], 1, 0)

    group = ("a", "b", "c")
    sums, parts, token = work(group, sums)
    far["h"], far["e"] = tie([far["h"], far["e"]], token)
    early = sum(give_back(group, parts))
    far["f"] = move(far["h"], 0, 1)
    far["k"] = move(far["e"], -1, 0, top_half)

    group = ("d", "e", "g", "h")
    sums, parts, token = work(group, sums)
    returned = give_back(group, parts)

    far["f"], far["k"] = tie([far["f"], far["k"]], early[0:8, 0:128])
    group = ("f", "k")
    sums, parts, token = work(group, sums)
    returned = [early] + returned + give_back(group, parts)

    kept = sums[:SIDE] + swap(sums[SIDE:])
    returned += [kept[0]] + [turn(kept[k], SIDE - k) for k in range(1, SIDE)]
    owned = sum(returned)

    smoothed = owned[0:EIGS] / owned[EIGS : EIGS + 1]
    gram = jnp.dot(
        smoothed, smoothed.T, precision=lax.Precision.HIGHEST, preferred_element_type=jnp.float32
    ) / (BLOCK * NBLOCKS)
    gram = gram + swap(gram)
    gram = gram + (turn(gram, 1) + turn(gram, 2) + turn(gram, 3))
    gram = gram + (move(gram, 0, 1) + move(gram, 0, 2) + move(gram, 0, 3))
    gram = gram + (move(gram, 1, 0) + move(gram, 2, 0) + move(gram, 3, 0))
    return solve(gram, smoothed)


def solution(mesh):
    return jax.shard_map(
        per_device,
        mesh=mesh,
        in_specs=(P("row", None), P(None, ("row", "col")), P()),
        out_specs=P(None, ("row", "col")),
        check_vma=False,
    )
```

```python
import functools
import math

import jax
import jax.numpy as jnp
from jax import lax
from jax.experimental import pallas as pl
from jax.experimental.pallas import tpu as pltpu
from jax.sharding import PartitionSpec as P

BLOCK = 512
WIDTH = 1024
EIGS = 64
NBLOCKS = 128
SIDE = 4
COLS = 8
CORES = 2
VROWS = BLOCK + EIGS // 2
PAYLOAD = VROWS + 16
ACC = EIGS + 8
SENT = EIGS + 16
SCALE = math.sqrt(math.log2(math.e) / math.sqrt(WIDTH))
COST = 8
NT = (((1,), (1,)), ((), ()))


def shift(dy, dx, keep=None):
    pairs = []
    for y in range(SIDE):
        for x in range(SIDE):
            to_y, to_x = (y + dy) % SIDE, (x + dx) % SIDE
            if keep is None or keep(to_y, to_x):
                pairs.append((y * SIDE + x, to_y * SIDE + to_x))
    return pairs


def top_half(y, x):
    return y < SIDE // 2


def turn_step(y, x):
    half = SIDE // 2
    return (0, half) if (y < half) == (x < half) else (half, 0)


def cycle():
    pairs = []
    for y in range(SIDE):
        for x in range(SIDE):
            dy, dx = turn_step(y, x)
            pairs.append(((y - dy) % SIDE * SIDE + (x - dx) % SIDE, y * SIDE + x))
    return pairs


STAGES = {
    "own": ((0, 0), None),
    "a": ((0, 1), None),
    "b": ((1, 0), None),
    "c": ((-1, -1), None),
    "d": ((-1, 1), None),
    "e": ((-1, -2), None),
    "m": (None, None),
    "f": ((-2, -1), None),
    "k": ((2, 2), top_half),
}


def pairs_of(name):
    moved, keep = STAGES[name]
    return cycle() if moved is None else shift(*moved, keep)


def row_norm(x):
    return lax.rsqrt(jnp.sum(x * x, axis=1, keepdims=True) * (1.0 / WIDTH) + 1e-06)


def payload_kernel(index_ref, x_ref, v_ref, out_ref):
    x = x_ref[0]
    out_ref[0:BLOCK, :] = x
    half = EIGS // 2
    out_ref[BLOCK:VROWS, 0:BLOCK] = v_ref[0:half, :]
    out_ref[BLOCK:VROWS, BLOCK : 2 * BLOCK] = v_ref[half:EIGS, :]
    norms = jnp.broadcast_to(row_norm(x.astype(jnp.float32)) * SCALE, (BLOCK, 128))
    rows = norms.T[0:16, :]
    high = rows.astype(jnp.bfloat16)
    low = (rows - high.astype(jnp.float32)).astype(jnp.bfloat16)
    out_ref[VROWS:PAYLOAD, 0:BLOCK] = high
    out_ref[VROWS:PAYLOAD, BLOCK : 2 * BLOCK] = low


def make_payload(here_col, blocks, vectors):
    return pl.pallas_call(
        payload_kernel,
        out_shape=jax.ShapeDtypeStruct((PAYLOAD, WIDTH), jnp.bfloat16),
        grid_spec=pltpu.PrefetchScalarGridSpec(
            num_scalar_prefetch=1,
            grid=(1,),
            in_specs=[
                pl.BlockSpec((1, BLOCK, WIDTH), lambda g, index: (index[0], 0, 0)),
                pl.BlockSpec((EIGS, BLOCK), lambda g, index: (0, 0)),
            ],
            out_specs=pl.BlockSpec((PAYLOAD, WIDTH), lambda g, index: (0, 0)),
        ),
        name="payload",
    )(here_col, blocks, vectors)


def side_vectors(side):
    half = EIGS // 2
    ones = jnp.ones((16, BLOCK), jnp.bfloat16)
    return jnp.concatenate([side[0:half, 0:BLOCK], side[0:half, BLOCK : 2 * BLOCK], ones], axis=0)


def side_norms(side):
    row = side[EIGS // 2 : EIGS // 2 + 1, :].astype(jnp.float32)
    return row[:, 0:BLOCK] + row[:, BLOCK : 2 * BLOCK]


def double(columns):
    return jnp.concatenate([columns, columns], axis=1)


def own_kernel(order_ref, flags_ref, x_ref, far_ref, new_ref, norm_ref, token_ref, p_ref):
    step = pl.program_id(0)
    new_ref[...] = jnp.zeros_like(new_ref)
    token_ref[...] = jnp.zeros_like(token_ref)
    norm_ref[0] = jnp.broadcast_to(row_norm(x_ref[0].astype(jnp.float32)) * SCALE, (BLOCK, 128))

    @pl.when(flags_ref[step] > 0)
    def _():
        side = far_ref[BLOCK:PAYLOAD, :]
        near, far = double(norm_ref[0]), side_norms(side)
        for at in range(0, BLOCK, 256):
            scores = lax.dot_general(
                x_ref[0], far_ref[at : at + 256, :], NT, preferred_element_type=jnp.float32
            )
            p_ref[:, at : at + 256] = jnp.exp2(scores * near * far[:, at : at + 256]).astype(jnp.bfloat16)
        part = lax.dot_general(side_vectors(side), p_ref[...], NT, preferred_element_type=jnp.float32)
        new_ref[0] = part[0:ACC, :]


def cells_kernel(count, order_ref, flags_ref, x_ref, side_ref, *refs):
    far_refs, refs = refs[:count], refs[count:]
    norm_ref, old_ref, new_ref, refs = refs[0], refs[1], refs[2], refs[3:]
    sent_refs, token_ref, (p_ref, column_ref, far_sums_ref) = refs[:count], refs[count], refs[count + 1 :]
    step = pl.program_id(0)

    @pl.when(step == 0)
    def _():
        token_ref[...] = jnp.zeros_like(token_ref)
        far_sums_ref[...] = jnp.zeros_like(far_sums_ref)
        for at in range(count):
            column_ref[at] = jnp.broadcast_to(side_norms(far_refs[at][BLOCK:PAYLOAD, :]), (128, BLOCK)).T

    new_ref[...] = old_ref[...]

    def forward_only(at):
        far_ref = far_refs[at]
        near, far = side_norms(side_ref[0, 0]), double(column_ref[at])
        for to in range(0, BLOCK, 256):
            scores = lax.dot_general(
                far_ref[0:BLOCK, :], x_ref[0, to : to + 256, :], NT, preferred_element_type=jnp.float32
            )
            p_ref[:, to : to + 256] = jnp.exp2(scores * near[:, to : to + 256] * far).astype(jnp.bfloat16)
        part = jnp.dot(side_vectors(far_ref[BLOCK:PAYLOAD, :]), p_ref[...], preferred_element_type=jnp.float32)
        new_ref[0] += part[0:ACC, :]

    def backward(at, both):
        far_ref = far_refs[at]
        side = far_ref[BLOCK:PAYLOAD, :]
        near, far = double(norm_ref[0]), side_norms(side)
        for to in range(0, BLOCK, 256):
            scores = lax.dot_general(
                x_ref[0], far_ref[to : to + 256, :], NT, preferred_element_type=jnp.float32
            )
            p_ref[:, to : to + 256] = jnp.exp2(scores * near * far[:, to : to + 256]).astype(jnp.bfloat16)
        part = jnp.dot(side_vectors(side_ref[0, 0]), p_ref[...], preferred_element_type=jnp.float32)
        far_sums_ref[at] += part[0:ACC, :]
        if both:
            part = lax.dot_general(side_vectors(side), p_ref[...], NT, preferred_element_type=jnp.float32)
            new_ref[0] += part[0:ACC, :]

    for at in range(count):
        flag = flags_ref[at * COLS + step]
        pl.when(flag == 1)(functools.partial(forward_only, at))
        pl.when(flag == 2)(functools.partial(backward, at, False))
        pl.when(flag == 3)(functools.partial(backward, at, True))

    @pl.when(step == COLS - 1)
    def _():
        for at in range(count):
            degrees = far_sums_ref[at, EIGS:ACC, :]
            high = degrees.astype(jnp.bfloat16).astype(jnp.float32)
            sent = jnp.concatenate([far_sums_ref[at, 0:EIGS, :], high, degrees - high], axis=0)
            sent_refs[at][...] = sent.astype(jnp.bfloat16)


NEAR = lambda g, order, flags: (order[g], 0, 0)
STEP = lambda g, order, flags: (g, 0, 0)
WHOLE = lambda g, order, flags: (0, 0)
X_SPEC = pl.BlockSpec((1, BLOCK, WIDTH), NEAR)
FAR_SPEC = pl.BlockSpec((PAYLOAD, WIDTH), WHOLE)
NORM = (pl.BlockSpec((1, BLOCK, 128), STEP), (COLS, BLOCK, 128), jnp.float32)
SUMS = (pl.BlockSpec((1, ACC, BLOCK), STEP), (COLS, ACC, BLOCK), jnp.float32)
PART = (pl.BlockSpec((SENT, BLOCK), WHOLE), (SENT, BLOCK), jnp.bfloat16)
TOKEN = (pl.BlockSpec((8, 128), WHOLE), (8, 128), jnp.float32)


def cells_call(kernel, count, ins, outs, scratch, aliases, name, args):
    return pl.pallas_call(
        kernel,
        out_shape=[jax.ShapeDtypeStruct(shape, dtype) for _, shape, dtype in outs],
        grid_spec=pltpu.PrefetchScalarGridSpec(
            num_scalar_prefetch=2, grid=(COLS,), in_specs=ins, out_specs=[spec for spec, _, _ in outs], scratch_shapes=scratch
        ),
        input_output_aliases=aliases,
        compiler_params=pltpu.CompilerParams(vmem_limit_bytes=56 << 20),
        cost_estimate=pl.CostEstimate(
            flops=count * COST * BLOCK * BLOCK * WIDTH,
            bytes_accessed=(12 + count) << 20,
            transcendentals=count * 4 * BLOCK * BLOCK,
        ),
        name=name,
    )(*args)


SCORES = pltpu.VMEM((BLOCK, BLOCK), jnp.bfloat16)


def own_cells(order, flags, blocks, far):
    ins, outs = [X_SPEC, FAR_SPEC], [SUMS, NORM, TOKEN]
    return cells_call(own_kernel, 1, ins, outs, [SCORES], {}, "cells_own", (order, flags, blocks, far))


def cells(order, flags, blocks, sides, fars, norms, sums):
    count = len(fars)
    side = pl.BlockSpec((1, 1, PAYLOAD - BLOCK, WIDTH), lambda g, order, flags: (g % SIDE, g // SIDE, 0, 0))
    ins = [X_SPEC, side] + [FAR_SPEC] * count + [NORM[0], SUMS[0]]
    outs = [SUMS] + [PART] * count + [TOKEN]
    scratch = [SCORES] + [pltpu.VMEM((count, *shape), jnp.float32) for shape in ((BLOCK, 128), (ACC, BLOCK))]
    args = (order, flags, blocks, sides, *fars, norms, sums)
    kernel = functools.partial(cells_kernel, count)
    result = cells_call(kernel, count, ins, outs, scratch, {5 + count: 0}, "cells", args)
    return result[0], result[1:-1], result[-1]


def tie_kernel(*refs):
    pass


def tie(arrays, *tokens):
    return pl.pallas_call(
        tie_kernel,
        out_shape=[jax.ShapeDtypeStruct(array.shape, array.dtype) for array in arrays],
        in_specs=[pl.BlockSpec(memory_space=pltpu.HBM)] * (len(arrays) + len(tokens)),
        out_specs=[pl.BlockSpec(memory_space=pltpu.HBM)] * len(arrays),
        input_output_aliases={at: at for at in range(len(arrays))},
        name="tie",
    )(*arrays, *tokens)


def solve_kernel(gram_ref, smoothed_ref, out_ref):
    rows = lax.broadcasted_iota(jnp.int32, (EIGS, 2 * EIGS), 0)
    lanes = lax.broadcasted_iota(jnp.int32, (EIGS, 2 * EIGS), 1)
    eye = jnp.where(rows + EIGS == lanes, 1.0, 0.0)[:, EIGS:]
    work = jnp.concatenate([gram_ref[...], eye], axis=1)
    pivots = jnp.ones((EIGS, 1), jnp.float32)
    below = rows[:, 0:1]
    for j in range(0, EIGS, 2):
        row1, row2 = work[j : j + 1, :], work[j + 1 : j + 2, :]
        first, cross = work[j : j + 1, j : j + 1], work[j : j + 1, j + 1 : j + 2]
        second = work[j + 1 : j + 2, j + 1 : j + 2]
        column1, column2 = work[:, j : j + 1], work[:, j + 1 : j + 2]
        scale = 1.0 / (first * second - cross * cross)
        ratio = cross / first
        pivots = jnp.where(below == j, first, jnp.where(below == j + 1, second - cross * ratio, pivots))
        factor1 = jnp.where(below > j + 1, (column1 * second - column2 * cross) * scale, 0.0)
        factor1 = jnp.where(below == j + 1, ratio, factor1)
        factor2 = jnp.where(below > j + 1, (column2 * first - column1 * cross) * scale, 0.0)
        work = work - (factor1 * row1 + factor2 * row2)
    inverse = work[:, EIGS:] * lax.rsqrt(pivots)
    out_ref[...] = jnp.dot(
        inverse, smoothed_ref[...], precision=lax.Precision.HIGHEST, preferred_element_type=jnp.float32
    )


def solve(gram, smoothed):
    return pl.pallas_call(
        solve_kernel,
        out_shape=jax.ShapeDtypeStruct(smoothed.shape, jnp.float32),
        in_specs=[pl.BlockSpec(memory_space=pltpu.VMEM)] * 2,
        out_specs=pl.BlockSpec(memory_space=pltpu.VMEM),
        name="solve",
    )(gram, smoothed)


def per_device(embeddings, vectors, block_pairs):
    here_row = lax.axis_index("row")
    here_col = lax.axis_index("col")
    here_y, here_x = here_row // SIDE, here_row % SIDE
    blocks = embeddings.reshape(COLS, BLOCK, WIDTH)

    def move(array, dy, dx, keep=None):
        return lax.ppermute(array, "row", shift(dy, dx, keep))

    def turn(array, by):
        return lax.ppermute(array, "col", [(i, (i + by * CORES) % COLS) for i in range(COLS)])

    def swap(array):
        return lax.ppermute(array, "col", [(i, i ^ 1) for i in range(COLS)])

    far = {"own": make_payload(here_col[None], blocks, vectors)}
    far["a"] = move(far["own"], 0, 1)
    far["b"] = move(far["own"], 1, 0)
    far["c"] = move(far["own"], -1, -1)
    order = jnp.stack([(here_col - CORES * k) % COLS ^ core for core in range(CORES) for k in range(SIDE)])

    far_ids, works = [], []
    diagonal = (here_y < SIDE // 2) == (here_x < SIDE // 2)
    for moved, keep in STAGES.values():
        dy, dx = moved or (jnp.where(diagonal, 0, SIDE // 2), jnp.where(diagonal, SIDE // 2, 0))
        from_row = (here_y - dy) % SIDE * SIDE + (here_x - dx) % SIDE
        far_ids.append(from_row * COLS + here_col)
        works.append(jnp.broadcast_to(True if keep is None else keep(here_y, here_x), (COLS,)))
    far_ids = jnp.stack(far_ids)[:, None]
    near_ids = (here_row * COLS + order)[None, :]
    wanted = jnp.stack([near_ids * NBLOCKS + far_ids, far_ids * NBLOCKS + near_ids])
    listed = block_pairs[:, 0] * NBLOCKS + block_pairs[:, 1]
    found = jnp.any(wanted[..., None] == listed, axis=-1)
    both_ways = (jnp.arange(len(STAGES)) > 0)[:, None]
    flags = jnp.where(jnp.stack(works), found[0] + 2 * (found[1] & both_ways), 0).astype(jnp.int32)

    starts = {name: at for at, name in enumerate(STAGES)}

    def work(group, sums):
        at = starts[group[0]]
        return cells(
            order, flags[at : at + len(group)].reshape(-1), blocks, sides, [far[name] for name in group], norms, sums
        )

    def give_back(group, parts):
        returned = []
        for name, part in zip(group, parts):
            part = lax.ppermute(part, "row", [(to, source) for source, to in pairs_of(name)]).astype(jnp.float32)
            degrees = part[EIGS:ACC] + part[ACC:SENT]
            returned.append(jnp.concatenate([part[0:EIGS], degrees], axis=0))
        return returned

    side = far["own"][BLOCK:PAYLOAD]
    pair = jnp.stack([side, swap(side)])
    sums, norms, token = own_cells(order, flags[0], blocks, far["own"])
    (pair,) = tie([pair], token)
    sides = jnp.stack([pair] + [turn(pair, k) for k in range(1, SIDE)])
    far["a"], far["b"], far["c"] = tie([far["a"], far["b"], far["c"]], sides)
    far["d"] = move(far["a"], -1, 0)
    far["e"] = move(far["c"], 0, -1)
    far["m"] = lax.ppermute(far["own"], "row", cycle())
    far["f"] = move(far["c"], -1, 0)
    far["k"] = move(far["e"], -1, 0, top_half)

    returned = []
    for group in (("a", "b", "c"), ("d", "e", "m"), ("f", "k")):
        sums, parts, token = work(group, sums)
        returned += give_back(group, parts)

    kept = sums[:SIDE] + swap(sums[SIDE:])
    returned += [kept[0]] + [turn(kept[k], SIDE - k) for k in range(1, SIDE)]
    owned = sum(returned)

    smoothed = owned[0:EIGS] / owned[EIGS : EIGS + 1]
    gram = jnp.dot(
        smoothed, smoothed.T, precision=lax.Precision.HIGHEST, preferred_element_type=jnp.float32
    ) / (BLOCK * NBLOCKS)
    gram = gram + swap(gram)
    gram = gram + (turn(gram, 1) + turn(gram, 2) + turn(gram, 3))
    gram = gram + (move(gram, 0, 1) + move(gram, 0, 2) + move(gram, 0, 3))
    gram = gram + (move(gram, 1, 0) + move(gram, 2, 0) + move(gram, 3, 0))
    return solve(gram, smoothed)


def solution(mesh):
    return jax.shard_map(
        per_device,
        mesh=mesh,
        in_specs=(P("row", None), P(None, ("row", "col")), P()),
        out_specs=P(None, ("row", "col")),
        check_vma=False,
    )
```

```python
import functools
import math

import jax
import jax.numpy as jnp
from jax import lax
from jax.experimental import pallas as pl
from jax.experimental.pallas import tpu as pltpu
from jax.sharding import PartitionSpec as P

BLOCK = 512
WIDTH = 1024
EIGS = 64
NBLOCKS = 128
SIDE = 4
COLS = 8
CORES = 2
VROWS = BLOCK + EIGS // 2
PAYLOAD = VROWS + 16
ACC = EIGS + 8
SENT = EIGS + 16
SCALE = math.sqrt(math.log2(math.e) / math.sqrt(WIDTH))
COST = 8
NT = (((1,), (1,)), ((), ()))


def shift(dy, dx, keep=None):
    pairs = []
    for y in range(SIDE):
        for x in range(SIDE):
            to_y, to_x = (y + dy) % SIDE, (x + dx) % SIDE
            if keep is None or keep(to_y, to_x):
                pairs.append((y * SIDE + x, to_y * SIDE + to_x))
    return pairs


def left_half(y, x):
    return x < SIDE // 2


def top_half(y, x):
    return y < SIDE // 2


STAGES = {
    "own": ((0, 0), None),
    "a": ((0, 1), None),
    "b": ((1, 0), None),
    "c": ((-1, -1), None),
    "d": ((-1, 1), None),
    "e": ((-1, -2), None),
    "g": ((0, 2), left_half),
    "h": ((2, 0), top_half),
    "f": ((2, 1), None),
    "k": ((2, 2), top_half),
}


def row_norm(x):
    return lax.rsqrt(jnp.sum(x * x, axis=1, keepdims=True) * (1.0 / WIDTH) + 1e-06)


def payload_kernel(index_ref, x_ref, v_ref, out_ref):
    x = x_ref[0]
    out_ref[0:BLOCK, :] = x
    half = EIGS // 2
    out_ref[BLOCK:VROWS, 0:BLOCK] = v_ref[0:half, :]
    out_ref[BLOCK:VROWS, BLOCK : 2 * BLOCK] = v_ref[half:EIGS, :]
    norms = jnp.broadcast_to(row_norm(x.astype(jnp.float32)) * SCALE, (BLOCK, 128))
    rows = norms.T[0:16, :]
    high = rows.astype(jnp.bfloat16)
    low = (rows - high.astype(jnp.float32)).astype(jnp.bfloat16)
    out_ref[VROWS:PAYLOAD, 0:BLOCK] = high
    out_ref[VROWS:PAYLOAD, BLOCK : 2 * BLOCK] = low


def make_payload(here_col, blocks, vectors):
    return pl.pallas_call(
        payload_kernel,
        out_shape=jax.ShapeDtypeStruct((PAYLOAD, WIDTH), jnp.bfloat16),
        grid_spec=pltpu.PrefetchScalarGridSpec(
            num_scalar_prefetch=1,
            grid=(1,),
            in_specs=[
                pl.BlockSpec((1, BLOCK, WIDTH), lambda g, index: (index[0], 0, 0)),
                pl.BlockSpec((EIGS, BLOCK), lambda g, index: (0, 0)),
            ],
            out_specs=pl.BlockSpec((PAYLOAD, WIDTH), lambda g, index: (0, 0)),
        ),
        name="payload",
    )(here_col, blocks, vectors)


def side_vectors(side):
    half = EIGS // 2
    ones = jnp.ones((16, BLOCK), jnp.bfloat16)
    return jnp.concatenate([side[0:half, 0:BLOCK], side[0:half, BLOCK : 2 * BLOCK], ones], axis=0)


def side_norms(side):
    row = side[EIGS // 2 : EIGS // 2 + 1, :].astype(jnp.float32)
    return row[:, 0:BLOCK] + row[:, BLOCK : 2 * BLOCK]


def double(columns):
    return jnp.concatenate([columns, columns], axis=1)


def own_kernel(order_ref, flags_ref, x_ref, far_ref, new_ref, norm_ref, row_ref, token_ref, p_ref):
    step = pl.program_id(0)
    new_ref[...] = jnp.zeros_like(new_ref)
    token_ref[...] = jnp.zeros_like(token_ref)
    norms = jnp.broadcast_to(row_norm(x_ref[0].astype(jnp.float32)) * SCALE, (BLOCK, 128))
    norm_ref[0] = norms
    row_ref[0] = norms.T[0:8, :]

    @pl.when(flags_ref[step] > 0)
    def _():
        side = far_ref[BLOCK:PAYLOAD, :]
        near, far = double(norm_ref[0]), side_norms(side)
        for at in range(0, BLOCK, 256):
            scores = lax.dot_general(
                x_ref[0], far_ref[at : at + 256, :], NT, preferred_element_type=jnp.float32
            )
            p_ref[:, at : at + 256] = jnp.exp2(scores * near * far[:, at : at + 256]).astype(jnp.bfloat16)
        part = lax.dot_general(side_vectors(side), p_ref[...], NT, preferred_element_type=jnp.float32)
        new_ref[0] = part[0:ACC, :]


def cells_kernel(count, order_ref, flags_ref, x_ref, near_v_ref, *refs):
    far_refs, refs = refs[:count], refs[count:]
    norm_ref, row_ref, old_ref, new_ref, refs = refs[0], refs[1], refs[2], refs[3], refs[4:]
    sent_refs, token_ref, (p_ref, column_ref, far_sums_ref) = refs[:count], refs[count], refs[count + 1 :]
    step = pl.program_id(0)

    @pl.when(step == 0)
    def _():
        token_ref[...] = jnp.zeros_like(token_ref)
        far_sums_ref[...] = jnp.zeros_like(far_sums_ref)
        for at in range(count):
            column_ref[at] = jnp.broadcast_to(side_norms(far_refs[at][BLOCK:PAYLOAD, :]), (128, BLOCK)).T

    new_ref[...] = old_ref[...]

    def forward_only(at):
        far_ref = far_refs[at]
        near, far = row_ref[0, 0:1, :], double(column_ref[at])
        for to in range(0, BLOCK, 256):
            scores = lax.dot_general(
                far_ref[0:BLOCK, :], x_ref[0, to : to + 256, :], NT, preferred_element_type=jnp.float32
            )
            p_ref[:, to : to + 256] = jnp.exp2(scores * near[:, to : to + 256] * far).astype(jnp.bfloat16)
        part = jnp.dot(side_vectors(far_ref[BLOCK:PAYLOAD, :]), p_ref[...], preferred_element_type=jnp.float32)
        new_ref[0] += part[0:ACC, :]

    def backward(at, both):
        far_ref = far_refs[at]
        side = far_ref[BLOCK:PAYLOAD, :]
        near, far = double(norm_ref[0]), side_norms(side)
        for to in range(0, BLOCK, 256):
            scores = lax.dot_general(
                x_ref[0], far_ref[to : to + 256, :], NT, preferred_element_type=jnp.float32
            )
            p_ref[:, to : to + 256] = jnp.exp2(scores * near * far[:, to : to + 256]).astype(jnp.bfloat16)
        vectors = jnp.concatenate([near_v_ref[0], jnp.ones((16, BLOCK), jnp.bfloat16)], axis=0)
        part = jnp.dot(vectors, p_ref[...], preferred_element_type=jnp.float32)
        far_sums_ref[at] += part[0:ACC, :]
        if both:
            part = lax.dot_general(side_vectors(side), p_ref[...], NT, preferred_element_type=jnp.float32)
            new_ref[0] += part[0:ACC, :]

    for at in range(count):
        flag = flags_ref[at * COLS + step]
        pl.when(flag == 1)(functools.partial(forward_only, at))
        pl.when(flag == 2)(functools.partial(backward, at, False))
        pl.when(flag == 3)(functools.partial(backward, at, True))

    @pl.when(step == COLS - 1)
    def _():
        for at in range(count):
            degrees = far_sums_ref[at, EIGS:ACC, :]
            high = degrees.astype(jnp.bfloat16).astype(jnp.float32)
            sent = jnp.concatenate([far_sums_ref[at, 0:EIGS, :], high, degrees - high], axis=0)
            sent_refs[at][...] = sent.astype(jnp.bfloat16)


NEAR = lambda g, order, flags: (order[g], 0, 0)
STEP = lambda g, order, flags: (g, 0, 0)
WHOLE = lambda g, order, flags: (0, 0)
X_SPEC = pl.BlockSpec((1, BLOCK, WIDTH), NEAR)
FAR_SPEC = pl.BlockSpec((PAYLOAD, WIDTH), WHOLE)
NORM = (pl.BlockSpec((1, BLOCK, 128), STEP), (COLS, BLOCK, 128), jnp.float32)
ROW = (pl.BlockSpec((1, 8, BLOCK), STEP), (COLS, 8, BLOCK), jnp.float32)
SUMS = (pl.BlockSpec((1, ACC, BLOCK), STEP), (COLS, ACC, BLOCK), jnp.float32)
PART = (pl.BlockSpec((SENT, BLOCK), WHOLE), (SENT, BLOCK), jnp.bfloat16)
TOKEN = (pl.BlockSpec((8, 128), WHOLE), (8, 128), jnp.float32)


def cells_call(kernel, count, ins, outs, scratch, aliases, name, args):
    return pl.pallas_call(
        kernel,
        out_shape=[jax.ShapeDtypeStruct(shape, dtype) for _, shape, dtype in outs],
        grid_spec=pltpu.PrefetchScalarGridSpec(
            num_scalar_prefetch=2, grid=(COLS,), in_specs=ins, out_specs=[spec for spec, _, _ in outs], scratch_shapes=scratch
        ),
        input_output_aliases=aliases,
        compiler_params=pltpu.CompilerParams(vmem_limit_bytes=56 << 20),
        cost_estimate=pl.CostEstimate(
            flops=count * COST * BLOCK * BLOCK * WIDTH,
            bytes_accessed=(12 + count) << 20,
            transcendentals=count * 4 * BLOCK * BLOCK,
        ),
        name=name,
    )(*args)


SCORES = pltpu.VMEM((BLOCK, BLOCK), jnp.bfloat16)


def own_cells(order, flags, blocks, far):
    ins, outs = [X_SPEC, FAR_SPEC], [SUMS, NORM, ROW, TOKEN]
    return cells_call(own_kernel, 1, ins, outs, [SCORES], {}, "cells_own", (order, flags, blocks, far))


def cells(order, flags, blocks, near_v, fars, norms, rows, sums):
    count = len(fars)
    ins = [X_SPEC, pl.BlockSpec((1, EIGS, BLOCK), NEAR)] + [FAR_SPEC] * count + [NORM[0], ROW[0], SUMS[0]]
    outs = [SUMS] + [PART] * count + [TOKEN]
    scratch = [SCORES] + [pltpu.VMEM((count, *shape), jnp.float32) for shape in ((BLOCK, 128), (ACC, BLOCK))]
    args = (order, flags, blocks, near_v, *fars, norms, rows, sums)
    kernel = functools.partial(cells_kernel, count)
    result = cells_call(kernel, count, ins, outs, scratch, {6 + count: 0}, "cells", args)
    return result[0], result[1:-1], result[-1]


def tie_kernel(*refs):
    pass


def tie(arrays, *tokens):
    return pl.pallas_call(
        tie_kernel,
        out_shape=[jax.ShapeDtypeStruct(array.shape, array.dtype) for array in arrays],
        in_specs=[pl.BlockSpec(memory_space=pltpu.HBM)] * (len(arrays) + len(tokens)),
        out_specs=[pl.BlockSpec(memory_space=pltpu.HBM)] * len(arrays),
        input_output_aliases={at: at for at in range(len(arrays))},
        name="tie",
    )(*arrays, *tokens)


def solve_kernel(gram_ref, smoothed_ref, out_ref):
    rows = lax.broadcasted_iota(jnp.int32, (EIGS, 2 * EIGS), 0)
    lanes = lax.broadcasted_iota(jnp.int32, (EIGS, 2 * EIGS), 1)
    eye = jnp.where(rows + EIGS == lanes, 1.0, 0.0)[:, EIGS:]
    work = jnp.concatenate([gram_ref[...], eye], axis=1)
    below = rows[0:8, :]
    tiles, done = [work[at : at + 8, :] for at in range(0, EIGS, 8)], []
    while tiles:
        for j in range(8):
            at = len(done) * 8 + j
            columns = [jnp.broadcast_to(tile[:, at : at + 1], tile.shape) for tile in tiles]
            pivot = columns[0][j : j + 1, :]
            row = tiles[0][j : j + 1, :]
            scaled = row / pivot
            columns[0] = jnp.where(below > j, columns[0], 0.0)
            tiles = [tile - column * scaled for tile, column in zip(tiles, columns)]
            tiles[0] = jnp.where(below == j, row * lax.rsqrt(pivot), tiles[0])
        done.append(tiles.pop(0))
    inverse = jnp.concatenate(done, axis=0)[:, EIGS:]
    out_ref[...] = jnp.dot(
        inverse, smoothed_ref[...], precision=lax.Precision.HIGHEST, preferred_element_type=jnp.float32
    )


def solve(gram, smoothed):
    return pl.pallas_call(
        solve_kernel,
        out_shape=jax.ShapeDtypeStruct(smoothed.shape, jnp.float32),
        in_specs=[pl.BlockSpec(memory_space=pltpu.VMEM)] * 2,
        out_specs=pl.BlockSpec(memory_space=pltpu.VMEM),
        name="solve",
    )(gram, smoothed)


def per_device(embeddings, vectors, block_pairs):
    here_row = lax.axis_index("row")
    here_col = lax.axis_index("col")
    here_y, here_x = here_row // SIDE, here_row % SIDE
    blocks = embeddings.reshape(COLS, BLOCK, WIDTH)

    def move(array, dy, dx, keep=None):
        return lax.ppermute(array, "row", shift(dy, dx, keep))

    def turn(array, by):
        return lax.ppermute(array, "col", [(i, (i + by * CORES) % COLS) for i in range(COLS)])

    def swap(array):
        return lax.ppermute(array, "col", [(i, i ^ 1) for i in range(COLS)])

    far = {"own": make_payload(here_col[None], blocks, vectors)}
    far["a"] = move(far["own"], 0, 1)
    far["b"] = move(far["own"], 1, 0)
    far["c"] = move(far["own"], -1, -1)
    order = jnp.stack([(here_col - CORES * k) % COLS ^ core for core in range(CORES) for k in range(SIDE)])

    far_ids, works = [], []
    for (dy, dx), keep in STAGES.values():
        from_row = (here_y - dy) % SIDE * SIDE + (here_x - dx) % SIDE
        far_ids.append(from_row * COLS + here_col)
        works.append(jnp.broadcast_to(True if keep is None else keep(here_y, here_x), (COLS,)))
    far_ids = jnp.stack(far_ids)[:, None]
    near_ids = (here_row * COLS + order)[None, :]
    wanted = jnp.stack([near_ids * NBLOCKS + far_ids, far_ids * NBLOCKS + near_ids])
    listed = block_pairs[:, 0] * NBLOCKS + block_pairs[:, 1]
    found = jnp.any(wanted[..., None] == listed, axis=-1)
    both_ways = (jnp.arange(len(STAGES)) > 0)[:, None]
    flags = jnp.where(jnp.stack(works), found[0] + 2 * (found[1] & both_ways), 0).astype(jnp.int32)

    starts = {name: at for at, name in enumerate(STAGES)}

    def work(group, sums):
        at = starts[group[0]]
        return cells(
            order,
            flags[at : at + len(group)].reshape(-1),
            blocks,
            near_v,
            [far[name] for name in group],
            norms,
            rows,
            sums,
        )

    def give_back(group, parts):
        returned = []
        for name, part in zip(group, parts):
            back = [(to, source) for source, to in shift(*STAGES[name][0], STAGES[name][1])]
            returned.append(lax.ppermute(part, "row", back))
        return returned

    near_v = lax.all_gather(vectors, "col")
    sums, norms, rows, token = own_cells(order, flags[0], blocks, far["own"])

    far["a"], far["b"], far["c"] = tie([far["a"], far["b"], far["c"]], token, near_v)
    far["d"] = move(far["a"], -1, 0)
    far["e"] = move(far["c"], 0, -1)
    far["g"] = move(far["a"], 0, 1, left_half)
    far["h"] = move(far["b"], 1, 0)
    group1, group2, group3 = ("a", "b", "c"), ("d", "e", "g", "h"), ("f", "k")
    sums, parts, token = work(group1, sums)

    far["h"], far["e"], *parts = tie([far["h"], far["e"], *parts], token, far["d"], far["g"])
    far["f"] = move(far["h"], 0, 1)
    far["k"] = move(far["e"], -1, 0, top_half)
    returned1 = give_back(group1, parts)
    sums, parts, token = work(group2, sums)

    far["f"], far["k"], *parts = tie([far["f"], far["k"], *parts], *returned1)
    returned2 = give_back(group2, parts)
    sums, parts, token = work(group3, sums)

    sums, *parts = tie([sums, *parts], *returned2)
    returned = returned1 + returned2 + give_back(group3, parts)

    kept = sums[:SIDE] + swap(sums[SIDE:])
    summed = kept[0] + (turn(kept[1], 3) + turn(kept[2], 2) + turn(kept[3], 1))
    totals, degrees = summed[0:EIGS], summed[EIGS : EIGS + 1]
    for part in returned:
        part = part.astype(jnp.float32)
        totals, degrees = totals + part[0:EIGS], degrees + (part[EIGS : EIGS + 1] + part[ACC : ACC + 1])
    smoothed = totals / degrees
    gram = jnp.dot(
        smoothed, smoothed.T, precision=lax.Precision.HIGHEST, preferred_element_type=jnp.float32
    ) / (BLOCK * NBLOCKS)
    gram = gram + swap(gram)
    gram = gram + (turn(gram, 1) + turn(gram, 2) + turn(gram, 3))
    gram = gram + (move(gram, 0, 1) + move(gram, 0, 2) + move(gram, 0, 3))
    gram = gram + (move(gram, 1, 0) + move(gram, 2, 0) + move(gram, 3, 0))
    return solve(gram, smoothed)


def solution(mesh):
    return jax.shard_map(
        per_device,
        mesh=mesh,
        in_specs=(P("row", None), P(None, ("row", "col")), P()),
        out_specs=P(None, ("row", "col")),
        check_vma=False,
    )
```

```python
import functools
import math

import jax
import jax.numpy as jnp
from jax import lax
from jax.experimental import pallas as pl
from jax.experimental.pallas import tpu as pltpu
from jax.sharding import PartitionSpec as P

BLOCK = 512
WIDTH = 1024
EIGS = 64
NBLOCKS = 128
SIDE = 4
COLS = 8
CORES = 2
VROWS = BLOCK + EIGS // 2
PAYLOAD = VROWS + 16
ACC = EIGS + 8
SENT = EIGS + 16
SCALE = math.sqrt(math.log2(math.e) / math.sqrt(WIDTH))
COST = 8
NT = (((1,), (1,)), ((), ()))


def shift(dy, dx, keep=None):
    pairs = []
    for y in range(SIDE):
        for x in range(SIDE):
            to_y, to_x = (y + dy) % SIDE, (x + dx) % SIDE
            if keep is None or keep(to_y, to_x):
                pairs.append((y * SIDE + x, to_y * SIDE + to_x))
    return pairs


def left_half(y, x):
    return x < SIDE // 2


def top_half(y, x):
    return y < SIDE // 2


STAGES = {
    "own": ((0, 0), None),
    "a": ((0, 1), None),
    "b": ((1, 0), None),
    "c": ((-1, -1), None),
    "d": ((-1, 1), None),
    "e": ((-1, -2), None),
    "h": ((2, 0), top_half),
    "f": ((2, 1), None),
    "g": ((0, 2), left_half),
    "k": ((2, 2), top_half),
}


def row_norm(x):
    return lax.rsqrt(jnp.sum(x * x, axis=1, keepdims=True) * (1.0 / WIDTH) + 1e-06)


def payload_kernel(index_ref, x_ref, v_ref, out_ref):
    x = x_ref[0]
    out_ref[0:BLOCK, :] = x
    half = EIGS // 2
    out_ref[BLOCK:VROWS, 0:BLOCK] = v_ref[0:half, :]
    out_ref[BLOCK:VROWS, BLOCK : 2 * BLOCK] = v_ref[half:EIGS, :]
    norms = jnp.broadcast_to(row_norm(x.astype(jnp.float32)) * SCALE, (BLOCK, 128))
    rows = norms.T[0:16, :]
    high = rows.astype(jnp.bfloat16)
    low = (rows - high.astype(jnp.float32)).astype(jnp.bfloat16)
    out_ref[VROWS:PAYLOAD, 0:BLOCK] = high
    out_ref[VROWS:PAYLOAD, BLOCK : 2 * BLOCK] = low


def make_payload(here_col, blocks, vectors):
    return pl.pallas_call(
        payload_kernel,
        out_shape=jax.ShapeDtypeStruct((PAYLOAD, WIDTH), jnp.bfloat16),
        grid_spec=pltpu.PrefetchScalarGridSpec(
            num_scalar_prefetch=1,
            grid=(1,),
            in_specs=[
                pl.BlockSpec((1, BLOCK, WIDTH), lambda g, index: (index[0], 0, 0)),
                pl.BlockSpec((EIGS, BLOCK), lambda g, index: (0, 0)),
            ],
            out_specs=pl.BlockSpec((PAYLOAD, WIDTH), lambda g, index: (0, 0)),
        ),
        name="payload",
    )(here_col, blocks, vectors)


def side_vectors(side):
    half = EIGS // 2
    ones = jnp.ones((16, BLOCK), jnp.bfloat16)
    return jnp.concatenate([side[0:half, 0:BLOCK], side[0:half, BLOCK : 2 * BLOCK], ones], axis=0)


def side_norms(side):
    row = side[EIGS // 2 : EIGS // 2 + 1, :].astype(jnp.float32)
    return row[:, 0:BLOCK] + row[:, BLOCK : 2 * BLOCK]


def double(columns):
    return jnp.concatenate([columns, columns], axis=1)


def own_kernel(order_ref, flags_ref, x_ref, far_ref, new_ref, norm_ref, row_ref, token_ref, p_ref):
    step = pl.program_id(0)
    new_ref[...] = jnp.zeros_like(new_ref)
    token_ref[...] = jnp.zeros_like(token_ref)
    norms = jnp.broadcast_to(row_norm(x_ref[0].astype(jnp.float32)) * SCALE, (BLOCK, 128))
    norm_ref[0] = norms
    row_ref[0] = norms.T[0:8, :]

    @pl.when(flags_ref[step] > 0)
    def _():
        side = far_ref[BLOCK:PAYLOAD, :]
        near, far = double(norm_ref[0]), side_norms(side)
        for at in range(0, BLOCK, 256):
            scores = lax.dot_general(
                x_ref[0], far_ref[at : at + 256, :], NT, preferred_element_type=jnp.float32
            )
            p_ref[:, at : at + 256] = jnp.exp2(scores * near * far[:, at : at + 256]).astype(jnp.bfloat16)
        part = lax.dot_general(side_vectors(side), p_ref[...], NT, preferred_element_type=jnp.float32)
        new_ref[0] = part[0:ACC, :]


def cells_kernel(count, order_ref, flags_ref, x_ref, near_v_ref, *refs):
    far_refs, refs = refs[:count], refs[count:]
    norm_ref, row_ref, old_ref, new_ref, refs = refs[0], refs[1], refs[2], refs[3], refs[4:]
    sent_refs, token_ref, (p_ref, column_ref, far_sums_ref) = refs[:count], refs[count], refs[count + 1 :]
    step = pl.program_id(0)

    @pl.when(step == 0)
    def _():
        token_ref[...] = jnp.zeros_like(token_ref)
        far_sums_ref[...] = jnp.zeros_like(far_sums_ref)
        for at in range(count):
            column_ref[at] = jnp.broadcast_to(side_norms(far_refs[at][BLOCK:PAYLOAD, :]), (128, BLOCK)).T

    new_ref[...] = old_ref[...]

    def forward_only(at):
        far_ref = far_refs[at]
        near, far = row_ref[0, 0:1, :], double(column_ref[at])
        for to in range(0, BLOCK, 256):
            scores = lax.dot_general(
                far_ref[0:BLOCK, :], x_ref[0, to : to + 256, :], NT, preferred_element_type=jnp.float32
            )
            p_ref[:, to : to + 256] = jnp.exp2(scores * near[:, to : to + 256] * far).astype(jnp.bfloat16)
        part = jnp.dot(side_vectors(far_ref[BLOCK:PAYLOAD, :]), p_ref[...], preferred_element_type=jnp.float32)
        new_ref[0] += part[0:ACC, :]

    def backward(at, both):
        far_ref = far_refs[at]
        side = far_ref[BLOCK:PAYLOAD, :]
        near, far = double(norm_ref[0]), side_norms(side)
        for to in range(0, BLOCK, 256):
            scores = lax.dot_general(
                x_ref[0], far_ref[to : to + 256, :], NT, preferred_element_type=jnp.float32
            )
            p_ref[:, to : to + 256] = jnp.exp2(scores * near * far[:, to : to + 256]).astype(jnp.bfloat16)
        vectors = jnp.concatenate([near_v_ref[0], jnp.ones((16, BLOCK), jnp.bfloat16)], axis=0)
        part = jnp.dot(vectors, p_ref[...], preferred_element_type=jnp.float32)
        far_sums_ref[at] += part[0:ACC, :]
        if both:
            part = lax.dot_general(side_vectors(side), p_ref[...], NT, preferred_element_type=jnp.float32)
            new_ref[0] += part[0:ACC, :]

    for at in range(count):
        flag = flags_ref[at * COLS + step]
        pl.when(flag == 1)(functools.partial(forward_only, at))
        pl.when(flag == 2)(functools.partial(backward, at, False))
        pl.when(flag == 3)(functools.partial(backward, at, True))

    @pl.when(step == COLS - 1)
    def _():
        for at in range(count):
            degrees = far_sums_ref[at, EIGS:ACC, :]
            high = degrees.astype(jnp.bfloat16).astype(jnp.float32)
            sent = jnp.concatenate([far_sums_ref[at, 0:EIGS, :], high, degrees - high], axis=0)
            sent_refs[at][...] = sent.astype(jnp.bfloat16)


NEAR = lambda g, order, flags: (order[g], 0, 0)
STEP = lambda g, order, flags: (g, 0, 0)
WHOLE = lambda g, order, flags: (0, 0)
X_SPEC = pl.BlockSpec((1, BLOCK, WIDTH), NEAR)
FAR_SPEC = pl.BlockSpec((PAYLOAD, WIDTH), WHOLE)
NORM = (pl.BlockSpec((1, BLOCK, 128), STEP), (COLS, BLOCK, 128), jnp.float32)
ROW = (pl.BlockSpec((1, 8, BLOCK), STEP), (COLS, 8, BLOCK), jnp.float32)
SUMS = (pl.BlockSpec((1, ACC, BLOCK), STEP), (COLS, ACC, BLOCK), jnp.float32)
PART = (pl.BlockSpec((SENT, BLOCK), WHOLE), (SENT, BLOCK), jnp.bfloat16)
TOKEN = (pl.BlockSpec((8, 128), WHOLE), (8, 128), jnp.float32)


def cells_call(kernel, count, ins, outs, scratch, aliases, name, args):
    return pl.pallas_call(
        kernel,
        out_shape=[jax.ShapeDtypeStruct(shape, dtype) for _, shape, dtype in outs],
        grid_spec=pltpu.PrefetchScalarGridSpec(
            num_scalar_prefetch=2, grid=(COLS,), in_specs=ins, out_specs=[spec for spec, _, _ in outs], scratch_shapes=scratch
        ),
        input_output_aliases=aliases,
        compiler_params=pltpu.CompilerParams(vmem_limit_bytes=56 << 20),
        cost_estimate=pl.CostEstimate(
            flops=count * COST * BLOCK * BLOCK * WIDTH,
            bytes_accessed=(12 + count) << 20,
            transcendentals=count * 4 * BLOCK * BLOCK,
        ),
        name=name,
    )(*args)


SCORES = pltpu.VMEM((BLOCK, BLOCK), jnp.bfloat16)


def own_cells(order, flags, blocks, far):
    ins, outs = [X_SPEC, FAR_SPEC], [SUMS, NORM, ROW, TOKEN]
    return cells_call(own_kernel, 1, ins, outs, [SCORES], {}, "cells_own", (order, flags, blocks, far))


def cells(order, flags, blocks, near_v, fars, norms, rows, sums):
    count = len(fars)
    ins = [X_SPEC, pl.BlockSpec((1, EIGS, BLOCK), NEAR)] + [FAR_SPEC] * count + [NORM[0], ROW[0], SUMS[0]]
    outs = [SUMS] + [PART] * count + [TOKEN]
    scratch = [SCORES] + [pltpu.VMEM((count, *shape), jnp.float32) for shape in ((BLOCK, 128), (ACC, BLOCK))]
    args = (order, flags, blocks, near_v, *fars, norms, rows, sums)
    kernel = functools.partial(cells_kernel, count)
    result = cells_call(kernel, count, ins, outs, scratch, {6 + count: 0}, "cells", args)
    return result[0], result[1:-1], result[-1]


def tie_kernel(*refs):
    pass


def tie(arrays, *tokens):
    return pl.pallas_call(
        tie_kernel,
        out_shape=[jax.ShapeDtypeStruct(array.shape, array.dtype) for array in arrays],
        in_specs=[pl.BlockSpec(memory_space=pltpu.HBM)] * (len(arrays) + len(tokens)),
        out_specs=[pl.BlockSpec(memory_space=pltpu.HBM)] * len(arrays),
        input_output_aliases={at: at for at in range(len(arrays))},
        name="tie",
    )(*arrays, *tokens)


def solve_kernel(gram_ref, smoothed_ref, out_ref):
    rows = lax.broadcasted_iota(jnp.int32, (EIGS, 2 * EIGS), 0)
    lanes = lax.broadcasted_iota(jnp.int32, (EIGS, 2 * EIGS), 1)
    eye = jnp.where(rows + EIGS == lanes, 1.0, 0.0)[:, EIGS:]
    work = jnp.concatenate([gram_ref[...], eye], axis=1)
    below = rows[0:8, :]
    tiles, done = [work[at : at + 8, :] for at in range(0, EIGS, 8)], []
    while tiles:
        for j in range(0, 8, 2):
            at = len(done) * 8 + j
            columns1 = [jnp.broadcast_to(tile[:, at : at + 1], tile.shape) for tile in tiles]
            columns2 = [jnp.broadcast_to(tile[:, at + 1 : at + 2], tile.shape) for tile in tiles]
            first, cross = columns1[0][j : j + 1, :], columns1[0][j + 1 : j + 2, :]
            second = columns2[0][j + 1 : j + 2, :]
            row1, row2 = tiles[0][j : j + 1, :], tiles[0][j + 1 : j + 2, :]
            scale = 1.0 / (first * second - cross * cross)
            scaled1 = (second * row1 - cross * row2) * scale
            scaled2 = (first * row2 - cross * row1) * scale
            ratio = cross / first
            columns1[0] = jnp.where(below > j + 1, columns1[0], 0.0)
            columns2[0] = jnp.where(below > j + 1, columns2[0], 0.0)
            tiles = [
                tile - (column1 * scaled1 + column2 * scaled2)
                for tile, column1, column2 in zip(tiles, columns1, columns2)
            ]
            tiles[0] = jnp.where(below == j, row1 * lax.rsqrt(first), tiles[0])
            last = (row2 - ratio * row1) * lax.rsqrt(second - ratio * cross)
            tiles[0] = jnp.where(below == j + 1, last, tiles[0])
        done.append(tiles.pop(0))
    inverse = jnp.concatenate(done, axis=0)[:, EIGS:]
    out_ref[...] = jnp.dot(
        inverse, smoothed_ref[...], precision=lax.Precision.HIGHEST, preferred_element_type=jnp.float32
    )


def solve(gram, smoothed):
    return pl.pallas_call(
        solve_kernel,
        out_shape=jax.ShapeDtypeStruct(smoothed.shape, jnp.float32),
        in_specs=[pl.BlockSpec(memory_space=pltpu.VMEM)] * 2,
        out_specs=pl.BlockSpec(memory_space=pltpu.VMEM),
        name="solve",
    )(gram, smoothed)


def per_device(embeddings, vectors, block_pairs):
    here_row = lax.axis_index("row")
    here_col = lax.axis_index("col")
    here_y, here_x = here_row // SIDE, here_row % SIDE
    blocks = embeddings.reshape(COLS, BLOCK, WIDTH)

    def move(array, dy, dx, keep=None):
        return lax.ppermute(array, "row", shift(dy, dx, keep))

    def turn(array, by):
        return lax.ppermute(array, "col", [(i, (i + by * CORES) % COLS) for i in range(COLS)])

    def swap(array):
        return lax.ppermute(array, "col", [(i, i ^ 1) for i in range(COLS)])

    far = {"own": make_payload(here_col[None], blocks, vectors)}
    far["a"] = move(far["own"], 0, 1)
    far["b"] = move(far["own"], 1, 0)
    far["c"] = move(far["own"], -1, -1)
    order = jnp.stack([(here_col - CORES * k) % COLS ^ core for core in range(CORES) for k in range(SIDE)])

    far_ids, works = [], []
    for (dy, dx), keep in STAGES.values():
        from_row = (here_y - dy) % SIDE * SIDE + (here_x - dx) % SIDE
        far_ids.append(from_row * COLS + here_col)
        works.append(jnp.broadcast_to(True if keep is None else keep(here_y, here_x), (COLS,)))
    far_ids = jnp.stack(far_ids)[:, None]
    near_ids = (here_row * COLS + order)[None, :]
    wanted = jnp.stack([near_ids * NBLOCKS + far_ids, far_ids * NBLOCKS + near_ids])
    listed = block_pairs[:, 0] * NBLOCKS + block_pairs[:, 1]
    found = jnp.any(wanted[..., None] == listed, axis=-1)
    both_ways = (jnp.arange(len(STAGES)) > 0)[:, None]
    flags = jnp.where(jnp.stack(works), found[0] + 2 * (found[1] & both_ways), 0).astype(jnp.int32)

    starts = {name: at for at, name in enumerate(STAGES)}

    def work(group, sums):
        at = starts[group[0]]
        return cells(
            order,
            flags[at : at + len(group)].reshape(-1),
            blocks,
            near_v,
            [far[name] for name in group],
            norms,
            rows,
            sums,
        )

    def give_back(group, parts):
        returned = []
        for name, part in zip(group, parts):
            back = [(to, source) for source, to in shift(*STAGES[name][0], STAGES[name][1])]
            returned.append(lax.ppermute(part, "row", back))
        return returned

    near_v = lax.all_gather(vectors, "col")
    sums, norms, rows, token = own_cells(order, flags[0], blocks, far["own"])

    far["a"], far["b"], far["c"] = tie([far["a"], far["b"], far["c"]], token, near_v)
    far["d"] = move(far["a"], -1, 0)
    far["e"] = move(far["c"], 0, -1)
    far["g"] = move(far["a"], 0, 1, left_half)
    far["h"] = move(far["b"], 1, 0)
    group1, group2, group3 = ("a", "b", "c"), ("d", "e", "h"), ("f", "g", "k")
    sums, parts, token = work(group1, sums)

    far["h"], far["e"], *parts = tie([far["h"], far["e"], *parts], token, far["d"], far["g"])
    far["f"] = move(far["h"], 0, 1)
    far["k"] = move(far["e"], -1, 0, top_half)
    returned1 = give_back(group1, parts)
    sums, parts, token = work(group2, sums)

    far["f"], far["k"], *parts = tie([far["f"], far["k"], *parts], *returned1)
    returned2 = give_back(group2, parts)
    sums, parts, token = work(group3, sums)

    sums, *parts = tie([sums, *parts], *returned2)
    returned = returned1 + returned2 + give_back(group3, parts)

    kept = sums[:SIDE] + swap(sums[SIDE:])
    summed = kept[0] + (turn(kept[1], 3) + turn(kept[2], 2) + turn(kept[3], 1))
    totals, degrees = summed[0:EIGS], summed[EIGS : EIGS + 1]
    for part in returned:
        part = part.astype(jnp.float32)
        totals, degrees = totals + part[0:EIGS], degrees + (part[EIGS : EIGS + 1] + part[ACC : ACC + 1])
    smoothed = totals / degrees
    gram = jnp.dot(
        smoothed, smoothed.T, precision=lax.Precision.HIGHEST, preferred_element_type=jnp.float32
    ) / (BLOCK * NBLOCKS)
    gram = gram + swap(gram)
    gram = gram + (turn(gram, 1) + turn(gram, 2) + turn(gram, 3))
    everyone = jnp.broadcast_to(gram, (SIDE * SIDE, EIGS, EIGS))
    gram = jnp.sum(lax.all_to_all(everyone, "row", 0, 0), axis=0)
    return solve(gram, smoothed)


def solution(mesh):
    return jax.shard_map(
        per_device,
        mesh=mesh,
        in_specs=(P("row", None), P(None, ("row", "col")), P()),
        out_specs=P(None, ("row", "col")),
        check_vma=False,
    )
```

```python
import functools
import math

import jax
import jax.numpy as jnp
from jax import lax
from jax.experimental import pallas as pl
from jax.experimental.pallas import tpu as pltpu
from jax.sharding import PartitionSpec as P

BLOCK = 512
WIDTH = 1024
EIGS = 64
NBLOCKS = 128
SIDE = 4
COLS = 8
CORES = 2
VROWS = BLOCK + EIGS // 2
PAYLOAD = VROWS + 16
ACC = EIGS + 8
SENT = EIGS + 16
SCALE = math.sqrt(math.log2(math.e) / math.sqrt(WIDTH))
COST = 8
NT = (((1,), (1,)), ((), ()))


def shift(dy, dx, keep=None):
    pairs = []
    for y in range(SIDE):
        for x in range(SIDE):
            to_y, to_x = (y + dy) % SIDE, (x + dx) % SIDE
            if keep is None or keep(to_y, to_x):
                pairs.append((y * SIDE + x, to_y * SIDE + to_x))
    return pairs


def left_half(y, x):
    return x < SIDE // 2


def top_half(y, x):
    return y < SIDE // 2


STAGES = {
    "own": ((0, 0), None),
    "a": ((0, 1), None),
    "b": ((1, 0), None),
    "c": ((-1, -1), None),
    "d": ((-1, 1), None),
    "e": ((-1, -2), None),
    "h": ((2, 0), top_half),
    "f": ((2, 1), None),
    "g": ((0, 2), left_half),
    "k": ((2, 2), top_half),
}


def row_norm(x):
    return lax.rsqrt(jnp.sum(x * x, axis=1, keepdims=True) * (1.0 / WIDTH) + 1e-06)


def payload_kernel(index_ref, x_ref, v_ref, out_ref):
    x = x_ref[0]
    out_ref[0:BLOCK, :] = x
    half = EIGS // 2
    out_ref[BLOCK:VROWS, 0:BLOCK] = v_ref[0:half, :]
    out_ref[BLOCK:VROWS, BLOCK : 2 * BLOCK] = v_ref[half:EIGS, :]
    norms = jnp.broadcast_to(row_norm(x.astype(jnp.float32)) * SCALE, (BLOCK, 128))
    rows = norms.T[0:16, :]
    high = rows.astype(jnp.bfloat16)
    low = (rows - high.astype(jnp.float32)).astype(jnp.bfloat16)
    out_ref[VROWS:PAYLOAD, 0:BLOCK] = high
    out_ref[VROWS:PAYLOAD, BLOCK : 2 * BLOCK] = low


def make_payload(here_col, blocks, vectors):
    return pl.pallas_call(
        payload_kernel,
        out_shape=jax.ShapeDtypeStruct((PAYLOAD, WIDTH), jnp.bfloat16),
        grid_spec=pltpu.PrefetchScalarGridSpec(
            num_scalar_prefetch=1,
            grid=(1,),
            in_specs=[
                pl.BlockSpec((1, BLOCK, WIDTH), lambda g, index: (index[0], 0, 0)),
                pl.BlockSpec((EIGS, BLOCK), lambda g, index: (0, 0)),
            ],
            out_specs=pl.BlockSpec((PAYLOAD, WIDTH), lambda g, index: (0, 0)),
        ),
        name="payload",
    )(here_col, blocks, vectors)


def side_vectors(side):
    half = EIGS // 2
    ones = jnp.ones((16, BLOCK), jnp.bfloat16)
    return jnp.concatenate([side[0:half, 0:BLOCK], side[0:half, BLOCK : 2 * BLOCK], ones], axis=0)


def side_norms(side):
    row = side[EIGS // 2 : EIGS // 2 + 1, :].astype(jnp.float32)
    return row[:, 0:BLOCK] + row[:, BLOCK : 2 * BLOCK]


def double(columns):
    return jnp.concatenate([columns, columns], axis=1)


def own_kernel(flags_ref, x_ref, far_ref, new_ref, norm_ref, row_ref, token_ref, p_ref):
    step = pl.program_id(0)
    new_ref[...] = jnp.zeros_like(new_ref)
    token_ref[...] = jnp.zeros_like(token_ref)
    norms = jnp.broadcast_to(row_norm(x_ref[0].astype(jnp.float32)) * SCALE, (BLOCK, 128))
    norm_ref[0] = norms
    row_ref[0] = norms.T[0:8, :]

    @pl.when(flags_ref[step] > 0)
    def _():
        side = far_ref[BLOCK:PAYLOAD, :]
        near, far = double(norm_ref[0]), side_norms(side)
        for at in range(0, BLOCK, 256):
            scores = lax.dot_general(
                x_ref[0], far_ref[at : at + 256, :], NT, preferred_element_type=jnp.float32
            )
            p_ref[:, at : at + 256] = jnp.exp2(scores * near * far[:, at : at + 256]).astype(jnp.bfloat16)
        part = lax.dot_general(side_vectors(side), p_ref[...], NT, preferred_element_type=jnp.float32)
        new_ref[0] = part[0:ACC, :]


def cells_kernel(count, flags_ref, x_hbm, v_hbm, *refs):
    far_hbms, (norm_hbm, row_hbm, old_hbm, new_hbm), refs = refs[:count], refs[count : count + 4], refs[count + 4 :]
    sent_refs, token_ref, refs = refs[:count], refs[count], refs[count + 1 :]
    x_ref, v_ref, far_ref, norm_ref, row_ref, old_ref, sums_ref, p_ref, column_ref, far_sums_ref = refs[:10]
    near_sem, far_sem, sem = refs[10:]

    def near_copies(near):
        pairs = ((x_hbm, x_ref), (norm_hbm, norm_ref), (v_hbm, v_ref))
        return [
            pltpu.make_async_copy(source.at[near], to.at[near], near_sem.at[at, near])
            for at, (source, to) in enumerate(pairs)
        ]

    far_copies = [pltpu.make_async_copy(far_hbms[at], far_ref.at[at], far_sem.at[at]) for at in range(count)]
    row_copy = pltpu.make_async_copy(row_hbm, row_ref, sem.at[0])
    old_copy = pltpu.make_async_copy(old_hbm, old_ref, sem.at[1])
    for copy in (far_copies[0], *near_copies(0), row_copy, *far_copies[1:], *near_copies(1), old_copy):
        copy.start()

    token_ref[...] = jnp.zeros_like(token_ref)
    far_sums_ref[...] = jnp.zeros_like(far_sums_ref)
    sums_ref[...] = jnp.zeros_like(sums_ref)

    def forward_only(at, near):
        rows, far = row_ref[near, 0:1, :], double(column_ref[at])
        for to in range(0, BLOCK, 256):
            scores = lax.dot_general(
                far_ref[at, 0:BLOCK, :], x_ref[near, to : to + 256, :], NT, preferred_element_type=jnp.float32
            )
            p_ref[:, to : to + 256] = jnp.exp2(scores * rows[:, to : to + 256] * far).astype(jnp.bfloat16)
        part = jnp.dot(side_vectors(far_ref[at, BLOCK:PAYLOAD, :]), p_ref[...], preferred_element_type=jnp.float32)
        sums_ref[near] += part[0:ACC, :]

    def backward(at, near, both):
        side = far_ref[at, BLOCK:PAYLOAD, :]
        columns, far = double(norm_ref[near]), side_norms(side)
        for to in range(0, BLOCK, 256):
            scores = lax.dot_general(
                x_ref[near], far_ref[at, to : to + 256, :], NT, preferred_element_type=jnp.float32
            )
            p_ref[:, to : to + 256] = jnp.exp2(scores * columns * far[:, to : to + 256]).astype(jnp.bfloat16)
        vectors = jnp.concatenate([v_ref[near], jnp.ones((16, BLOCK), jnp.bfloat16)], axis=0)
        part = jnp.dot(vectors, p_ref[...], preferred_element_type=jnp.float32)
        far_sums_ref[at] += part[0:ACC, :]
        if both:
            part = lax.dot_general(side_vectors(side), p_ref[...], NT, preferred_element_type=jnp.float32)
            sums_ref[near] += part[0:ACC, :]

    @pl.loop(0, COLS)
    def _(near):
        @pl.when(near + 2 < COLS)
        def _():
            for copy in near_copies(near + 2):
                copy.start()

        for copy in near_copies(near):
            copy.wait()
        for at in range(count):

            @pl.when(near == 0)
            def _():
                if at == 0:
                    row_copy.wait()
                far_copies[at].wait()
                column_ref[at] = jnp.broadcast_to(side_norms(far_ref[at, BLOCK:PAYLOAD, :]), (128, BLOCK)).T

            flag = flags_ref[at * COLS + near]
            pl.when(flag == 1)(functools.partial(forward_only, at, near))
            pl.when(flag == 2)(functools.partial(backward, at, near, False))
            pl.when(flag == 3)(functools.partial(backward, at, near, True))

    old_copy.wait()
    sums_ref[...] += old_ref[...]
    out_copy = pltpu.make_async_copy(sums_ref, new_hbm, sem.at[0])
    out_copy.start()
    for at in range(count):
        degrees = far_sums_ref[at, EIGS:ACC, :]
        high = degrees.astype(jnp.bfloat16).astype(jnp.float32)
        sent = jnp.concatenate([far_sums_ref[at, 0:EIGS, :], high, degrees - high], axis=0)
        sent_refs[at][...] = sent.astype(jnp.bfloat16)
    out_copy.wait()


SUMS = jax.ShapeDtypeStruct((COLS, ACC, BLOCK), jnp.float32)
NORM = jax.ShapeDtypeStruct((COLS, BLOCK, 128), jnp.float32)
ROW = jax.ShapeDtypeStruct((COLS, 8, BLOCK), jnp.float32)
TOKEN = jax.ShapeDtypeStruct((8, 128), jnp.float32)
SENT_SHAPE = jax.ShapeDtypeStruct((SENT, BLOCK), jnp.bfloat16)


def block_of(shape):
    return pl.BlockSpec((1, *shape[1:]), lambda g, flags: (g, 0, 0))


def whole(shape):
    return pl.BlockSpec(shape, lambda g, flags: (0, 0))


def own_cells(flags, blocks, far):
    return pl.pallas_call(
        own_kernel,
        out_shape=[SUMS, NORM, ROW, TOKEN],
        grid_spec=pltpu.PrefetchScalarGridSpec(
            num_scalar_prefetch=1,
            grid=(COLS,),
            in_specs=[block_of(blocks.shape), whole(far.shape)],
            out_specs=[block_of(SUMS.shape), block_of(NORM.shape), block_of(ROW.shape), whole(TOKEN.shape)],
            scratch_shapes=[pltpu.VMEM((BLOCK, BLOCK), jnp.bfloat16)],
        ),
        compiler_params=pltpu.CompilerParams(vmem_limit_bytes=56 << 20),
        cost_estimate=estimate(1),
        name="cells_own",
    )(flags, blocks, far)


def estimate(count):
    return pl.CostEstimate(
        flops=count * COST * BLOCK * BLOCK * WIDTH,
        bytes_accessed=(12 + count) << 20,
        transcendentals=count * 4 * BLOCK * BLOCK,
    )


def cells(flags, blocks, near_v, fars, norms, rows, sums):
    count = len(fars)
    buffers = [
        ((COLS, BLOCK, WIDTH), jnp.bfloat16),
        ((COLS, EIGS, BLOCK), jnp.bfloat16),
        ((count, PAYLOAD, WIDTH), jnp.bfloat16),
        ((COLS, BLOCK, 128), jnp.float32),
        ((COLS, 8, BLOCK), jnp.float32),
        ((COLS, ACC, BLOCK), jnp.float32),
        ((COLS, ACC, BLOCK), jnp.float32),
        ((BLOCK, BLOCK), jnp.bfloat16),
        ((count, BLOCK, 128), jnp.float32),
        ((count, ACC, BLOCK), jnp.float32),
    ]
    in_place = pl.BlockSpec(memory_space=pltpu.HBM)
    result = pl.pallas_call(
        functools.partial(cells_kernel, count),
        out_shape=[SUMS] + [SENT_SHAPE] * count + [TOKEN],
        grid_spec=pltpu.PrefetchScalarGridSpec(
            num_scalar_prefetch=1,
            grid=(1,),
            in_specs=[in_place] * (5 + count),
            out_specs=[in_place] + [whole(SENT_SHAPE.shape)] * count + [whole(TOKEN.shape)],
            scratch_shapes=[pltpu.VMEM(*buffer) for buffer in buffers]
            + [pltpu.SemaphoreType.DMA(size) for size in ((3, COLS), (count,), (2,))],
        ),
        input_output_aliases={5 + count: 0},
        compiler_params=pltpu.CompilerParams(vmem_limit_bytes=56 << 20),
        cost_estimate=estimate(count),
        name="cells",
    )(flags, blocks, near_v, *fars, norms, rows, sums)
    return result[0], result[1:-1], result[-1]


def tie_kernel(*refs):
    pass


def tie(arrays, *tokens):
    return pl.pallas_call(
        tie_kernel,
        out_shape=[jax.ShapeDtypeStruct(array.shape, array.dtype) for array in arrays],
        in_specs=[pl.BlockSpec(memory_space=pltpu.HBM)] * (len(arrays) + len(tokens)),
        out_specs=[pl.BlockSpec(memory_space=pltpu.HBM)] * len(arrays),
        input_output_aliases={at: at for at in range(len(arrays))},
        name="tie",
    )(*arrays, *tokens)


def solve_kernel(gram_ref, smoothed_ref, out_ref):
    rows = lax.broadcasted_iota(jnp.int32, (EIGS, 2 * EIGS), 0)
    lanes = lax.broadcasted_iota(jnp.int32, (EIGS, 2 * EIGS), 1)
    eye = jnp.where(rows + EIGS == lanes, 1.0, 0.0)[:, EIGS:]
    work = jnp.concatenate([gram_ref[...], eye], axis=1)
    below = rows[0:8, :]
    tiles, done = [work[at : at + 8, :] for at in range(0, EIGS, 8)], []
    while tiles:
        for j in range(0, 8, 2):
            at = len(done) * 8 + j
            columns1 = [jnp.broadcast_to(tile[:, at : at + 1], tile.shape) for tile in tiles]
            columns2 = [jnp.broadcast_to(tile[:, at + 1 : at + 2], tile.shape) for tile in tiles]
            first, cross = columns1[0][j : j + 1, :], columns1[0][j + 1 : j + 2, :]
            second = columns2[0][j + 1 : j + 2, :]
            row1, row2 = tiles[0][j : j + 1, :], tiles[0][j + 1 : j + 2, :]
            scale = 1.0 / (first * second - cross * cross)
            scaled1 = (second * row1 - cross * row2) * scale
            scaled2 = (first * row2 - cross * row1) * scale
            ratio = cross / first
            columns1[0] = jnp.where(below > j + 1, columns1[0], 0.0)
            columns2[0] = jnp.where(below > j + 1, columns2[0], 0.0)
            tiles = [
                tile - (column1 * scaled1 + column2 * scaled2)
                for tile, column1, column2 in zip(tiles, columns1, columns2)
            ]
            tiles[0] = jnp.where(below == j, row1 * lax.rsqrt(first), tiles[0])
            last = (row2 - ratio * row1) * lax.rsqrt(second - ratio * cross)
            tiles[0] = jnp.where(below == j + 1, last, tiles[0])
        done.append(tiles.pop(0))
    inverse = jnp.concatenate(done, axis=0)[:, EIGS:]
    out_ref[...] = jnp.dot(
        inverse, smoothed_ref[...], precision=lax.Precision.HIGHEST, preferred_element_type=jnp.float32
    )


def solve(gram, smoothed):
    return pl.pallas_call(
        solve_kernel,
        out_shape=jax.ShapeDtypeStruct(smoothed.shape, jnp.float32),
        in_specs=[pl.BlockSpec(memory_space=pltpu.VMEM)] * 2,
        out_specs=pl.BlockSpec(memory_space=pltpu.VMEM),
        name="solve",
    )(gram, smoothed)


def per_device(embeddings, vectors, block_pairs):
    here_row = lax.axis_index("row")
    here_col = lax.axis_index("col")
    here_y, here_x = here_row // SIDE, here_row % SIDE
    blocks = embeddings.reshape(COLS, BLOCK, WIDTH)

    def move(array, dy, dx, keep=None):
        return lax.ppermute(array, "row", shift(dy, dx, keep))

    def turn(array, by):
        return lax.ppermute(array, "col", [(i, (i + by * CORES) % COLS) for i in range(COLS)])

    def swap(array):
        return lax.ppermute(array, "col", [(i, i ^ 1) for i in range(COLS)])

    far = {"own": make_payload(here_col[None], blocks, vectors)}
    far["a"] = move(far["own"], 0, 1)
    far["b"] = move(far["own"], 1, 0)
    far["c"] = move(far["own"], -1, -1)
    far_ids, works = [], []
    for (dy, dx), keep in STAGES.values():
        from_row = (here_y - dy) % SIDE * SIDE + (here_x - dx) % SIDE
        far_ids.append(from_row * COLS + here_col)
        works.append(jnp.broadcast_to(True if keep is None else keep(here_y, here_x), (COLS,)))
    far_ids = jnp.stack(far_ids)[:, None]
    near_ids = (here_row * COLS + jnp.arange(COLS, dtype=jnp.int32))[None, :]
    wanted = jnp.stack([near_ids * NBLOCKS + far_ids, far_ids * NBLOCKS + near_ids])
    listed = block_pairs[:, 0] * NBLOCKS + block_pairs[:, 1]
    found = jnp.any(wanted[..., None] == listed, axis=-1)
    both_ways = (jnp.arange(len(STAGES)) > 0)[:, None]
    flags = jnp.where(jnp.stack(works), found[0] + 2 * (found[1] & both_ways), 0).astype(jnp.int32)

    starts = {name: at for at, name in enumerate(STAGES)}

    def work(group, sums):
        at = starts[group[0]]
        return cells(
            flags[at : at + len(group)].reshape(-1),
            blocks,
            near_v,
            [far[name] for name in group],
            norms,
            rows,
            sums,
        )

    def give_back(group, parts):
        returned = []
        for name, part in zip(group, parts):
            back = [(to, source) for source, to in shift(*STAGES[name][0], STAGES[name][1])]
            returned.append(lax.ppermute(part, "row", back))
        return returned

    near_v = lax.all_gather(vectors, "col")
    sums, norms, rows, token = own_cells(flags[0], blocks, far["own"])

    far["a"], far["b"], far["c"] = tie([far["a"], far["b"], far["c"]], token, near_v)
    far["d"] = move(far["a"], -1, 0)
    far["e"] = move(far["c"], 0, -1)
    far["g"] = move(far["a"], 0, 1, left_half)
    far["h"] = move(far["b"], 1, 0)
    group1, group2, group3 = ("a", "b", "c"), ("d", "e", "h"), ("f", "g", "k")
    sums, parts, token = work(group1, sums)

    far["h"], far["e"], *parts = tie([far["h"], far["e"], *parts], token, far["d"], far["g"])
    far["f"] = move(far["h"], 0, 1)
    far["k"] = move(far["e"], -1, 0, top_half)
    returned1 = give_back(group1, parts)
    sums, parts, token = work(group2, sums)

    far["f"], far["k"], *parts = tie([far["f"], far["k"], *parts], *returned1)
    returned2 = give_back(group2, parts)
    sums, parts, token = work(group3, sums)

    sums, *parts = tie([sums, *parts], *returned2)
    returned = returned1 + returned2 + give_back(group3, parts)

    layer, core = here_col // CORES, here_col % CORES
    halves = sums.reshape(SIDE, CORES, ACC, BLOCK)
    mine = lax.dynamic_index_in_dim(halves, core, 1, keepdims=False)
    kept = mine + swap(lax.dynamic_index_in_dim(halves, 1 - core, 1, keepdims=False))
    layers = [lax.dynamic_index_in_dim(kept, (layer - k) % SIDE, 0, keepdims=False) for k in range(SIDE)]
    summed = layers[0] + (turn(layers[1], 3) + turn(layers[2], 2) + turn(layers[3], 1))
    totals, degrees = summed[0:EIGS], summed[EIGS : EIGS + 1]
    for part in returned:
        part = part.astype(jnp.float32)
        totals, degrees = totals + part[0:EIGS], degrees + (part[EIGS : EIGS + 1] + part[ACC : ACC + 1])
    smoothed = totals / degrees
    gram = jnp.dot(
        smoothed, smoothed.T, precision=lax.Precision.HIGHEST, preferred_element_type=jnp.float32
    ) / (BLOCK * NBLOCKS)
    gram = gram + swap(gram)
    gram = gram + (turn(gram, 1) + turn(gram, 2) + turn(gram, 3))
    everyone = jnp.broadcast_to(gram, (SIDE * SIDE, EIGS, EIGS))
    gram = jnp.sum(lax.all_to_all(everyone, "row", 0, 0), axis=0)
    return solve(gram, smoothed)


def solution(mesh):
    return jax.shard_map(
        per_device,
        mesh=mesh,
        in_specs=(P("row", None), P(None, ("row", "col")), P()),
        out_specs=P(None, ("row", "col")),
        check_vma=False,
    )
```

```python
import functools
import math

import jax
import jax.numpy as jnp
from jax import lax
from jax.experimental import pallas as pl
from jax.experimental.pallas import tpu as pltpu
from jax.sharding import PartitionSpec as P

BLOCK = 512
WIDTH = 1024
EIGS = 64
NBLOCKS = 128
SIDE = 4
COLS = 8
CORES = 2
VROWS = BLOCK + EIGS // 2
PAYLOAD = VROWS + 16
ACC = EIGS + 8
SENT = EIGS + 16
SCALE = math.sqrt(math.log2(math.e) / math.sqrt(WIDTH))
COST = 8
NT = (((1,), (1,)), ((), ()))


def shift(dy, dx, keep=None):
    pairs = []
    for y in range(SIDE):
        for x in range(SIDE):
            to_y, to_x = (y + dy) % SIDE, (x + dx) % SIDE
            if keep is None or keep(to_y, to_x):
                pairs.append((y * SIDE + x, to_y * SIDE + to_x))
    return pairs


def left_half(y, x):
    return x < SIDE // 2


def top_half(y, x):
    return y < SIDE // 2


STAGES = {
    "own": ((0, 0), None),
    "a": ((0, 1), None),
    "b": ((1, 0), None),
    "c": ((-1, -1), None),
    "d": ((-1, 1), None),
    "e": ((-1, -2), None),
    "h": ((2, 0), top_half),
    "f": ((-2, -1), None),
    "g": ((0, 2), left_half),
    "k": ((2, 2), top_half),
}


def row_norm(x):
    return lax.rsqrt(jnp.sum(x * x, axis=1, keepdims=True) * (1.0 / WIDTH) + 1e-06)


def payload_kernel(index_ref, x_ref, v_ref, out_ref):
    x = x_ref[0]
    out_ref[0:BLOCK, :] = x
    half = EIGS // 2
    out_ref[BLOCK:VROWS, 0:BLOCK] = v_ref[0:half, :]
    out_ref[BLOCK:VROWS, BLOCK : 2 * BLOCK] = v_ref[half:EIGS, :]
    norms = jnp.broadcast_to(row_norm(x.astype(jnp.float32)) * SCALE, (BLOCK, 128))
    rows = norms.T[0:16, :]
    high = rows.astype(jnp.bfloat16)
    low = (rows - high.astype(jnp.float32)).astype(jnp.bfloat16)
    out_ref[VROWS:PAYLOAD, 0:BLOCK] = high
    out_ref[VROWS:PAYLOAD, BLOCK : 2 * BLOCK] = low


def make_payload(here_col, blocks, vectors):
    return pl.pallas_call(
        payload_kernel,
        out_shape=jax.ShapeDtypeStruct((PAYLOAD, WIDTH), jnp.bfloat16),
        grid_spec=pltpu.PrefetchScalarGridSpec(
            num_scalar_prefetch=1,
            grid=(1,),
            in_specs=[
                pl.BlockSpec((1, BLOCK, WIDTH), lambda g, index: (index[0], 0, 0)),
                pl.BlockSpec((EIGS, BLOCK), lambda g, index: (0, 0)),
            ],
            out_specs=pl.BlockSpec((PAYLOAD, WIDTH), lambda g, index: (0, 0)),
        ),
        name="payload",
    )(here_col, blocks, vectors)


def side_vectors(side):
    half = EIGS // 2
    ones = jnp.ones((16, BLOCK), jnp.bfloat16)
    return jnp.concatenate([side[0:half, 0:BLOCK], side[0:half, BLOCK : 2 * BLOCK], ones], axis=0)


def side_norms(side):
    row = side[EIGS // 2 : EIGS // 2 + 1, :].astype(jnp.float32)
    return row[:, 0:BLOCK] + row[:, BLOCK : 2 * BLOCK]


def double(columns):
    return jnp.concatenate([columns, columns], axis=1)


def own_kernel(flags_ref, x_ref, far_ref, new_ref, norm_ref, row_ref, token_ref, p_ref):
    step = pl.program_id(0)
    new_ref[...] = jnp.zeros_like(new_ref)
    token_ref[...] = jnp.zeros_like(token_ref)
    norms = jnp.broadcast_to(row_norm(x_ref[0].astype(jnp.float32)) * SCALE, (BLOCK, 128))
    norm_ref[0] = norms
    row_ref[0] = norms.T[0:8, :]

    @pl.when(flags_ref[step] > 0)
    def _():
        side = far_ref[BLOCK:PAYLOAD, :]
        near, far = double(norm_ref[0]), side_norms(side)
        for at in range(0, BLOCK, 256):
            scores = lax.dot_general(
                x_ref[0], far_ref[at : at + 256, :], NT, preferred_element_type=jnp.float32
            )
            p_ref[:, at : at + 256] = jnp.exp2(scores * near * far[:, at : at + 256]).astype(jnp.bfloat16)
        part = lax.dot_general(side_vectors(side), p_ref[...], NT, preferred_element_type=jnp.float32)
        new_ref[0] = part[0:ACC, :]


def cells_kernel(count, flags_ref, x_hbm, v_hbm, *refs):
    far_hbms, (norm_hbm, row_hbm, old_hbm, new_hbm), refs = refs[:count], refs[count : count + 4], refs[count + 4 :]
    sent_refs, token_ref, refs = refs[:count], refs[count], refs[count + 1 :]
    x_ref, v_ref, far_ref, norm_ref, row_ref, old_ref, sums_ref, p_ref, column_ref, far_sums_ref = refs[:10]
    near_sem, far_sem, sem = refs[10:]

    def near_copies(near):
        pairs = ((x_hbm, x_ref), (norm_hbm, norm_ref), (v_hbm, v_ref))
        return [
            pltpu.make_async_copy(source.at[near], to.at[near], near_sem.at[at, near])
            for at, (source, to) in enumerate(pairs)
        ]

    far_copies = [pltpu.make_async_copy(far_hbms[at], far_ref.at[at], far_sem.at[at]) for at in range(count)]
    row_copy = pltpu.make_async_copy(row_hbm, row_ref, sem.at[0])
    old_copy = pltpu.make_async_copy(old_hbm, old_ref, sem.at[1])
    for copy in (far_copies[0], *near_copies(0), row_copy, *far_copies[1:], *near_copies(1), old_copy):
        copy.start()

    token_ref[...] = jnp.zeros_like(token_ref)
    far_sums_ref[...] = jnp.zeros_like(far_sums_ref)
    sums_ref[...] = jnp.zeros_like(sums_ref)

    def forward_only(at, near):
        rows, far = row_ref[near, 0:1, :], double(column_ref[at])
        for to in range(0, BLOCK, 256):
            scores = lax.dot_general(
                far_ref[at, 0:BLOCK, :], x_ref[near, to : to + 256, :], NT, preferred_element_type=jnp.float32
            )
            p_ref[:, to : to + 256] = jnp.exp2(scores * rows[:, to : to + 256] * far).astype(jnp.bfloat16)
        part = jnp.dot(side_vectors(far_ref[at, BLOCK:PAYLOAD, :]), p_ref[...], preferred_element_type=jnp.float32)
        sums_ref[near] += part[0:ACC, :]

    def backward(at, near, both):
        side = far_ref[at, BLOCK:PAYLOAD, :]
        columns, far = double(norm_ref[near]), side_norms(side)
        for to in range(0, BLOCK, 256):
            scores = lax.dot_general(
                x_ref[near], far_ref[at, to : to + 256, :], NT, preferred_element_type=jnp.float32
            )
            p_ref[:, to : to + 256] = jnp.exp2(scores * columns * far[:, to : to + 256]).astype(jnp.bfloat16)
        vectors = jnp.concatenate([v_ref[near], jnp.ones((16, BLOCK), jnp.bfloat16)], axis=0)
        part = jnp.dot(vectors, p_ref[...], preferred_element_type=jnp.float32)
        far_sums_ref[at] += part[0:ACC, :]
        if both:
            part = lax.dot_general(side_vectors(side), p_ref[...], NT, preferred_element_type=jnp.float32)
            sums_ref[near] += part[0:ACC, :]

    @pl.loop(0, COLS)
    def _(near):
        @pl.when(near + 2 < COLS)
        def _():
            for copy in near_copies(near + 2):
                copy.start()

        for copy in near_copies(near):
            copy.wait()
        for at in range(count):

            @pl.when(near == 0)
            def _():
                if at == 0:
                    row_copy.wait()
                far_copies[at].wait()
                column_ref[at] = jnp.broadcast_to(side_norms(far_ref[at, BLOCK:PAYLOAD, :]), (128, BLOCK)).T

            flag = flags_ref[at * COLS + near]
            pl.when(flag == 1)(functools.partial(forward_only, at, near))
            pl.when(flag == 2)(functools.partial(backward, at, near, False))
            pl.when(flag == 3)(functools.partial(backward, at, near, True))

    old_copy.wait()
    sums_ref[...] += old_ref[...]
    out_copy = pltpu.make_async_copy(sums_ref, new_hbm, sem.at[0])
    out_copy.start()
    for at in range(count):
        degrees = far_sums_ref[at, EIGS:ACC, :]
        high = degrees.astype(jnp.bfloat16).astype(jnp.float32)
        sent = jnp.concatenate([far_sums_ref[at, 0:EIGS, :], high, degrees - high], axis=0)
        sent_refs[at][...] = sent.astype(jnp.bfloat16)
    out_copy.wait()


SUMS = jax.ShapeDtypeStruct((COLS, ACC, BLOCK), jnp.float32)
NORM = jax.ShapeDtypeStruct((COLS, BLOCK, 128), jnp.float32)
ROW = jax.ShapeDtypeStruct((COLS, 8, BLOCK), jnp.float32)
TOKEN = jax.ShapeDtypeStruct((8, 128), jnp.float32)
SENT_SHAPE = jax.ShapeDtypeStruct((SENT, BLOCK), jnp.bfloat16)


def block_of(shape):
    return pl.BlockSpec((1, *shape[1:]), lambda g, flags: (g, 0, 0))


def whole(shape):
    return pl.BlockSpec(shape, lambda g, flags: (0, 0))


def own_cells(flags, blocks, far):
    return pl.pallas_call(
        own_kernel,
        out_shape=[SUMS, NORM, ROW, TOKEN],
        grid_spec=pltpu.PrefetchScalarGridSpec(
            num_scalar_prefetch=1,
            grid=(COLS,),
            in_specs=[block_of(blocks.shape), whole(far.shape)],
            out_specs=[block_of(SUMS.shape), block_of(NORM.shape), block_of(ROW.shape), whole(TOKEN.shape)],
            scratch_shapes=[pltpu.VMEM((BLOCK, BLOCK), jnp.bfloat16)],
        ),
        compiler_params=pltpu.CompilerParams(vmem_limit_bytes=56 << 20),
        cost_estimate=estimate(1),
        name="cells_own",
    )(flags, blocks, far)


def estimate(count):
    return pl.CostEstimate(
        flops=count * COST * BLOCK * BLOCK * WIDTH,
        bytes_accessed=(12 + count) << 20,
        transcendentals=count * 4 * BLOCK * BLOCK,
    )


def cells(flags, blocks, near_v, fars, norms, rows, sums):
    count = len(fars)
    buffers = [
        ((COLS, BLOCK, WIDTH), jnp.bfloat16),
        ((COLS, EIGS, BLOCK), jnp.bfloat16),
        ((count, PAYLOAD, WIDTH), jnp.bfloat16),
        ((COLS, BLOCK, 128), jnp.float32),
        ((COLS, 8, BLOCK), jnp.float32),
        ((COLS, ACC, BLOCK), jnp.float32),
        ((COLS, ACC, BLOCK), jnp.float32),
        ((BLOCK, BLOCK), jnp.bfloat16),
        ((count, BLOCK, 128), jnp.float32),
        ((count, ACC, BLOCK), jnp.float32),
    ]
    in_place = pl.BlockSpec(memory_space=pltpu.HBM)
    result = pl.pallas_call(
        functools.partial(cells_kernel, count),
        out_shape=[SUMS] + [SENT_SHAPE] * count + [TOKEN],
        grid_spec=pltpu.PrefetchScalarGridSpec(
            num_scalar_prefetch=1,
            grid=(1,),
            in_specs=[in_place] * (5 + count),
            out_specs=[in_place] + [whole(SENT_SHAPE.shape)] * count + [whole(TOKEN.shape)],
            scratch_shapes=[pltpu.VMEM(*buffer) for buffer in buffers]
            + [pltpu.SemaphoreType.DMA(size) for size in ((3, COLS), (count,), (2,))],
        ),
        input_output_aliases={5 + count: 0},
        compiler_params=pltpu.CompilerParams(vmem_limit_bytes=56 << 20),
        cost_estimate=estimate(count),
        name="cells",
    )(flags, blocks, near_v, *fars, norms, rows, sums)
    return result[0], result[1:-1], result[-1]


def tie_kernel(*refs):
    pass


def tie(arrays, *tokens):
    return pl.pallas_call(
        tie_kernel,
        out_shape=[jax.ShapeDtypeStruct(array.shape, array.dtype) for array in arrays],
        in_specs=[pl.BlockSpec(memory_space=pltpu.HBM)] * (len(arrays) + len(tokens)),
        out_specs=[pl.BlockSpec(memory_space=pltpu.HBM)] * len(arrays),
        input_output_aliases={at: at for at in range(len(arrays))},
        name="tie",
    )(*arrays, *tokens)


def solve_kernel(gram_ref, smoothed_ref, out_ref):
    rows = lax.broadcasted_iota(jnp.int32, (EIGS, 2 * EIGS), 0)
    lanes = lax.broadcasted_iota(jnp.int32, (EIGS, 2 * EIGS), 1)
    eye = jnp.where(rows + EIGS == lanes, 1.0, 0.0)[:, EIGS:]
    work = jnp.concatenate([gram_ref[...], eye], axis=1)
    below = rows[0:8, :]
    tiles, done = [work[at : at + 8, :] for at in range(0, EIGS, 8)], []
    while tiles:
        for j in range(0, 8, 2):
            at = len(done) * 8 + j
            columns1 = [jnp.broadcast_to(tile[:, at : at + 1], tile.shape) for tile in tiles]
            columns2 = [jnp.broadcast_to(tile[:, at + 1 : at + 2], tile.shape) for tile in tiles]
            first, cross = columns1[0][j : j + 1, :], columns1[0][j + 1 : j + 2, :]
            second = columns2[0][j + 1 : j + 2, :]
            row1, row2 = tiles[0][j : j + 1, :], tiles[0][j + 1 : j + 2, :]
            scale = 1.0 / (first * second - cross * cross)
            scaled1 = (second * row1 - cross * row2) * scale
            scaled2 = (first * row2 - cross * row1) * scale
            ratio = cross / first
            columns1[0] = jnp.where(below > j + 1, columns1[0], 0.0)
            columns2[0] = jnp.where(below > j + 1, columns2[0], 0.0)
            tiles = [
                tile - (column1 * scaled1 + column2 * scaled2)
                for tile, column1, column2 in zip(tiles, columns1, columns2)
            ]
            tiles[0] = jnp.where(below == j, row1 * lax.rsqrt(first), tiles[0])
            last = (row2 - ratio * row1) * lax.rsqrt(second - ratio * cross)
            tiles[0] = jnp.where(below == j + 1, last, tiles[0])
        done.append(tiles.pop(0))
    inverse = jnp.concatenate(done, axis=0)[:, EIGS:]
    out_ref[...] = jnp.dot(
        inverse, smoothed_ref[...], precision=lax.Precision.HIGHEST, preferred_element_type=jnp.float32
    )


def solve(gram, smoothed):
    return pl.pallas_call(
        solve_kernel,
        out_shape=jax.ShapeDtypeStruct(smoothed.shape, jnp.float32),
        in_specs=[pl.BlockSpec(memory_space=pltpu.VMEM)] * 2,
        out_specs=pl.BlockSpec(memory_space=pltpu.VMEM),
        name="solve",
    )(gram, smoothed)


def per_device(embeddings, vectors, block_pairs):
    here_row = lax.axis_index("row")
    here_col = lax.axis_index("col")
    here_y, here_x = here_row // SIDE, here_row % SIDE
    blocks = embeddings.reshape(COLS, BLOCK, WIDTH)

    def move(array, dy, dx, keep=None):
        return lax.ppermute(array, "row", shift(dy, dx, keep))

    def turn(array, by):
        return lax.ppermute(array, "col", [(i, (i + by * CORES) % COLS) for i in range(COLS)])

    def swap(array):
        return lax.ppermute(array, "col", [(i, i ^ 1) for i in range(COLS)])

    far = {"own": make_payload(here_col[None], blocks, vectors)}
    far["a"] = move(far["own"], 0, 1)
    far["b"] = move(far["own"], 1, 0)
    far["c"] = move(far["own"], -1, -1)
    far_ids, works = [], []
    for (dy, dx), keep in STAGES.values():
        from_row = (here_y - dy) % SIDE * SIDE + (here_x - dx) % SIDE
        far_ids.append(from_row * COLS + here_col)
        works.append(jnp.broadcast_to(True if keep is None else keep(here_y, here_x), (COLS,)))
    far_ids = jnp.stack(far_ids)[:, None]
    near_ids = (here_row * COLS + jnp.arange(COLS, dtype=jnp.int32))[None, :]
    wanted = jnp.stack([near_ids * NBLOCKS + far_ids, far_ids * NBLOCKS + near_ids])
    listed = block_pairs[:, 0] * NBLOCKS + block_pairs[:, 1]
    found = jnp.any(wanted[..., None] == listed, axis=-1)
    both_ways = (jnp.arange(len(STAGES)) > 0)[:, None]
    flags = jnp.where(jnp.stack(works), found[0] + 2 * (found[1] & both_ways), 0).astype(jnp.int32)

    starts = {name: at for at, name in enumerate(STAGES)}

    def work(group, sums):
        at = starts[group[0]]
        return cells(
            flags[at : at + len(group)].reshape(-1),
            blocks,
            near_v,
            [far[name] for name in group],
            norms,
            rows,
            sums,
        )

    def give_back(group, parts):
        returned = []
        for name, part in zip(group, parts):
            back = [(to, source) for source, to in shift(*STAGES[name][0], STAGES[name][1])]
            returned.append(lax.ppermute(part, "row", back))
        return returned

    near_v = lax.all_gather(vectors, "col")
    sums, norms, rows, token = own_cells(flags[0], blocks, far["own"])

    far["a"], far["b"], far["c"] = tie([far["a"], far["b"], far["c"]], token, near_v)
    far["d"] = move(far["a"], -1, 0)
    far["e"] = move(far["c"], 0, -1)
    far["g"] = move(far["a"], 0, 1, left_half)
    far["h"] = move(far["b"], 1, 0, top_half)
    far["f"] = move(far["c"], -1, 0)
    group1, group2, group3 = ("a", "b", "c"), ("d", "e", "h"), ("f", "g", "k")
    sums, parts, token = work(group1, sums)

    far["e"], *parts = tie([far["e"], *parts], token, far["d"], far["h"], far["g"])
    returned1 = give_back(group1, parts)
    far["k"] = move(far["e"], -1, 0, top_half)
    sums, parts, token = work(group2, sums)

    far["f"], far["k"], *parts = tie([far["f"], far["k"], *parts], *returned1)
    returned2 = give_back(group2, parts)
    sums, parts, token = work(group3, sums)

    sums, *parts = tie([sums, *parts], *returned2)
    returned = returned1 + returned2 + give_back(group3, parts)

    layer, core = here_col // CORES, here_col % CORES
    halves = sums.reshape(SIDE, CORES, ACC, BLOCK)
    mine = lax.dynamic_index_in_dim(halves, core, 1, keepdims=False)
    kept = mine + swap(lax.dynamic_index_in_dim(halves, 1 - core, 1, keepdims=False))
    layers = [lax.dynamic_index_in_dim(kept, (layer - k) % SIDE, 0, keepdims=False) for k in range(SIDE)]
    summed = layers[0] + (turn(layers[1], 3) + turn(layers[2], 2) + turn(layers[3], 1))
    totals, degrees = summed[0:EIGS], summed[EIGS : EIGS + 1]
    for part in returned:
        part = part.astype(jnp.float32)
        totals, degrees = totals + part[0:EIGS], degrees + (part[EIGS : EIGS + 1] + part[ACC : ACC + 1])
    smoothed = totals / degrees
    gram = jnp.dot(
        smoothed, smoothed.T, precision=lax.Precision.HIGHEST, preferred_element_type=jnp.float32
    ) / (BLOCK * NBLOCKS)
    gram = gram + swap(gram)
    gram = gram + (turn(gram, 1) + turn(gram, 2) + turn(gram, 3))
    everyone = jnp.broadcast_to(gram, (SIDE * SIDE, EIGS, EIGS))
    gram = jnp.sum(lax.all_to_all(everyone, "row", 0, 0), axis=0)
    return solve(gram, smoothed)


def solution(mesh):
    return jax.shard_map(
        per_device,
        mesh=mesh,
        in_specs=(P("row", None), P(None, ("row", "col")), P()),
        out_specs=P(None, ("row", "col")),
        check_vma=False,
    )
```

```python
import functools
import math

import jax
import jax.numpy as jnp
from jax import lax
from jax.experimental import pallas as pl
from jax.experimental.pallas import tpu as pltpu
from jax.sharding import PartitionSpec as P

BLOCK = 512
WIDTH = 1024
EIGS = 64
NBLOCKS = 128
SIDE = 4
COLS = 8
CORES = 2
VROWS = BLOCK + EIGS // 2
PAYLOAD = VROWS + 16
ACC = EIGS + 8
SENT = EIGS + 16
SCALE = math.sqrt(math.log2(math.e) / math.sqrt(WIDTH))
COST = 8
NT = (((1,), (1,)), ((), ()))


def shift(dy, dx, keep=None):
    pairs = []
    for y in range(SIDE):
        for x in range(SIDE):
            to_y, to_x = (y + dy) % SIDE, (x + dx) % SIDE
            if keep is None or keep(to_y, to_x):
                pairs.append((y * SIDE + x, to_y * SIDE + to_x))
    return pairs


def left_half(y, x):
    return x < SIDE // 2


def top_half(y, x):
    return y < SIDE // 2


STAGES = {
    "own": ((0, 0), None),
    "a": ((0, 1), None),
    "b": ((1, 0), None),
    "c": ((-1, -1), None),
    "d": ((-1, 1), None),
    "e": ((-1, -2), None),
    "h": ((2, 0), top_half),
    "f": ((2, 1), None),
    "g": ((0, 2), left_half),
    "k": ((2, 2), top_half),
}


def row_norm(x):
    return lax.rsqrt(jnp.sum(x * x, axis=1, keepdims=True) * (1.0 / WIDTH) + 1e-06)


def payload_kernel(index_ref, x_ref, v_ref, out_ref):
    x = x_ref[0]
    out_ref[0:BLOCK, :] = x
    half = EIGS // 2
    out_ref[BLOCK:VROWS, 0:BLOCK] = v_ref[0:half, :]
    out_ref[BLOCK:VROWS, BLOCK : 2 * BLOCK] = v_ref[half:EIGS, :]
    norms = jnp.broadcast_to(row_norm(x.astype(jnp.float32)) * SCALE, (BLOCK, 128))
    rows = norms.T[0:16, :]
    high = rows.astype(jnp.bfloat16)
    low = (rows - high.astype(jnp.float32)).astype(jnp.bfloat16)
    out_ref[VROWS:PAYLOAD, 0:BLOCK] = high
    out_ref[VROWS:PAYLOAD, BLOCK : 2 * BLOCK] = low


def make_payload(here_col, blocks, vectors):
    return pl.pallas_call(
        payload_kernel,
        out_shape=jax.ShapeDtypeStruct((PAYLOAD, WIDTH), jnp.bfloat16),
        grid_spec=pltpu.PrefetchScalarGridSpec(
            num_scalar_prefetch=1,
            grid=(1,),
            in_specs=[
                pl.BlockSpec((1, BLOCK, WIDTH), lambda g, index: (index[0], 0, 0)),
                pl.BlockSpec((EIGS, BLOCK), lambda g, index: (0, 0)),
            ],
            out_specs=pl.BlockSpec((PAYLOAD, WIDTH), lambda g, index: (0, 0)),
        ),
        name="payload",
    )(here_col, blocks, vectors)


def side_vectors(side):
    half = EIGS // 2
    ones = jnp.ones((16, BLOCK), jnp.bfloat16)
    return jnp.concatenate([side[0:half, 0:BLOCK], side[0:half, BLOCK : 2 * BLOCK], ones], axis=0)


def side_norms(side):
    row = side[EIGS // 2 : EIGS // 2 + 1, :].astype(jnp.float32)
    return row[:, 0:BLOCK] + row[:, BLOCK : 2 * BLOCK]


def double(columns):
    return jnp.concatenate([columns, columns], axis=1)


def own_kernel(flags_ref, x_ref, far_ref, new_ref, norm_ref, row_ref, token_ref, p_ref):
    step = pl.program_id(0)
    new_ref[...] = jnp.zeros_like(new_ref)
    token_ref[...] = jnp.zeros_like(token_ref)
    norms = jnp.broadcast_to(row_norm(x_ref[0].astype(jnp.float32)) * SCALE, (BLOCK, 128))
    norm_ref[0] = norms
    row_ref[0] = norms.T[0:8, :]

    @pl.when(flags_ref[step] > 0)
    def _():
        side = far_ref[BLOCK:PAYLOAD, :]
        near, far = double(norm_ref[0]), side_norms(side)
        for at in range(0, BLOCK, 256):
            scores = lax.dot_general(
                x_ref[0], far_ref[at : at + 256, :], NT, preferred_element_type=jnp.float32
            )
            p_ref[:, at : at + 256] = jnp.exp2(scores * near * far[:, at : at + 256]).astype(jnp.bfloat16)
        part = lax.dot_general(side_vectors(side), p_ref[...], NT, preferred_element_type=jnp.float32)
        new_ref[0] = part[0:ACC, :]


def cells_kernel(count, flags_ref, x_hbm, v_hbm, *refs):
    far_hbms, (norm_hbm, row_hbm, old_hbm, new_hbm), refs = refs[:count], refs[count : count + 4], refs[count + 4 :]
    sent_refs, token_ref, refs = refs[:count], refs[count], refs[count + 1 :]
    x_ref, v_ref, far_ref, norm_ref, row_ref, old_ref, sums_ref, p_ref, column_ref, far_sums_ref = refs[:10]
    near_sem, far_sem, sem = refs[10:]

    def near_copies(near):
        pairs = ((x_hbm, x_ref), (norm_hbm, norm_ref), (v_hbm, v_ref))
        return [
            pltpu.make_async_copy(source.at[near], to.at[near], near_sem.at[at, near])
            for at, (source, to) in enumerate(pairs)
        ]

    far_copies = [pltpu.make_async_copy(far_hbms[at], far_ref.at[at], far_sem.at[at]) for at in range(count)]
    row_copy = pltpu.make_async_copy(row_hbm, row_ref, sem.at[0])
    old_copy = pltpu.make_async_copy(old_hbm, old_ref, sem.at[1])
    for copy in (far_copies[0], *near_copies(0), row_copy, *far_copies[1:], *near_copies(1), old_copy):
        copy.start()

    token_ref[...] = jnp.zeros_like(token_ref)
    far_sums_ref[...] = jnp.zeros_like(far_sums_ref)
    sums_ref[...] = jnp.zeros_like(sums_ref)

    def forward_only(at, near):
        rows, far = row_ref[near, 0:1, :], double(column_ref[at])
        for to in range(0, BLOCK, 256):
            scores = lax.dot_general(
                far_ref[at, 0:BLOCK, :], x_ref[near, to : to + 256, :], NT, preferred_element_type=jnp.float32
            )
            p_ref[:, to : to + 256] = jnp.exp2(scores * rows[:, to : to + 256] * far).astype(jnp.bfloat16)
        part = jnp.dot(side_vectors(far_ref[at, BLOCK:PAYLOAD, :]), p_ref[...], preferred_element_type=jnp.float32)
        sums_ref[near] += part[0:ACC, :]

    def backward(at, near, both):
        side = far_ref[at, BLOCK:PAYLOAD, :]
        columns, far = double(norm_ref[near]), side_norms(side)
        for to in range(0, BLOCK, 256):
            scores = lax.dot_general(
                x_ref[near], far_ref[at, to : to + 256, :], NT, preferred_element_type=jnp.float32
            )
            p_ref[:, to : to + 256] = jnp.exp2(scores * columns * far[:, to : to + 256]).astype(jnp.bfloat16)
        vectors = jnp.concatenate([v_ref[near], jnp.ones((16, BLOCK), jnp.bfloat16)], axis=0)
        part = jnp.dot(vectors, p_ref[...], preferred_element_type=jnp.float32)
        far_sums_ref[at] += part[0:ACC, :]
        if both:
            part = lax.dot_general(side_vectors(side), p_ref[...], NT, preferred_element_type=jnp.float32)
            sums_ref[near] += part[0:ACC, :]

    @pl.loop(0, COLS)
    def _(near):
        @pl.when(near + 2 < COLS)
        def _():
            for copy in near_copies(near + 2):
                copy.start()

        for copy in near_copies(near):
            copy.wait()
        for at in range(count):

            @pl.when(near == 0)
            def _():
                if at == 0:
                    row_copy.wait()
                far_copies[at].wait()
                column_ref[at] = jnp.broadcast_to(side_norms(far_ref[at, BLOCK:PAYLOAD, :]), (128, BLOCK)).T

            flag = flags_ref[at * COLS + near]
            pl.when(flag == 1)(functools.partial(forward_only, at, near))
            pl.when(flag == 2)(functools.partial(backward, at, near, False))
            pl.when(flag == 3)(functools.partial(backward, at, near, True))

    old_copy.wait()
    sums_ref[...] += old_ref[...]
    out_copy = pltpu.make_async_copy(sums_ref, new_hbm, sem.at[0])
    out_copy.start()
    for at in range(count):
        degrees = far_sums_ref[at, EIGS:ACC, :]
        high = degrees.astype(jnp.bfloat16).astype(jnp.float32)
        sent = jnp.concatenate([far_sums_ref[at, 0:EIGS, :], high, degrees - high], axis=0)
        sent_refs[at][...] = sent.astype(jnp.bfloat16)
    out_copy.wait()


SUMS = jax.ShapeDtypeStruct((COLS, ACC, BLOCK), jnp.float32)
NORM = jax.ShapeDtypeStruct((COLS, BLOCK, 128), jnp.float32)
ROW = jax.ShapeDtypeStruct((COLS, 8, BLOCK), jnp.float32)
TOKEN = jax.ShapeDtypeStruct((8, 128), jnp.float32)
SENT_SHAPE = jax.ShapeDtypeStruct((SENT, BLOCK), jnp.bfloat16)


def block_of(shape):
    return pl.BlockSpec((1, *shape[1:]), lambda g, flags: (g, 0, 0))


def whole(shape):
    return pl.BlockSpec(shape, lambda g, flags: (0, 0))


def own_cells(flags, blocks, far):
    return pl.pallas_call(
        own_kernel,
        out_shape=[SUMS, NORM, ROW, TOKEN],
        grid_spec=pltpu.PrefetchScalarGridSpec(
            num_scalar_prefetch=1,
            grid=(COLS,),
            in_specs=[block_of(blocks.shape), whole(far.shape)],
            out_specs=[block_of(SUMS.shape), block_of(NORM.shape), block_of(ROW.shape), whole(TOKEN.shape)],
            scratch_shapes=[pltpu.VMEM((BLOCK, BLOCK), jnp.bfloat16)],
        ),
        compiler_params=pltpu.CompilerParams(vmem_limit_bytes=56 << 20),
        cost_estimate=estimate(1),
        name="cells_own",
    )(flags, blocks, far)


def estimate(count):
    return pl.CostEstimate(
        flops=count * COST * BLOCK * BLOCK * WIDTH,
        bytes_accessed=(12 + count) << 20,
        transcendentals=count * 4 * BLOCK * BLOCK,
    )


def cells(flags, blocks, near_v, fars, norms, rows, sums):
    count = len(fars)
    buffers = [
        ((COLS, BLOCK, WIDTH), jnp.bfloat16),
        ((COLS, EIGS, BLOCK), jnp.bfloat16),
        ((count, PAYLOAD, WIDTH), jnp.bfloat16),
        ((COLS, BLOCK, 128), jnp.float32),
        ((COLS, 8, BLOCK), jnp.float32),
        ((COLS, ACC, BLOCK), jnp.float32),
        ((COLS, ACC, BLOCK), jnp.float32),
        ((BLOCK, BLOCK), jnp.bfloat16),
        ((count, BLOCK, 128), jnp.float32),
        ((count, ACC, BLOCK), jnp.float32),
    ]
    in_place = pl.BlockSpec(memory_space=pltpu.HBM)
    result = pl.pallas_call(
        functools.partial(cells_kernel, count),
        out_shape=[SUMS] + [SENT_SHAPE] * count + [TOKEN],
        grid_spec=pltpu.PrefetchScalarGridSpec(
            num_scalar_prefetch=1,
            grid=(1,),
            in_specs=[in_place] * (5 + count),
            out_specs=[in_place] + [whole(SENT_SHAPE.shape)] * count + [whole(TOKEN.shape)],
            scratch_shapes=[pltpu.VMEM(*buffer) for buffer in buffers]
            + [pltpu.SemaphoreType.DMA(size) for size in ((3, COLS), (count,), (2,))],
        ),
        input_output_aliases={5 + count: 0},
        compiler_params=pltpu.CompilerParams(vmem_limit_bytes=56 << 20),
        cost_estimate=estimate(count),
        name="cells",
    )(flags, blocks, near_v, *fars, norms, rows, sums)
    return result[0], result[1:-1], result[-1]


def tie_kernel(*refs):
    pass


def tie(arrays, *tokens):
    return pl.pallas_call(
        tie_kernel,
        out_shape=[jax.ShapeDtypeStruct(array.shape, array.dtype) for array in arrays],
        in_specs=[pl.BlockSpec(memory_space=pltpu.HBM)] * (len(arrays) + len(tokens)),
        out_specs=[pl.BlockSpec(memory_space=pltpu.HBM)] * len(arrays),
        input_output_aliases={at: at for at in range(len(arrays))},
        name="tie",
    )(*arrays, *tokens)


def solve_kernel(gram_ref, smoothed_ref, out_ref):
    rows = lax.broadcasted_iota(jnp.int32, (EIGS, 2 * EIGS), 0)
    lanes = lax.broadcasted_iota(jnp.int32, (EIGS, 2 * EIGS), 1)
    eye = jnp.where(rows + EIGS == lanes, 1.0, 0.0)[:, EIGS:]
    work = jnp.concatenate([gram_ref[...], eye], axis=1)
    below = rows[0:8, :]
    tiles, done = [work[at : at + 8, :] for at in range(0, EIGS, 8)], []
    while tiles:
        for j in range(0, 8, 2):
            at = len(done) * 8 + j
            columns1 = [jnp.broadcast_to(tile[:, at : at + 1], tile.shape) for tile in tiles]
            columns2 = [jnp.broadcast_to(tile[:, at + 1 : at + 2], tile.shape) for tile in tiles]
            first, cross = columns1[0][j : j + 1, :], columns1[0][j + 1 : j + 2, :]
            second = columns2[0][j + 1 : j + 2, :]
            row1, row2 = tiles[0][j : j + 1, :], tiles[0][j + 1 : j + 2, :]
            scale = 1.0 / (first * second - cross * cross)
            scaled1 = (second * row1 - cross * row2) * scale
            scaled2 = (first * row2 - cross * row1) * scale
            ratio = cross / first
            columns1[0] = jnp.where(below > j + 1, columns1[0], 0.0)
            columns2[0] = jnp.where(below > j + 1, columns2[0], 0.0)
            tiles = [
                tile - (column1 * scaled1 + column2 * scaled2)
                for tile, column1, column2 in zip(tiles, columns1, columns2)
            ]
            tiles[0] = jnp.where(below == j, row1 * lax.rsqrt(first), tiles[0])
            last = (row2 - ratio * row1) * lax.rsqrt(second - ratio * cross)
            tiles[0] = jnp.where(below == j + 1, last, tiles[0])
        done.append(tiles.pop(0))
    inverse = jnp.concatenate(done, axis=0)[:, EIGS:]
    out_ref[...] = jnp.dot(
        inverse, smoothed_ref[...], precision=lax.Precision.HIGHEST, preferred_element_type=jnp.float32
    )


def solve(gram, smoothed):
    return pl.pallas_call(
        solve_kernel,
        out_shape=jax.ShapeDtypeStruct(smoothed.shape, jnp.float32),
        in_specs=[pl.BlockSpec(memory_space=pltpu.VMEM)] * 2,
        out_specs=pl.BlockSpec(memory_space=pltpu.VMEM),
        name="solve",
    )(gram, smoothed)


def per_device(embeddings, vectors, block_pairs):
    here_row = lax.axis_index("row")
    here_col = lax.axis_index("col")
    here_y, here_x = here_row // SIDE, here_row % SIDE
    blocks = embeddings.reshape(COLS, BLOCK, WIDTH)

    def move(array, dy, dx, keep=None):
        return lax.ppermute(array, "row", shift(dy, dx, keep))

    def turn(array, by):
        return lax.ppermute(array, "col", [(i, (i + by * CORES) % COLS) for i in range(COLS)])

    def swap(array):
        return lax.ppermute(array, "col", [(i, i ^ 1) for i in range(COLS)])

    far = {"own": make_payload(here_col[None], blocks, vectors)}
    far["a"] = move(far["own"], 0, 1)
    far["b"] = move(far["own"], 1, 0)
    far["c"] = move(far["own"], -1, -1)
    far_ids, works = [], []
    for (dy, dx), keep in STAGES.values():
        from_row = (here_y - dy) % SIDE * SIDE + (here_x - dx) % SIDE
        far_ids.append(from_row * COLS + here_col)
        works.append(jnp.broadcast_to(True if keep is None else keep(here_y, here_x), (COLS,)))
    far_ids = jnp.stack(far_ids)[:, None]
    near_ids = (here_row * COLS + jnp.arange(COLS, dtype=jnp.int32))[None, :]
    wanted = jnp.stack([near_ids * NBLOCKS + far_ids, far_ids * NBLOCKS + near_ids])
    listed = block_pairs[:, 0] * NBLOCKS + block_pairs[:, 1]
    found = jnp.any(wanted[..., None] == listed, axis=-1)
    both_ways = (jnp.arange(len(STAGES)) > 0)[:, None]
    flags = jnp.where(jnp.stack(works), found[0] + 2 * (found[1] & both_ways), 0).astype(jnp.int32)

    starts = {name: at for at, name in enumerate(STAGES)}

    def work(group, sums):
        at = starts[group[0]]
        return cells(
            flags[at : at + len(group)].reshape(-1),
            blocks,
            near_v,
            [far[name] for name in group],
            norms,
            rows,
            sums,
        )

    def give_back(group, parts):
        returned = []
        for name, part in zip(group, parts):
            back = [(to, source) for source, to in shift(*STAGES[name][0], STAGES[name][1])]
            returned.append(lax.ppermute(part, "row", back))
        return returned

    near_v = lax.all_gather(vectors, "col")
    sums, norms, rows, token = own_cells(flags[0], blocks, far["own"])

    far["a"], far["b"], far["c"] = tie([far["a"], far["b"], far["c"]], token, near_v)
    far["d"] = move(far["a"], -1, 0)
    far["e"] = move(far["c"], 0, -1)
    far["g"] = move(far["a"], 0, 1, left_half)
    far["h"] = move(far["b"], 1, 0)
    group1, group2, group3 = ("a", "b", "c"), ("d", "e", "h"), ("f", "g", "k")
    sums, parts, token = work(group1, sums)

    far["h"], far["e"], *parts = tie([far["h"], far["e"], *parts], token, far["d"], far["g"])
    far["f"] = move(far["h"], 0, 1)
    far["k"] = move(far["e"], -1, 0, top_half)
    returned = give_back(("a",), parts[0:1])
    later = parts[1:]
    sums, parts, token = work(group2, sums)

    far["f"], far["k"], *parts = tie([far["f"], far["k"], *later, *parts], *returned)
    returned += give_back(("b", "c", *group2), parts)
    sums, parts, token = work(group3, sums)

    sums, *parts = tie([sums, *parts], *returned[1:])
    returned += give_back(group3, parts)

    layer, core = here_col // CORES, here_col % CORES
    halves = sums.reshape(SIDE, CORES, ACC, BLOCK)
    mine = lax.dynamic_index_in_dim(halves, core, 1, keepdims=False)
    kept = mine + swap(lax.dynamic_index_in_dim(halves, 1 - core, 1, keepdims=False))
    layers = [lax.dynamic_index_in_dim(kept, (layer - k) % SIDE, 0, keepdims=False) for k in range(SIDE)]
    summed = layers[0] + (turn(layers[1], 3) + turn(layers[2], 2) + turn(layers[3], 1))
    totals, degrees = summed[0:EIGS], summed[EIGS : EIGS + 1]
    for part in returned:
        part = part.astype(jnp.float32)
        totals, degrees = totals + part[0:EIGS], degrees + (part[EIGS : EIGS + 1] + part[ACC : ACC + 1])
    smoothed = totals / degrees
    gram = jnp.dot(
        smoothed, smoothed.T, precision=lax.Precision.HIGHEST, preferred_element_type=jnp.float32
    ) / (BLOCK * NBLOCKS)
    gram = gram + swap(gram)
    gram = gram + (turn(gram, 1) + turn(gram, 2) + turn(gram, 3))
    everyone = jnp.broadcast_to(gram, (SIDE * SIDE, EIGS, EIGS))
    gram = jnp.sum(lax.all_to_all(everyone, "row", 0, 0), axis=0)
    return solve(gram, smoothed)


def solution(mesh):
    return jax.shard_map(
        per_device,
        mesh=mesh,
        in_specs=(P("row", None), P(None, ("row", "col")), P()),
        out_specs=P(None, ("row", "col")),
        check_vma=False,
    )
```

```python
import functools
import math

import jax
import jax.numpy as jnp
from jax import lax
from jax.experimental import pallas as pl
from jax.experimental.pallas import tpu as pltpu
from jax.sharding import PartitionSpec as P

BLOCK = 512
WIDTH = 1024
EIGS = 64
NBLOCKS = 128
SIDE = 4
COLS = 8
CORES = 2
VROWS = BLOCK + EIGS // 2
PAYLOAD = VROWS + 16
ACC = EIGS + 8
SENT = EIGS + 16
SCALE = math.sqrt(math.log2(math.e) / math.sqrt(WIDTH))
COST = 8
NT = (((1,), (1,)), ((), ()))


def shift(dy, dx, keep=None):
    pairs = []
    for y in range(SIDE):
        for x in range(SIDE):
            to_y, to_x = (y + dy) % SIDE, (x + dx) % SIDE
            if keep is None or keep(to_y, to_x):
                pairs.append((y * SIDE + x, to_y * SIDE + to_x))
    return pairs


def left_half(y, x):
    return x < SIDE // 2


def top_half(y, x):
    return y < SIDE // 2


STAGES = {
    "own": ((0, 0), None),
    "a": ((0, 1), None),
    "b": ((1, 0), None),
    "c": ((-1, -1), None),
    "d": ((-1, 1), None),
    "e": ((-1, -2), None),
    "h": ((2, 0), top_half),
    "f": ((2, 1), None),
    "g": ((0, 2), left_half),
    "k": ((2, 2), top_half),
}


def row_norm(x):
    return lax.rsqrt(jnp.sum(x * x, axis=1, keepdims=True) * (1.0 / WIDTH) + 1e-06)


def payload_kernel(index_ref, x_ref, v_ref, out_ref):
    x = x_ref[0]
    out_ref[0:BLOCK, :] = x
    half = EIGS // 2
    out_ref[BLOCK:VROWS, 0:BLOCK] = v_ref[0:half, :]
    out_ref[BLOCK:VROWS, BLOCK : 2 * BLOCK] = v_ref[half:EIGS, :]
    norms = jnp.broadcast_to(row_norm(x.astype(jnp.float32)) * SCALE, (BLOCK, 128))
    rows = norms.T[0:16, :]
    high = rows.astype(jnp.bfloat16)
    low = (rows - high.astype(jnp.float32)).astype(jnp.bfloat16)
    out_ref[VROWS:PAYLOAD, 0:BLOCK] = high
    out_ref[VROWS:PAYLOAD, BLOCK : 2 * BLOCK] = low


def make_payload(here_col, blocks, vectors):
    return pl.pallas_call(
        payload_kernel,
        out_shape=jax.ShapeDtypeStruct((PAYLOAD, WIDTH), jnp.bfloat16),
        grid_spec=pltpu.PrefetchScalarGridSpec(
            num_scalar_prefetch=1,
            grid=(1,),
            in_specs=[
                pl.BlockSpec((1, BLOCK, WIDTH), lambda g, index: (index[0], 0, 0)),
                pl.BlockSpec((EIGS, BLOCK), lambda g, index: (0, 0)),
            ],
            out_specs=pl.BlockSpec((PAYLOAD, WIDTH), lambda g, index: (0, 0)),
        ),
        name="payload",
    )(here_col, blocks, vectors)


def side_vectors(side):
    half = EIGS // 2
    ones = jnp.ones((16, BLOCK), jnp.bfloat16)
    return jnp.concatenate([side[0:half, 0:BLOCK], side[0:half, BLOCK : 2 * BLOCK], ones], axis=0)


def side_norms(side):
    row = side[EIGS // 2 : EIGS // 2 + 1, :].astype(jnp.float32)
    return row[:, 0:BLOCK] + row[:, BLOCK : 2 * BLOCK]


def double(columns):
    return jnp.concatenate([columns, columns], axis=1)


def own_kernel(flags_ref, x_ref, far_ref, new_ref, norm_ref, row_ref, token_ref, p_ref):
    step = pl.program_id(0)
    new_ref[...] = jnp.zeros_like(new_ref)
    token_ref[...] = jnp.zeros_like(token_ref)
    norms = jnp.broadcast_to(row_norm(x_ref[0].astype(jnp.float32)) * SCALE, (BLOCK, 128))
    norm_ref[0] = norms
    row_ref[0] = norms.T[0:8, :]

    @pl.when(flags_ref[step] > 0)
    def _():
        side = far_ref[BLOCK:PAYLOAD, :]
        near, far = double(norm_ref[0]), side_norms(side)
        for at in range(0, BLOCK, 256):
            scores = lax.dot_general(
                x_ref[0], far_ref[at : at + 256, :], NT, preferred_element_type=jnp.float32
            )
            p_ref[:, at : at + 256] = jnp.exp2(scores * near * far[:, at : at + 256]).astype(jnp.bfloat16)
        part = lax.dot_general(side_vectors(side), p_ref[...], NT, preferred_element_type=jnp.float32)
        new_ref[0] = part[0:ACC, :]


def cells_kernel(count, flags_ref, x_hbm, v_hbm, *refs):
    far_hbms, (norm_hbm, row_hbm, old_hbm, new_hbm), refs = refs[:count], refs[count : count + 4], refs[count + 4 :]
    sent_refs, token_ref, refs = refs[:count], refs[count], refs[count + 1 :]
    x_ref, v_ref, far_ref, norm_ref, row_ref, old_ref, sums_ref, p_ref, column_ref, far_sums_ref = refs[:10]
    near_sem, far_sem, sem = refs[10:]

    def near_copies(near):
        pairs = ((x_hbm, x_ref), (norm_hbm, norm_ref), (v_hbm, v_ref))
        return [
            pltpu.make_async_copy(source.at[near], to.at[near], near_sem.at[at, near])
            for at, (source, to) in enumerate(pairs)
        ]

    far_copies = [pltpu.make_async_copy(far_hbms[at], far_ref.at[at], far_sem.at[at]) for at in range(count)]
    row_copy = pltpu.make_async_copy(row_hbm, row_ref, sem.at[0])
    old_copy = pltpu.make_async_copy(old_hbm, old_ref, sem.at[1])
    for copy in (far_copies[0], *near_copies(0), row_copy, *far_copies[1:], *near_copies(1), old_copy):
        copy.start()

    token_ref[...] = jnp.zeros_like(token_ref)
    far_sums_ref[...] = jnp.zeros_like(far_sums_ref)
    sums_ref[...] = jnp.zeros_like(sums_ref)

    def forward_only(at, near):
        rows, far = row_ref[near, 0:1, :], double(column_ref[at])
        for to in range(0, BLOCK, 256):
            scores = lax.dot_general(
                far_ref[at, 0:BLOCK, :], x_ref[near, to : to + 256, :], NT, preferred_element_type=jnp.float32
            )
            p_ref[:, to : to + 256] = jnp.exp2(scores * rows[:, to : to + 256] * far).astype(jnp.bfloat16)
        part = jnp.dot(side_vectors(far_ref[at, BLOCK:PAYLOAD, :]), p_ref[...], preferred_element_type=jnp.float32)
        sums_ref[near] += part[0:ACC, :]

    def backward(at, near, both):
        side = far_ref[at, BLOCK:PAYLOAD, :]
        columns, far = double(norm_ref[near]), side_norms(side)
        for to in range(0, BLOCK, 256):
            scores = lax.dot_general(
                x_ref[near], far_ref[at, to : to + 256, :], NT, preferred_element_type=jnp.float32
            )
            p_ref[:, to : to + 256] = jnp.exp2(scores * columns * far[:, to : to + 256]).astype(jnp.bfloat16)
        vectors = jnp.concatenate([v_ref[near].astype(jnp.bfloat16), jnp.ones((16, BLOCK), jnp.bfloat16)], axis=0)
        part = jnp.dot(vectors, p_ref[...], preferred_element_type=jnp.float32)
        far_sums_ref[at] += part[0:ACC, :]
        if both:
            part = lax.dot_general(side_vectors(side), p_ref[...], NT, preferred_element_type=jnp.float32)
            sums_ref[near] += part[0:ACC, :]

    @pl.loop(0, COLS)
    def _(near):
        @pl.when(near + 2 < COLS)
        def _():
            for copy in near_copies(near + 2):
                copy.start()

        for copy in near_copies(near):
            copy.wait()

        @pl.when(near == 0)
        def _():
            row_copy.wait()
            for at in range(count):
                far_copies[at].wait()
                column_ref[at] = jnp.broadcast_to(side_norms(far_ref[at, BLOCK:PAYLOAD, :]), (128, BLOCK)).T

        @pl.loop(0, count)
        def _(at):
            flag = flags_ref[at * COLS + near]
            pl.when(flag == 1)(functools.partial(forward_only, at, near))
            pl.when(flag == 2)(functools.partial(backward, at, near, False))
            pl.when(flag == 3)(functools.partial(backward, at, near, True))

    old_copy.wait()
    sums_ref[...] += old_ref[...]
    out_copy = pltpu.make_async_copy(sums_ref, new_hbm, sem.at[0])
    out_copy.start()
    for at in range(count):
        degrees = far_sums_ref[at, EIGS:ACC, :]
        high = degrees.astype(jnp.bfloat16).astype(jnp.float32)
        sent = jnp.concatenate([far_sums_ref[at, 0:EIGS, :], high, degrees - high], axis=0)
        sent_refs[at][...] = sent.astype(jnp.bfloat16)
    out_copy.wait()


SUMS = jax.ShapeDtypeStruct((COLS, ACC, BLOCK), jnp.float32)
NORM = jax.ShapeDtypeStruct((COLS, BLOCK, 128), jnp.float32)
ROW = jax.ShapeDtypeStruct((COLS, 8, BLOCK), jnp.float32)
TOKEN = jax.ShapeDtypeStruct((8, 128), jnp.float32)
SENT_SHAPE = jax.ShapeDtypeStruct((SENT, BLOCK), jnp.bfloat16)


def block_of(shape):
    return pl.BlockSpec((1, *shape[1:]), lambda g, flags: (g, 0, 0))


def whole(shape):
    return pl.BlockSpec(shape, lambda g, flags: (0, 0))


def own_cells(flags, blocks, far):
    return pl.pallas_call(
        own_kernel,
        out_shape=[SUMS, NORM, ROW, TOKEN],
        grid_spec=pltpu.PrefetchScalarGridSpec(
            num_scalar_prefetch=1,
            grid=(COLS,),
            in_specs=[block_of(blocks.shape), whole(far.shape)],
            out_specs=[block_of(SUMS.shape), block_of(NORM.shape), block_of(ROW.shape), whole(TOKEN.shape)],
            scratch_shapes=[pltpu.VMEM((BLOCK, BLOCK), jnp.bfloat16)],
        ),
        compiler_params=pltpu.CompilerParams(vmem_limit_bytes=56 << 20),
        cost_estimate=estimate(1),
        name="cells_own",
    )(flags, blocks, far)


def estimate(count):
    return pl.CostEstimate(
        flops=count * COST * BLOCK * BLOCK * WIDTH,
        bytes_accessed=(12 + count) << 20,
        transcendentals=count * 4 * BLOCK * BLOCK,
    )


def cells(flags, blocks, near_v, fars, norms, rows, sums):
    count = len(fars)
    buffers = [
        ((COLS, BLOCK, WIDTH), jnp.bfloat16),
        ((COLS, EIGS, BLOCK), jnp.float32),
        ((count, PAYLOAD, WIDTH), jnp.bfloat16),
        ((COLS, BLOCK, 128), jnp.float32),
        ((COLS, 8, BLOCK), jnp.float32),
        ((COLS, ACC, BLOCK), jnp.float32),
        ((COLS, ACC, BLOCK), jnp.float32),
        ((BLOCK, BLOCK), jnp.bfloat16),
        ((count, BLOCK, 128), jnp.float32),
        ((count, ACC, BLOCK), jnp.float32),
    ]
    in_place = pl.BlockSpec(memory_space=pltpu.HBM)
    result = pl.pallas_call(
        functools.partial(cells_kernel, count),
        out_shape=[SUMS] + [SENT_SHAPE] * count + [TOKEN],
        grid_spec=pltpu.PrefetchScalarGridSpec(
            num_scalar_prefetch=1,
            grid=(1,),
            in_specs=[in_place] * (5 + count),
            out_specs=[in_place] + [whole(SENT_SHAPE.shape)] * count + [whole(TOKEN.shape)],
            scratch_shapes=[pltpu.VMEM(*buffer) for buffer in buffers]
            + [pltpu.SemaphoreType.DMA(size) for size in ((3, COLS), (count,), (2,))],
        ),
        input_output_aliases={5 + count: 0},
        compiler_params=pltpu.CompilerParams(vmem_limit_bytes=56 << 20),
        cost_estimate=estimate(count),
        name="cells",
    )(flags, blocks, near_v, *fars, norms, rows, sums)
    return result[0], result[1:-1], result[-1]


def tie_kernel(*refs):
    pass


def tie(arrays, *tokens):
    return pl.pallas_call(
        tie_kernel,
        out_shape=[jax.ShapeDtypeStruct(array.shape, array.dtype) for array in arrays],
        in_specs=[pl.BlockSpec(memory_space=pltpu.HBM)] * (len(arrays) + len(tokens)),
        out_specs=[pl.BlockSpec(memory_space=pltpu.HBM)] * len(arrays),
        input_output_aliases={at: at for at in range(len(arrays))},
        name="tie",
    )(*arrays, *tokens)


def solve_kernel(gram_ref, smoothed_ref, out_ref):
    rows = lax.broadcasted_iota(jnp.int32, (EIGS, 2 * EIGS), 0)
    lanes = lax.broadcasted_iota(jnp.int32, (EIGS, 2 * EIGS), 1)
    eye = jnp.where(rows + EIGS == lanes, 1.0, 0.0)[:, EIGS:]
    work = jnp.concatenate([gram_ref[...], eye], axis=1)
    below = rows[0:8, :]
    tiles, done = [work[at : at + 8, :] for at in range(0, EIGS, 8)], []
    while tiles:
        for j in range(0, 8, 2):
            at = len(done) * 8 + j
            columns1 = [jnp.broadcast_to(tile[:, at : at + 1], tile.shape) for tile in tiles]
            columns2 = [jnp.broadcast_to(tile[:, at + 1 : at + 2], tile.shape) for tile in tiles]
            first, cross = columns1[0][j : j + 1, :], columns1[0][j + 1 : j + 2, :]
            second = columns2[0][j + 1 : j + 2, :]
            row1, row2 = tiles[0][j : j + 1, :], tiles[0][j + 1 : j + 2, :]
            scale = 1.0 / (first * second - cross * cross)
            scaled1 = (second * row1 - cross * row2) * scale
            scaled2 = (first * row2 - cross * row1) * scale
            ratio = cross / first
            columns1[0] = jnp.where(below > j + 1, columns1[0], 0.0)
            columns2[0] = jnp.where(below > j + 1, columns2[0], 0.0)
            tiles = [
                tile - (column1 * scaled1 + column2 * scaled2)
                for tile, column1, column2 in zip(tiles, columns1, columns2)
            ]
            tiles[0] = jnp.where(below == j, row1 * lax.rsqrt(first), tiles[0])
            last = (row2 - ratio * row1) * lax.rsqrt(second - ratio * cross)
            tiles[0] = jnp.where(below == j + 1, last, tiles[0])
        done.append(tiles.pop(0))
    inverse = jnp.concatenate(done, axis=0)[:, EIGS:]
    out_ref[...] = jnp.dot(
        inverse, smoothed_ref[...], precision=lax.Precision.HIGHEST, preferred_element_type=jnp.float32
    )


def solve(gram, smoothed):
    return pl.pallas_call(
        solve_kernel,
        out_shape=jax.ShapeDtypeStruct(smoothed.shape, jnp.float32),
        in_specs=[pl.BlockSpec(memory_space=pltpu.VMEM)] * 2,
        out_specs=pl.BlockSpec(memory_space=pltpu.VMEM),
        name="solve",
    )(gram, smoothed)


def per_device(embeddings, vectors, block_pairs):
    here_row = lax.axis_index("row")
    here_col = lax.axis_index("col")
    here_y, here_x = here_row // SIDE, here_row % SIDE
    blocks = embeddings.reshape(COLS, BLOCK, WIDTH)

    def move(array, dy, dx, keep=None):
        return lax.ppermute(array, "row", shift(dy, dx, keep))

    def turn(array, by):
        return lax.ppermute(array, "col", [(i, (i + by * CORES) % COLS) for i in range(COLS)])

    def swap(array):
        return lax.ppermute(array, "col", [(i, i ^ 1) for i in range(COLS)])

    far = {"own": make_payload(here_col[None], blocks, vectors)}
    far["a"] = move(far["own"], 0, 1)
    far["b"] = move(far["own"], 1, 0)
    far["c"] = move(far["own"], -1, -1)
    far_ids, works = [], []
    for (dy, dx), keep in STAGES.values():
        from_row = (here_y - dy) % SIDE * SIDE + (here_x - dx) % SIDE
        far_ids.append(from_row * COLS + here_col)
        works.append(jnp.broadcast_to(True if keep is None else keep(here_y, here_x), (COLS,)))
    far_ids = jnp.stack(far_ids)[:, None]
    near_ids = (here_row * COLS + jnp.arange(COLS, dtype=jnp.int32))[None, :]
    wanted = jnp.stack([near_ids * NBLOCKS + far_ids, far_ids * NBLOCKS + near_ids])
    listed = block_pairs[:, 0] * NBLOCKS + block_pairs[:, 1]
    found = jnp.any(wanted[..., None] == listed, axis=-1)
    both_ways = (jnp.arange(len(STAGES)) > 0)[:, None]
    flags = jnp.where(jnp.stack(works), found[0] + 2 * (found[1] & both_ways), 0).astype(jnp.int32)

    starts = {name: at for at, name in enumerate(STAGES)}

    def work(group, sums):
        at = starts[group[0]]
        return cells(
            flags[at : at + len(group)].reshape(-1),
            blocks,
            near_v,
            [far[name] for name in group],
            norms,
            rows,
            sums,
        )

    def give_back(group, parts):
        returned = []
        for name, part in zip(group, parts):
            back = [(to, source) for source, to in shift(*STAGES[name][0], STAGES[name][1])]
            returned.append(lax.ppermute(part, "row", back))
        return returned

    near_v = lax.all_gather(vectors.astype(jnp.float32), "col")
    sums, norms, rows, token = own_cells(flags[0], blocks, far["own"])

    far["a"], far["b"], far["c"] = tie([far["a"], far["b"], far["c"]], token)
    far["d"] = move(far["a"], -1, 0)
    far["e"] = move(far["c"], 0, -1)
    far["g"] = move(far["a"], 0, 1, left_half)
    far["h"] = move(far["b"], 1, 0)
    group1, group2, group3 = ("a", "b", "c"), ("d", "e", "h"), ("f", "g", "k")
    sums, parts, token = work(group1, sums)

    far["h"], far["e"], *parts = tie([far["h"], far["e"], *parts], token, far["d"], far["g"])
    far["f"] = move(far["h"], 0, 1)
    far["k"] = move(far["e"], -1, 0, top_half)
    returned = give_back(("a",), parts[0:1])
    later = parts[1:]
    sums, parts, token = work(group2, sums)

    far["f"], far["k"], *parts = tie([far["f"], far["k"], *later, *parts], *returned)
    returned += give_back(("b", "c", *group2), parts)
    sums, parts, token = work(group3, sums)

    sums, *parts = tie([sums, *parts], *returned[1:])
    returned += give_back(group3, parts)

    layer, core = here_col // CORES, here_col % CORES
    halves = sums.reshape(SIDE, CORES, ACC, BLOCK)
    mine = lax.dynamic_index_in_dim(halves, core, 1, keepdims=False)
    kept = mine + swap(lax.dynamic_index_in_dim(halves, 1 - core, 1, keepdims=False))
    layers = [lax.dynamic_index_in_dim(kept, (layer - k) % SIDE, 0, keepdims=False) for k in range(SIDE)]
    summed = layers[0] + (turn(layers[1], 3) + turn(layers[2], 2) + turn(layers[3], 1))
    totals, degrees = summed[0:EIGS], summed[EIGS : EIGS + 1]
    for part in returned:
        part = part.astype(jnp.float32)
        totals, degrees = totals + part[0:EIGS], degrees + (part[EIGS : EIGS + 1] + part[ACC : ACC + 1])
    smoothed = totals / degrees
    gram = jnp.dot(
        smoothed, smoothed.T, precision=lax.Precision.HIGHEST, preferred_element_type=jnp.float32
    ) / (BLOCK * NBLOCKS)
    gram = gram + swap(gram)
    gram = gram + (turn(gram, 1) + turn(gram, 2) + turn(gram, 3))
    everyone = jnp.broadcast_to(gram, (SIDE * SIDE, EIGS, EIGS))
    gram = jnp.sum(lax.all_to_all(everyone, "row", 0, 0), axis=0)
    return solve(gram, smoothed)


def solution(mesh):
    return jax.shard_map(
        per_device,
        mesh=mesh,
        in_specs=(P("row", None), P(None, ("row", "col")), P()),
        out_specs=P(None, ("row", "col")),
        check_vma=False,
    )
```

```python
import functools
import math

import jax
import jax.numpy as jnp
from jax import lax
from jax.experimental import pallas as pl
from jax.experimental.pallas import tpu as pltpu
from jax.sharding import PartitionSpec as P

BLOCK = 512
WIDTH = 1024
EIGS = 64
NBLOCKS = 128
SIDE = 4
COLS = 8
CORES = 2
VROWS = BLOCK + EIGS // 2
PAYLOAD = VROWS + 16
ACC = EIGS + 8
SENT = EIGS + 16
SCALE = math.sqrt(math.log2(math.e) / math.sqrt(WIDTH))
COST = 8
NT = (((1,), (1,)), ((), ()))


def shift(dy, dx, keep=None):
    pairs = []
    for y in range(SIDE):
        for x in range(SIDE):
            to_y, to_x = (y + dy) % SIDE, (x + dx) % SIDE
            if keep is None or keep(to_y, to_x):
                pairs.append((y * SIDE + x, to_y * SIDE + to_x))
    return pairs


def left_half(y, x):
    return x < SIDE // 2


def top_half(y, x):
    return y < SIDE // 2


STAGES = {
    "own": ((0, 0), None),
    "a": ((0, 1), None),
    "b": ((1, 0), None),
    "c": ((-1, -1), None),
    "d": ((-1, 1), None),
    "e": ((-1, -2), None),
    "h": ((2, 0), top_half),
    "f": ((2, 1), None),
    "g": ((0, 2), left_half),
    "k": ((2, 2), top_half),
}


def row_norm(x):
    return lax.rsqrt(jnp.sum(x * x, axis=1, keepdims=True) * (1.0 / WIDTH) + 1e-06)


def payload_kernel(index_ref, x_ref, v_ref, out_ref):
    x = x_ref[0]
    out_ref[0:BLOCK, :] = x
    half = EIGS // 2
    out_ref[BLOCK:VROWS, 0:BLOCK] = v_ref[0:half, :]
    out_ref[BLOCK:VROWS, BLOCK : 2 * BLOCK] = v_ref[half:EIGS, :]
    norms = jnp.broadcast_to(row_norm(x.astype(jnp.float32)) * SCALE, (BLOCK, 128))
    rows = norms.T[0:16, :]
    high = rows.astype(jnp.bfloat16)
    low = (rows - high.astype(jnp.float32)).astype(jnp.bfloat16)
    out_ref[VROWS:PAYLOAD, 0:BLOCK] = high
    out_ref[VROWS:PAYLOAD, BLOCK : 2 * BLOCK] = low


def make_payload(here_col, blocks, vectors):
    return pl.pallas_call(
        payload_kernel,
        out_shape=jax.ShapeDtypeStruct((PAYLOAD, WIDTH), jnp.bfloat16),
        grid_spec=pltpu.PrefetchScalarGridSpec(
            num_scalar_prefetch=1,
            grid=(1,),
            in_specs=[
                pl.BlockSpec((1, BLOCK, WIDTH), lambda g, index: (index[0], 0, 0)),
                pl.BlockSpec((EIGS, BLOCK), lambda g, index: (0, 0)),
            ],
            out_specs=pl.BlockSpec((PAYLOAD, WIDTH), lambda g, index: (0, 0)),
        ),
        name="payload",
    )(here_col, blocks, vectors)


def side_vectors(side):
    half = EIGS // 2
    ones = jnp.ones((16, BLOCK), jnp.bfloat16)
    return jnp.concatenate([side[0:half, 0:BLOCK], side[0:half, BLOCK : 2 * BLOCK], ones], axis=0)


def side_norms(side):
    row = side[EIGS // 2 : EIGS // 2 + 1, :].astype(jnp.float32)
    return row[:, 0:BLOCK] + row[:, BLOCK : 2 * BLOCK]


def double(columns):
    return jnp.concatenate([columns, columns], axis=1)


def own_kernel(flags_ref, x_ref, far_ref, new_ref, norm_ref, row_ref, token_ref, p_ref):
    step = pl.program_id(0)
    new_ref[...] = jnp.zeros_like(new_ref)
    token_ref[...] = jnp.zeros_like(token_ref)
    norms = jnp.broadcast_to(row_norm(x_ref[0].astype(jnp.float32)) * SCALE, (BLOCK, 128))
    norm_ref[0] = norms
    row_ref[0] = norms.T[0:8, :]

    @pl.when(flags_ref[step] > 0)
    def _():
        side = far_ref[BLOCK:PAYLOAD, :]
        near, far = double(norm_ref[0]), side_norms(side)
        for at in range(0, BLOCK, 256):
            scores = lax.dot_general(
                x_ref[0], far_ref[at : at + 256, :], NT, preferred_element_type=jnp.float32
            )
            p_ref[:, at : at + 256] = jnp.exp2(scores * near * far[:, at : at + 256]).astype(jnp.bfloat16)
        part = lax.dot_general(side_vectors(side), p_ref[...], NT, preferred_element_type=jnp.float32)
        new_ref[0] = part[0:ACC, :]


def cells_kernel(count, flags_ref, x_hbm, v_hbm, *refs):
    far_hbms, (norm_hbm, row_hbm, old_hbm, new_hbm), refs = refs[:count], refs[count : count + 4], refs[count + 4 :]
    sent_refs, token_ref, refs = refs[:count], refs[count], refs[count + 1 :]
    x_ref, v_ref, far_ref, norm_ref, row_ref, old_ref, sums_ref, p_ref, column_ref, far_sums_ref = refs[:10]
    near_sem, far_sem, sem = refs[10:]

    def near_copies(near):
        pairs = ((x_hbm, x_ref), (norm_hbm, norm_ref), (v_hbm, v_ref))
        return [
            pltpu.make_async_copy(source.at[near], to.at[near], near_sem.at[at, near])
            for at, (source, to) in enumerate(pairs)
        ]

    far_copies = [pltpu.make_async_copy(far_hbms[at], far_ref.at[at], far_sem.at[at]) for at in range(count)]
    row_copy = pltpu.make_async_copy(row_hbm, row_ref, sem.at[0])
    old_copy = pltpu.make_async_copy(old_hbm, old_ref, sem.at[1])
    for copy in (far_copies[0], *near_copies(0), row_copy, *far_copies[1:], *near_copies(1), old_copy):
        copy.start()

    token_ref[...] = jnp.zeros_like(token_ref)
    far_sums_ref[...] = jnp.zeros_like(far_sums_ref)
    sums_ref[...] = jnp.zeros_like(sums_ref)

    def forward_only(at, near):
        rows, far = row_ref[near, 0:1, :], double(column_ref[at])
        for to in range(0, BLOCK, 256):
            scores = lax.dot_general(
                far_ref[at, 0:BLOCK, :], x_ref[near, to : to + 256, :], NT, preferred_element_type=jnp.float32
            )
            p_ref[:, to : to + 256] = jnp.exp2(scores * rows[:, to : to + 256] * far).astype(jnp.bfloat16)
        part = jnp.dot(side_vectors(far_ref[at, BLOCK:PAYLOAD, :]), p_ref[...], preferred_element_type=jnp.float32)
        sums_ref[near] += part[0:ACC, :]

    def backward(at, near, both):
        side = far_ref[at, BLOCK:PAYLOAD, :]
        columns, far = double(norm_ref[near]), side_norms(side)
        for to in range(0, BLOCK, 256):
            scores = lax.dot_general(
                x_ref[near], far_ref[at, to : to + 256, :], NT, preferred_element_type=jnp.float32
            )
            p_ref[:, to : to + 256] = jnp.exp2(scores * columns * far[:, to : to + 256]).astype(jnp.bfloat16)
        vectors = jnp.concatenate([v_ref[near], jnp.ones((16, BLOCK), jnp.bfloat16)], axis=0)
        part = jnp.dot(vectors, p_ref[...], preferred_element_type=jnp.float32)
        far_sums_ref[at] += part[0:ACC, :]
        if both:
            part = lax.dot_general(side_vectors(side), p_ref[...], NT, preferred_element_type=jnp.float32)
            sums_ref[near] += part[0:ACC, :]

    @pl.loop(0, COLS)
    def _(near):
        @pl.when(near + 2 < COLS)
        def _():
            for copy in near_copies(near + 2):
                copy.start()

        for copy in near_copies(near):
            copy.wait()

        @pl.when(near == 0)
        def _():
            row_copy.wait()
            for at in range(count):
                far_copies[at].wait()
                column_ref[at] = jnp.broadcast_to(side_norms(far_ref[at, BLOCK:PAYLOAD, :]), (128, BLOCK)).T

        @pl.loop(0, count)
        def _(at):
            flag = flags_ref[at * COLS + near]
            pl.when(flag == 1)(functools.partial(forward_only, at, near))
            pl.when(flag == 2)(functools.partial(backward, at, near, False))
            pl.when(flag == 3)(functools.partial(backward, at, near, True))

    old_copy.wait()
    sums_ref[...] += old_ref[...]
    out_copy = pltpu.make_async_copy(sums_ref, new_hbm, sem.at[0])
    out_copy.start()
    for at in range(count):
        degrees = far_sums_ref[at, EIGS:ACC, :]
        high = degrees.astype(jnp.bfloat16).astype(jnp.float32)
        sent = jnp.concatenate([far_sums_ref[at, 0:EIGS, :], high, degrees - high], axis=0)
        sent_refs[at][...] = sent.astype(jnp.bfloat16)
    out_copy.wait()


SUMS = jax.ShapeDtypeStruct((COLS, ACC, BLOCK), jnp.float32)
NORM = jax.ShapeDtypeStruct((COLS, BLOCK, 128), jnp.float32)
ROW = jax.ShapeDtypeStruct((COLS, 8, BLOCK), jnp.float32)
TOKEN = jax.ShapeDtypeStruct((8, 128), jnp.float32)
SENT_SHAPE = jax.ShapeDtypeStruct((SENT, BLOCK), jnp.bfloat16)


def block_of(shape):
    return pl.BlockSpec((1, *shape[1:]), lambda g, flags: (g, 0, 0))


def whole(shape):
    return pl.BlockSpec(shape, lambda g, flags: (0, 0))


def own_cells(flags, blocks, far):
    return pl.pallas_call(
        own_kernel,
        out_shape=[SUMS, NORM, ROW, TOKEN],
        grid_spec=pltpu.PrefetchScalarGridSpec(
            num_scalar_prefetch=1,
            grid=(COLS,),
            in_specs=[block_of(blocks.shape), whole(far.shape)],
            out_specs=[block_of(SUMS.shape), block_of(NORM.shape), block_of(ROW.shape), whole(TOKEN.shape)],
            scratch_shapes=[pltpu.VMEM((BLOCK, BLOCK), jnp.bfloat16)],
        ),
        compiler_params=pltpu.CompilerParams(vmem_limit_bytes=56 << 20),
        cost_estimate=estimate(1),
        name="cells_own",
    )(flags, blocks, far)


def estimate(count):
    return pl.CostEstimate(
        flops=count * COST * BLOCK * BLOCK * WIDTH,
        bytes_accessed=(12 + count) << 20,
        transcendentals=count * 4 * BLOCK * BLOCK,
    )


def cells(flags, blocks, near_v, fars, norms, rows, sums):
    count = len(fars)
    buffers = [
        ((COLS, BLOCK, WIDTH), jnp.bfloat16),
        ((COLS, EIGS, BLOCK), jnp.bfloat16),
        ((count, PAYLOAD, WIDTH), jnp.bfloat16),
        ((COLS, BLOCK, 128), jnp.float32),
        ((COLS, 8, BLOCK), jnp.float32),
        ((COLS, ACC, BLOCK), jnp.float32),
        ((COLS, ACC, BLOCK), jnp.float32),
        ((BLOCK, BLOCK), jnp.bfloat16),
        ((count, BLOCK, 128), jnp.float32),
        ((count, ACC, BLOCK), jnp.float32),
    ]
    in_place = pl.BlockSpec(memory_space=pltpu.HBM)
    result = pl.pallas_call(
        functools.partial(cells_kernel, count),
        out_shape=[SUMS] + [SENT_SHAPE] * count + [TOKEN],
        grid_spec=pltpu.PrefetchScalarGridSpec(
            num_scalar_prefetch=1,
            grid=(1,),
            in_specs=[in_place] * (5 + count),
            out_specs=[in_place] + [whole(SENT_SHAPE.shape)] * count + [whole(TOKEN.shape)],
            scratch_shapes=[pltpu.VMEM(*buffer) for buffer in buffers]
            + [pltpu.SemaphoreType.DMA(size) for size in ((3, COLS), (count,), (2,))],
        ),
        input_output_aliases={5 + count: 0},
        compiler_params=pltpu.CompilerParams(vmem_limit_bytes=56 << 20),
        cost_estimate=estimate(count),
        name="cells",
    )(flags, blocks, near_v, *fars, norms, rows, sums)
    return result[0], result[1:-1], result[-1]


def tie_kernel(*refs):
    pass


def tie(arrays, *tokens):
    return pl.pallas_call(
        tie_kernel,
        out_shape=[jax.ShapeDtypeStruct(array.shape, array.dtype) for array in arrays],
        in_specs=[pl.BlockSpec(memory_space=pltpu.HBM)] * (len(arrays) + len(tokens)),
        out_specs=[pl.BlockSpec(memory_space=pltpu.HBM)] * len(arrays),
        input_output_aliases={at: at for at in range(len(arrays))},
        name="tie",
    )(*arrays, *tokens)


def solve_kernel(gram_ref, smoothed_ref, out_ref):
    rows = lax.broadcasted_iota(jnp.int32, (EIGS, 2 * EIGS), 0)
    lanes = lax.broadcasted_iota(jnp.int32, (EIGS, 2 * EIGS), 1)
    eye = jnp.where(rows + EIGS == lanes, 1.0, 0.0)[:, EIGS:]
    work = jnp.concatenate([gram_ref[...], eye], axis=1)
    below = rows[0:8, :]
    tiles, done = [work[at : at + 8, :] for at in range(0, EIGS, 8)], []
    while tiles:
        for j in range(0, 8, 2):
            at = len(done) * 8 + j
            columns1 = [jnp.broadcast_to(tile[:, at : at + 1], tile.shape) for tile in tiles]
            columns2 = [jnp.broadcast_to(tile[:, at + 1 : at + 2], tile.shape) for tile in tiles]
            first, cross = columns1[0][j : j + 1, :], columns1[0][j + 1 : j + 2, :]
            second = columns2[0][j + 1 : j + 2, :]
            row1, row2 = tiles[0][j : j + 1, :], tiles[0][j + 1 : j + 2, :]
            scale = 1.0 / (first * second - cross * cross)
            scaled1 = (second * row1 - cross * row2) * scale
            scaled2 = (first * row2 - cross * row1) * scale
            ratio = cross / first
            columns1[0] = jnp.where(below > j + 1, columns1[0], 0.0)
            columns2[0] = jnp.where(below > j + 1, columns2[0], 0.0)
            tiles = [
                tile - (column1 * scaled1 + column2 * scaled2)
                for tile, column1, column2 in zip(tiles, columns1, columns2)
            ]
            tiles[0] = jnp.where(below == j, row1 * lax.rsqrt(first), tiles[0])
            last = (row2 - ratio * row1) * lax.rsqrt(second - ratio * cross)
            tiles[0] = jnp.where(below == j + 1, last, tiles[0])
        done.append(tiles.pop(0))
    inverse = jnp.concatenate(done, axis=0)[:, EIGS:]
    out_ref[...] = jnp.dot(
        inverse, smoothed_ref[...], precision=lax.Precision.HIGHEST, preferred_element_type=jnp.float32
    )


def solve(gram, smoothed):
    return pl.pallas_call(
        solve_kernel,
        out_shape=jax.ShapeDtypeStruct(smoothed.shape, jnp.float32),
        in_specs=[pl.BlockSpec(memory_space=pltpu.VMEM)] * 2,
        out_specs=pl.BlockSpec(memory_space=pltpu.VMEM),
        name="solve",
    )(gram, smoothed)


def per_device(embeddings, vectors, block_pairs):
    here_row = lax.axis_index("row")
    here_col = lax.axis_index("col")
    here_y, here_x = here_row // SIDE, here_row % SIDE
    blocks = embeddings.reshape(COLS, BLOCK, WIDTH)

    def move(array, dy, dx, keep=None):
        return lax.ppermute(array, "row", shift(dy, dx, keep))

    def turn(array, by):
        return lax.ppermute(array, "col", [(i, (i + by * CORES) % COLS) for i in range(COLS)])

    def swap(array):
        return lax.ppermute(array, "col", [(i, i ^ 1) for i in range(COLS)])

    far = {"own": make_payload(here_col[None], blocks, vectors)}
    far["a"] = move(far["own"], 0, 1)
    far["b"] = move(far["own"], 1, 0)
    far["c"] = move(far["own"], -1, -1)
    far_ids, works = [], []
    for (dy, dx), keep in STAGES.values():
        from_row = (here_y - dy) % SIDE * SIDE + (here_x - dx) % SIDE
        far_ids.append(from_row * COLS + here_col)
        works.append(jnp.broadcast_to(True if keep is None else keep(here_y, here_x), (COLS,)))
    far_ids = jnp.stack(far_ids)[:, None]
    near_ids = (here_row * COLS + jnp.arange(COLS, dtype=jnp.int32))[None, :]
    wanted = jnp.stack([near_ids * NBLOCKS + far_ids, far_ids * NBLOCKS + near_ids])
    listed = block_pairs[:, 0] * NBLOCKS + block_pairs[:, 1]
    found = jnp.any(wanted[..., None] == listed, axis=-1)
    both_ways = (jnp.arange(len(STAGES)) > 0)[:, None]
    flags = jnp.where(jnp.stack(works), found[0] + 2 * (found[1] & both_ways), 0).astype(jnp.int32)

    starts = {name: at for at, name in enumerate(STAGES)}

    def work(group, sums):
        at = starts[group[0]]
        return cells(
            flags[at : at + len(group)].reshape(-1),
            blocks,
            near_v,
            [far[name] for name in group],
            norms,
            rows,
            sums,
        )

    def give_back(group, parts):
        returned = []
        for name, part in zip(group, parts):
            back = [(to, source) for source, to in shift(*STAGES[name][0], STAGES[name][1])]
            returned.append(lax.ppermute(part, "row", back))
        return returned

    near_v = lax.all_to_all(jnp.broadcast_to(vectors, (COLS, EIGS, BLOCK)), "col", 0, 0)
    sums, norms, rows, token = own_cells(flags[0], blocks, far["own"])

    far["a"], far["b"], far["c"] = tie([far["a"], far["b"], far["c"]], token, near_v)
    far["d"] = move(far["a"], -1, 0)
    far["e"] = move(far["c"], 0, -1)
    far["g"] = move(far["a"], 0, 1, left_half)
    far["h"] = move(far["b"], 1, 0)
    group1, group2, group3 = ("a", "b", "c"), ("d", "e", "h"), ("f", "g", "k")
    sums, parts, token = work(group1, sums)

    far["h"], far["e"], *parts = tie([far["h"], far["e"], *parts], token, far["d"], far["g"])
    far["f"] = move(far["h"], 0, 1)
    far["k"] = move(far["e"], -1, 0, top_half)
    returned = give_back(("a",), parts[0:1])
    later = parts[1:]
    sums, parts, token = work(group2, sums)

    far["f"], far["k"], *parts = tie([far["f"], far["k"], *later, *parts], *returned)
    returned += give_back(("b", "c", *group2), parts)
    sums, parts, token = work(group3, sums)

    sums, *parts = tie([sums, *parts], *returned[1:])
    returned += give_back(group3, parts)

    layer, core = here_col // CORES, here_col % CORES
    halves = sums.reshape(SIDE, CORES, ACC, BLOCK)
    mine = lax.dynamic_index_in_dim(halves, core, 1, keepdims=False)
    kept = mine + swap(lax.dynamic_index_in_dim(halves, 1 - core, 1, keepdims=False))
    layers = [lax.dynamic_index_in_dim(kept, (layer - k) % SIDE, 0, keepdims=False) for k in range(SIDE)]
    summed = layers[0] + (turn(layers[1], 3) + turn(layers[2], 2) + turn(layers[3], 1))
    totals, degrees = summed[0:EIGS], summed[EIGS : EIGS + 1]
    for part in returned:
        part = part.astype(jnp.float32)
        totals, degrees = totals + part[0:EIGS], degrees + (part[EIGS : EIGS + 1] + part[ACC : ACC + 1])
    smoothed = totals / degrees
    gram = jnp.dot(
        smoothed, smoothed.T, precision=lax.Precision.HIGHEST, preferred_element_type=jnp.float32
    ) / (BLOCK * NBLOCKS)
    gram = gram + swap(gram)
    gram = gram + (turn(gram, 1) + turn(gram, 2) + turn(gram, 3))
    everyone = jnp.broadcast_to(gram, (SIDE * SIDE, EIGS, EIGS))
    gram = jnp.sum(lax.all_to_all(everyone, "row", 0, 0), axis=0)
    return solve(gram, smoothed)


def solution(mesh):
    return jax.shard_map(
        per_device,
        mesh=mesh,
        in_specs=(P("row", None), P(None, ("row", "col")), P()),
        out_specs=P(None, ("row", "col")),
        check_vma=False,
    )
```

```python
import functools
import math

import jax
import jax.numpy as jnp
from jax import lax
from jax.experimental import pallas as pl
from jax.experimental.pallas import tpu as pltpu
from jax.sharding import PartitionSpec as P

BLOCK = 512
WIDTH = 1024
EIGS = 64
NBLOCKS = 128
SIDE = 4
COLS = 8
CORES = 2
VROWS = BLOCK + EIGS // 2
PAYLOAD = VROWS + 16
ACC = EIGS + 8
SENT = EIGS + 16
SCALE = math.sqrt(math.log2(math.e) / math.sqrt(WIDTH))
COST = 8
NT = (((1,), (1,)), ((), ()))


def shift(dy, dx, keep=None):
    pairs = []
    for y in range(SIDE):
        for x in range(SIDE):
            to_y, to_x = (y + dy) % SIDE, (x + dx) % SIDE
            if keep is None or keep(to_y, to_x):
                pairs.append((y * SIDE + x, to_y * SIDE + to_x))
    return pairs


def left_half(y, x):
    return x < SIDE // 2


def top_half(y, x):
    return y < SIDE // 2


STAGES = {
    "own": ((0, 0), None),
    "a": ((0, 1), None),
    "b": ((1, 0), None),
    "c": ((-1, -1), None),
    "d": ((-1, 1), None),
    "e": ((-1, -2), None),
    "h": ((2, 0), top_half),
    "f": ((2, 1), None),
    "g": ((0, 2), left_half),
    "k": ((2, 2), top_half),
}


def row_norm(x):
    return lax.rsqrt(jnp.sum(x * x, axis=1, keepdims=True) * (1.0 / WIDTH) + 1e-06)


def payload_kernel(index_ref, x_ref, v_ref, out_ref):
    x = x_ref[0]
    out_ref[0:BLOCK, :] = x
    half = EIGS // 2
    out_ref[BLOCK:VROWS, 0:BLOCK] = v_ref[0:half, :]
    out_ref[BLOCK:VROWS, BLOCK : 2 * BLOCK] = v_ref[half:EIGS, :]
    norms = jnp.broadcast_to(row_norm(x.astype(jnp.float32)) * SCALE, (BLOCK, 128))
    rows = norms.T[0:16, :]
    high = rows.astype(jnp.bfloat16)
    low = (rows - high.astype(jnp.float32)).astype(jnp.bfloat16)
    out_ref[VROWS:PAYLOAD, 0:BLOCK] = high
    out_ref[VROWS:PAYLOAD, BLOCK : 2 * BLOCK] = low


def make_payload(here_col, blocks, vectors):
    return pl.pallas_call(
        payload_kernel,
        out_shape=jax.ShapeDtypeStruct((PAYLOAD, WIDTH), jnp.bfloat16),
        grid_spec=pltpu.PrefetchScalarGridSpec(
            num_scalar_prefetch=1,
            grid=(1,),
            in_specs=[
                pl.BlockSpec((1, BLOCK, WIDTH), lambda g, index: (index[0], 0, 0)),
                pl.BlockSpec((EIGS, BLOCK), lambda g, index: (0, 0)),
            ],
            out_specs=pl.BlockSpec((PAYLOAD, WIDTH), lambda g, index: (0, 0)),
        ),
        name="payload",
    )(here_col, blocks, vectors)


def side_vectors(side):
    half = EIGS // 2
    ones = jnp.ones((16, BLOCK), jnp.bfloat16)
    return jnp.concatenate([side[0:half, 0:BLOCK], side[0:half, BLOCK : 2 * BLOCK], ones], axis=0)


def side_norms(side):
    row = side[EIGS // 2 : EIGS // 2 + 1, :].astype(jnp.float32)
    return row[:, 0:BLOCK] + row[:, BLOCK : 2 * BLOCK]


def double(columns):
    return jnp.concatenate([columns, columns], axis=1)


def own_kernel(flags_ref, x_ref, far_ref, new_ref, norm_ref, row_ref, token_ref, p_ref):
    step = pl.program_id(0)
    new_ref[...] = jnp.zeros_like(new_ref)
    token_ref[...] = jnp.zeros_like(token_ref)
    norms = jnp.broadcast_to(row_norm(x_ref[0].astype(jnp.float32)) * SCALE, (BLOCK, 128))
    norm_ref[0] = norms
    row_ref[0] = norms.T[0:8, :]

    @pl.when(flags_ref[step] > 0)
    def _():
        side = far_ref[BLOCK:PAYLOAD, :]
        near, far = double(norm_ref[0]), side_norms(side)
        for at in range(0, BLOCK, 256):
            scores = lax.dot_general(
                x_ref[0], far_ref[at : at + 256, :], NT, preferred_element_type=jnp.float32
            )
            p_ref[:, at : at + 256] = jnp.exp2(scores * near * far[:, at : at + 256]).astype(jnp.bfloat16)
        part = lax.dot_general(side_vectors(side), p_ref[...], NT, preferred_element_type=jnp.float32)
        new_ref[0] = part[0:ACC, :]


def cells_kernel(count, flags_ref, x_hbm, v_hbm, *refs):
    far_hbms, (norm_hbm, row_hbm, old_hbm, new_hbm), refs = refs[:count], refs[count : count + 4], refs[count + 4 :]
    sent_refs, token_ref, refs = refs[:count], refs[count], refs[count + 1 :]
    x_ref, v_ref, far_ref, norm_ref, row_ref, old_ref, sums_ref, p_ref, column_ref, far_sums_ref = refs[:10]
    near_sem, far_sem, sem = refs[10:]

    def near_copies(near):
        pairs = ((x_hbm, x_ref), (norm_hbm, norm_ref), (v_hbm, v_ref))
        return [
            pltpu.make_async_copy(source.at[near], to.at[near], near_sem.at[at, near])
            for at, (source, to) in enumerate(pairs)
        ]

    far_copies = [pltpu.make_async_copy(far_hbms[at], far_ref.at[at], far_sem.at[at]) for at in range(count)]
    row_copy = pltpu.make_async_copy(row_hbm, row_ref, sem.at[0])
    old_copy = pltpu.make_async_copy(old_hbm, old_ref, sem.at[1])
    for copy in (far_copies[0], *near_copies(0), row_copy, *far_copies[1:], *near_copies(1), old_copy):
        copy.start()

    token_ref[...] = jnp.zeros_like(token_ref)
    far_sums_ref[...] = jnp.zeros_like(far_sums_ref)
    sums_ref[...] = jnp.zeros_like(sums_ref)

    def forward_only(at, near):
        rows, far = row_ref[near, 0:1, :], double(column_ref[at])
        for to in range(0, BLOCK, 256):
            scores = lax.dot_general(
                far_ref[at, 0:BLOCK, :], x_ref[near, to : to + 256, :], NT, preferred_element_type=jnp.float32
            )
            p_ref[:, to : to + 256] = jnp.exp2(scores * rows[:, to : to + 256] * far).astype(jnp.bfloat16)
        part = jnp.dot(side_vectors(far_ref[at, BLOCK:PAYLOAD, :]), p_ref[...], preferred_element_type=jnp.float32)
        sums_ref[near] += part[0:ACC, :]

    def backward(at, near, both):
        side = far_ref[at, BLOCK:PAYLOAD, :]
        columns, far = double(norm_ref[near]), side_norms(side)
        for to in range(0, BLOCK, 256):
            scores = lax.dot_general(
                x_ref[near], far_ref[at, to : to + 256, :], NT, preferred_element_type=jnp.float32
            )
            p_ref[:, to : to + 256] = jnp.exp2(scores * columns * far[:, to : to + 256]).astype(jnp.bfloat16)
        vectors = jnp.concatenate([v_ref[near], jnp.ones((16, BLOCK), jnp.bfloat16)], axis=0)
        part = jnp.dot(vectors, p_ref[...], preferred_element_type=jnp.float32)
        far_sums_ref[at] += part[0:ACC, :]
        if both:
            part = lax.dot_general(side_vectors(side), p_ref[...], NT, preferred_element_type=jnp.float32)
            sums_ref[near] += part[0:ACC, :]

    @pl.loop(0, COLS)
    def _(near):
        @pl.when(near + 2 < COLS)
        def _():
            for copy in near_copies(near + 2):
                copy.start()

        for copy in near_copies(near):
            copy.wait()

        @pl.when(near == 0)
        def _():
            row_copy.wait()

        @pl.loop(0, count)
        def _(at):
            @pl.when(near == 0)
            def _():
                pltpu.make_async_copy(far_hbms[0], far_ref.at[at], far_sem.at[at]).wait()
                column_ref[at] = jnp.broadcast_to(side_norms(far_ref[at, BLOCK:PAYLOAD, :]), (128, BLOCK)).T

            flag = flags_ref[at * COLS + near]
            pl.when(flag == 1)(functools.partial(forward_only, at, near))
            pl.when(flag == 2)(functools.partial(backward, at, near, False))
            pl.when(flag == 3)(functools.partial(backward, at, near, True))

    old_copy.wait()
    sums_ref[...] += old_ref[...]
    out_copy = pltpu.make_async_copy(sums_ref, new_hbm, sem.at[0])
    out_copy.start()
    for at in range(count):
        degrees = far_sums_ref[at, EIGS:ACC, :]
        high = degrees.astype(jnp.bfloat16).astype(jnp.float32)
        sent = jnp.concatenate([far_sums_ref[at, 0:EIGS, :], high, degrees - high], axis=0)
        sent_refs[at][...] = sent.astype(jnp.bfloat16)
    out_copy.wait()


SUMS = jax.ShapeDtypeStruct((COLS, ACC, BLOCK), jnp.float32)
NORM = jax.ShapeDtypeStruct((COLS, BLOCK, 128), jnp.float32)
ROW = jax.ShapeDtypeStruct((COLS, 8, BLOCK), jnp.float32)
TOKEN = jax.ShapeDtypeStruct((8, 128), jnp.float32)
SENT_SHAPE = jax.ShapeDtypeStruct((SENT, BLOCK), jnp.bfloat16)


def block_of(shape):
    return pl.BlockSpec((1, *shape[1:]), lambda g, flags: (g, 0, 0))


def whole(shape):
    return pl.BlockSpec(shape, lambda g, flags: (0, 0))


def own_cells(flags, blocks, far):
    return pl.pallas_call(
        own_kernel,
        out_shape=[SUMS, NORM, ROW, TOKEN],
        grid_spec=pltpu.PrefetchScalarGridSpec(
            num_scalar_prefetch=1,
            grid=(COLS,),
            in_specs=[block_of(blocks.shape), whole(far.shape)],
            out_specs=[block_of(SUMS.shape), block_of(NORM.shape), block_of(ROW.shape), whole(TOKEN.shape)],
            scratch_shapes=[pltpu.VMEM((BLOCK, BLOCK), jnp.bfloat16)],
        ),
        compiler_params=pltpu.CompilerParams(vmem_limit_bytes=56 << 20),
        cost_estimate=estimate(1),
        name="cells_own",
    )(flags, blocks, far)


def estimate(count):
    return pl.CostEstimate(
        flops=count * COST * BLOCK * BLOCK * WIDTH,
        bytes_accessed=(12 + count) << 20,
        transcendentals=count * 4 * BLOCK * BLOCK,
    )


def cells(flags, blocks, near_v, fars, norms, rows, sums):
    count = len(fars)
    buffers = [
        ((COLS, BLOCK, WIDTH), jnp.bfloat16),
        ((COLS, EIGS, BLOCK), jnp.bfloat16),
        ((count, PAYLOAD, WIDTH), jnp.bfloat16),
        ((COLS, BLOCK, 128), jnp.float32),
        ((COLS, 8, BLOCK), jnp.float32),
        ((COLS, ACC, BLOCK), jnp.float32),
        ((COLS, ACC, BLOCK), jnp.float32),
        ((BLOCK, BLOCK), jnp.bfloat16),
        ((count, BLOCK, 128), jnp.float32),
        ((count, ACC, BLOCK), jnp.float32),
    ]
    in_place = pl.BlockSpec(memory_space=pltpu.HBM)
    result = pl.pallas_call(
        functools.partial(cells_kernel, count),
        out_shape=[SUMS] + [SENT_SHAPE] * count + [TOKEN],
        grid_spec=pltpu.PrefetchScalarGridSpec(
            num_scalar_prefetch=1,
            grid=(1,),
            in_specs=[in_place] * (5 + count),
            out_specs=[in_place] + [whole(SENT_SHAPE.shape)] * count + [whole(TOKEN.shape)],
            scratch_shapes=[pltpu.VMEM(*buffer) for buffer in buffers]
            + [pltpu.SemaphoreType.DMA(size) for size in ((3, COLS), (count,), (2,))],
        ),
        input_output_aliases={5 + count: 0},
        compiler_params=pltpu.CompilerParams(vmem_limit_bytes=56 << 20),
        cost_estimate=estimate(count),
        name="cells",
    )(flags, blocks, near_v, *fars, norms, rows, sums)
    return result[0], result[1:-1], result[-1]


def tie_kernel(*refs):
    pass


def tie(arrays, *tokens):
    return pl.pallas_call(
        tie_kernel,
        out_shape=[jax.ShapeDtypeStruct(array.shape, array.dtype) for array in arrays],
        in_specs=[pl.BlockSpec(memory_space=pltpu.HBM)] * (len(arrays) + len(tokens)),
        out_specs=[pl.BlockSpec(memory_space=pltpu.HBM)] * len(arrays),
        input_output_aliases={at: at for at in range(len(arrays))},
        name="tie",
    )(*arrays, *tokens)


def solve_kernel(gram_ref, smoothed_ref, out_ref):
    rows = lax.broadcasted_iota(jnp.int32, (EIGS, 2 * EIGS), 0)
    lanes = lax.broadcasted_iota(jnp.int32, (EIGS, 2 * EIGS), 1)
    eye = jnp.where(rows + EIGS == lanes, 1.0, 0.0)[:, EIGS:]
    work = jnp.concatenate([gram_ref[...], eye], axis=1)
    below = rows[0:8, :]
    tiles, done = [work[at : at + 8, :] for at in range(0, EIGS, 8)], []
    while tiles:
        for j in range(0, 8, 2):
            at = len(done) * 8 + j
            columns1 = [jnp.broadcast_to(tile[:, at : at + 1], tile.shape) for tile in tiles]
            columns2 = [jnp.broadcast_to(tile[:, at + 1 : at + 2], tile.shape) for tile in tiles]
            first, cross = columns1[0][j : j + 1, :], columns1[0][j + 1 : j + 2, :]
            second = columns2[0][j + 1 : j + 2, :]
            row1, row2 = tiles[0][j : j + 1, :], tiles[0][j + 1 : j + 2, :]
            scale = 1.0 / (first * second - cross * cross)
            scaled1 = (second * row1 - cross * row2) * scale
            scaled2 = (first * row2 - cross * row1) * scale
            ratio = cross / first
            columns1[0] = jnp.where(below > j + 1, columns1[0], 0.0)
            columns2[0] = jnp.where(below > j + 1, columns2[0], 0.0)
            tiles = [
                tile - (column1 * scaled1 + column2 * scaled2)
                for tile, column1, column2 in zip(tiles, columns1, columns2)
            ]
            tiles[0] = jnp.where(below == j, row1 * lax.rsqrt(first), tiles[0])
            last = (row2 - ratio * row1) * lax.rsqrt(second - ratio * cross)
            tiles[0] = jnp.where(below == j + 1, last, tiles[0])
        done.append(tiles.pop(0))
    inverse = jnp.concatenate(done, axis=0)[:, EIGS:]
    out_ref[...] = jnp.dot(
        inverse, smoothed_ref[...], precision=lax.Precision.HIGHEST, preferred_element_type=jnp.float32
    )


def solve(gram, smoothed):
    return pl.pallas_call(
        solve_kernel,
        out_shape=jax.ShapeDtypeStruct(smoothed.shape, jnp.float32),
        in_specs=[pl.BlockSpec(memory_space=pltpu.VMEM)] * 2,
        out_specs=pl.BlockSpec(memory_space=pltpu.VMEM),
        name="solve",
    )(gram, smoothed)


def per_device(embeddings, vectors, block_pairs):
    here_row = lax.axis_index("row")
    here_col = lax.axis_index("col")
    here_y, here_x = here_row // SIDE, here_row % SIDE
    blocks = embeddings.reshape(COLS, BLOCK, WIDTH)

    def move(array, dy, dx, keep=None):
        return lax.ppermute(array, "row", shift(dy, dx, keep))

    def turn(array, by):
        return lax.ppermute(array, "col", [(i, (i + by * CORES) % COLS) for i in range(COLS)])

    def swap(array):
        return lax.ppermute(array, "col", [(i, i ^ 1) for i in range(COLS)])

    far = {"own": make_payload(here_col[None], blocks, vectors)}
    far["a"] = move(far["own"], 0, 1)
    far["b"] = move(far["own"], 1, 0)
    far["c"] = move(far["own"], -1, -1)
    far_ids, works = [], []
    for (dy, dx), keep in STAGES.values():
        from_row = (here_y - dy) % SIDE * SIDE + (here_x - dx) % SIDE
        far_ids.append(from_row * COLS + here_col)
        works.append(jnp.broadcast_to(True if keep is None else keep(here_y, here_x), (COLS,)))
    far_ids = jnp.stack(far_ids)[:, None]
    near_ids = (here_row * COLS + jnp.arange(COLS, dtype=jnp.int32))[None, :]
    wanted = jnp.stack([near_ids * NBLOCKS + far_ids, far_ids * NBLOCKS + near_ids])
    listed = block_pairs[:, 0] * NBLOCKS + block_pairs[:, 1]
    found = jnp.any(wanted[..., None] == listed, axis=-1)
    both_ways = (jnp.arange(len(STAGES)) > 0)[:, None]
    flags = jnp.where(jnp.stack(works), found[0] + 2 * (found[1] & both_ways), 0).astype(jnp.int32)

    starts = {name: at for at, name in enumerate(STAGES)}

    def work(group, sums):
        at = starts[group[0]]
        return cells(
            flags[at : at + len(group)].reshape(-1),
            blocks,
            near_v,
            [far[name] for name in group],
            norms,
            rows,
            sums,
        )

    def give_back(group, parts):
        returned = []
        for name, part in zip(group, parts):
            back = [(to, source) for source, to in shift(*STAGES[name][0], STAGES[name][1])]
            returned.append(lax.ppermute(part, "row", back))
        return returned

    near_v = lax.all_to_all(jnp.broadcast_to(vectors, (COLS, EIGS, BLOCK)), "col", 0, 0)
    sums, norms, rows, token = own_cells(flags[0], blocks, far["own"])

    far["a"], far["b"], far["c"] = tie([far["a"], far["b"], far["c"]], token, near_v)
    far["h"] = move(far["b"], 1, 0)
    far["e"] = move(far["c"], 0, -1)
    far["d"] = move(far["a"], -1, 0)
    far["g"] = move(far["a"], 0, 1, left_half)
    group1, group2, group3 = ("a", "b", "c"), ("d", "e", "h"), ("f", "g", "k")
    sums, parts, token = work(group1, sums)

    far["h"], far["e"], *parts = tie([far["h"], far["e"], *parts], token, far["d"], far["g"])
    far["f"] = move(far["h"], 0, 1)
    far["k"] = move(far["e"], -1, 0, top_half)
    returned = give_back(("a",), parts[0:1])
    later = parts[1:]
    sums, parts, token = work(group2, sums)

    far["f"], far["k"], *parts = tie([far["f"], far["k"], *later, *parts], *returned)
    returned += give_back(("b", "c", *group2), parts)
    sums, parts, token = work(group3, sums)

    sums, *parts = tie([sums, *parts], *returned[1:])
    returned += give_back(group3, parts)

    layer, core = here_col // CORES, here_col % CORES
    halves = sums.reshape(SIDE, CORES, ACC, BLOCK)
    mine = lax.dynamic_index_in_dim(halves, core, 1, keepdims=False)
    kept = mine + swap(lax.dynamic_index_in_dim(halves, 1 - core, 1, keepdims=False))
    layers = [lax.dynamic_index_in_dim(kept, (layer - k) % SIDE, 0, keepdims=False) for k in range(SIDE)]
    summed = layers[0] + (turn(layers[1], 3) + turn(layers[2], 2) + turn(layers[3], 1))
    totals, degrees = summed[0:EIGS], summed[EIGS : EIGS + 1]
    for part in returned:
        part = part.astype(jnp.float32)
        totals, degrees = totals + part[0:EIGS], degrees + (part[EIGS : EIGS + 1] + part[ACC : ACC + 1])
    smoothed = totals / degrees
    gram = jnp.dot(
        smoothed, smoothed.T, precision=lax.Precision.HIGHEST, preferred_element_type=jnp.float32
    ) / (BLOCK * NBLOCKS)
    gram = gram + swap(gram)
    gram = gram + (turn(gram, 1) + turn(gram, 2) + turn(gram, 3))
    everyone = jnp.broadcast_to(gram, (SIDE * SIDE, EIGS, EIGS))
    gram = jnp.sum(lax.all_to_all(everyone, "row", 0, 0), axis=0)
    return solve(gram, smoothed)


def solution(mesh):
    return jax.shard_map(
        per_device,
        mesh=mesh,
        in_specs=(P("row", None), P(None, ("row", "col")), P()),
        out_specs=P(None, ("row", "col")),
        check_vma=False,
    )
```

```python
import functools
import math

import jax
import jax.numpy as jnp
from jax import lax
from jax.experimental import pallas as pl
from jax.experimental.pallas import tpu as pltpu
from jax.sharding import PartitionSpec as P

BLOCK = 512
WIDTH = 1024
EIGS = 64
NBLOCKS = 128
SIDE = 4
COLS = 8
CORES = 2
VROWS = BLOCK + EIGS // 2
PAYLOAD = VROWS + 16
ACC = EIGS + 8
SENT = EIGS + 16
SCALE = math.sqrt(math.log2(math.e) / math.sqrt(WIDTH))
COST = 8
NT = (((1,), (1,)), ((), ()))


def shift(dy, dx, keep=None):
    pairs = []
    for y in range(SIDE):
        for x in range(SIDE):
            to_y, to_x = (y + dy) % SIDE, (x + dx) % SIDE
            if keep is None or keep(to_y, to_x):
                pairs.append((y * SIDE + x, to_y * SIDE + to_x))
    return pairs


def left_half(y, x):
    return x < SIDE // 2


def top_half(y, x):
    return y < SIDE // 2


STAGES = {
    "own": ((0, 0), None),
    "a": ((0, 1), None),
    "b": ((1, 0), None),
    "c": ((-1, -1), None),
    "d": ((-1, 1), None),
    "e": ((-1, -2), None),
    "h": ((2, 0), top_half),
    "f": ((2, 1), None),
    "g": ((0, 2), left_half),
    "k": ((2, 2), top_half),
}


def row_norm(x):
    return lax.rsqrt(jnp.sum(x * x, axis=1, keepdims=True) * (1.0 / WIDTH) + 1e-06)


def payload_kernel(index_ref, x_ref, v_ref, out_ref):
    x = x_ref[0]
    out_ref[0:BLOCK, :] = x
    half = EIGS // 2
    out_ref[BLOCK:VROWS, 0:BLOCK] = v_ref[0:half, :]
    out_ref[BLOCK:VROWS, BLOCK : 2 * BLOCK] = v_ref[half:EIGS, :]
    norms = jnp.broadcast_to(row_norm(x.astype(jnp.float32)) * SCALE, (BLOCK, 128))
    rows = norms.T[0:16, :]
    high = rows.astype(jnp.bfloat16)
    low = (rows - high.astype(jnp.float32)).astype(jnp.bfloat16)
    out_ref[VROWS:PAYLOAD, 0:BLOCK] = high
    out_ref[VROWS:PAYLOAD, BLOCK : 2 * BLOCK] = low


def make_payload(here_col, blocks, vectors):
    return pl.pallas_call(
        payload_kernel,
        out_shape=jax.ShapeDtypeStruct((PAYLOAD, WIDTH), jnp.bfloat16),
        grid_spec=pltpu.PrefetchScalarGridSpec(
            num_scalar_prefetch=1,
            grid=(1,),
            in_specs=[
                pl.BlockSpec((1, BLOCK, WIDTH), lambda g, index: (index[0], 0, 0)),
                pl.BlockSpec((EIGS, BLOCK), lambda g, index: (0, 0)),
            ],
            out_specs=pl.BlockSpec((PAYLOAD, WIDTH), lambda g, index: (0, 0)),
        ),
        name="payload",
    )(here_col, blocks, vectors)


def side_vectors(side):
    half = EIGS // 2
    ones = jnp.ones((16, BLOCK), jnp.bfloat16)
    return jnp.concatenate([side[0:half, 0:BLOCK], side[0:half, BLOCK : 2 * BLOCK], ones], axis=0)


def side_norms(side):
    row = side[EIGS // 2 : EIGS // 2 + 1, :].astype(jnp.float32)
    return row[:, 0:BLOCK] + row[:, BLOCK : 2 * BLOCK]


def double(columns):
    return jnp.concatenate([columns, columns], axis=1)


def own_kernel(flags_ref, x_ref, far_ref, new_ref, norm_ref, row_ref, token_ref, p_ref):
    step = pl.program_id(0)
    new_ref[...] = jnp.zeros_like(new_ref)
    token_ref[...] = jnp.zeros_like(token_ref)
    norms = jnp.broadcast_to(row_norm(x_ref[0].astype(jnp.float32)) * SCALE, (BLOCK, 128))
    norm_ref[0] = norms
    row_ref[0] = norms.T[0:8, :]

    @pl.when(flags_ref[step] > 0)
    def _():
        side = far_ref[BLOCK:PAYLOAD, :]
        near, far = double(norm_ref[0]), side_norms(side)
        for at in range(0, BLOCK, 256):
            scores = lax.dot_general(
                x_ref[0], far_ref[at : at + 256, :], NT, preferred_element_type=jnp.float32
            )
            p_ref[:, at : at + 256] = jnp.exp2(scores * near * far[:, at : at + 256]).astype(jnp.bfloat16)
        part = lax.dot_general(side_vectors(side), p_ref[...], NT, preferred_element_type=jnp.float32)
        new_ref[0] = part[0:ACC, :]


def cells_kernel(count, flags_ref, x_hbm, v_hbm, *refs):
    far_hbms, (norm_hbm, row_hbm, old_hbm, new_hbm), refs = refs[:count], refs[count : count + 4], refs[count + 4 :]
    sent_refs, token_ref, refs = refs[:count], refs[count], refs[count + 1 :]
    x_ref, v_ref, far_ref, norm_ref, row_ref, old_ref, sums_ref, p_ref, column_ref, far_sums_ref = refs[:10]
    near_sem, far_sem, sem = refs[10:]

    def near_copies(near):
        pairs = ((x_hbm, x_ref), (norm_hbm, norm_ref), (v_hbm, v_ref))
        return [
            pltpu.make_async_copy(source.at[near], to.at[near], near_sem.at[at, near])
            for at, (source, to) in enumerate(pairs)
        ]

    far_copies = [pltpu.make_async_copy(far_hbms[at], far_ref.at[at], far_sem.at[at]) for at in range(count)]
    row_copy = pltpu.make_async_copy(row_hbm, row_ref, sem.at[0])
    old_copy = pltpu.make_async_copy(old_hbm, old_ref, sem.at[1])
    for copy in (far_copies[0], *near_copies(0), row_copy, *far_copies[1:], *near_copies(1), old_copy):
        copy.start()

    token_ref[...] = jnp.zeros_like(token_ref)
    far_sums_ref[...] = jnp.zeros_like(far_sums_ref)
    sums_ref[...] = jnp.zeros_like(sums_ref)

    def forward_only(at, near):
        rows, far = row_ref[near, 0:1, :], double(column_ref[at])
        for to in range(0, BLOCK, 256):
            scores = lax.dot_general(
                far_ref[at, 0:BLOCK, :], x_ref[near, to : to + 256, :], NT, preferred_element_type=jnp.float32
            )
            p_ref[:, to : to + 256] = jnp.exp2(scores * rows[:, to : to + 256] * far).astype(jnp.bfloat16)
        part = jnp.dot(side_vectors(far_ref[at, BLOCK:PAYLOAD, :]), p_ref[...], preferred_element_type=jnp.float32)
        sums_ref[near] += part[0:ACC, :]

    def backward(at, near, both):
        side = far_ref[at, BLOCK:PAYLOAD, :]
        columns, far = double(norm_ref[near]), side_norms(side)
        for to in range(0, BLOCK, 256):
            scores = lax.dot_general(
                x_ref[near], far_ref[at, to : to + 256, :], NT, preferred_element_type=jnp.float32
            )
            p_ref[:, to : to + 256] = jnp.exp2(scores * columns * far[:, to : to + 256]).astype(jnp.bfloat16)
        vectors = jnp.concatenate([v_ref[near], jnp.ones((16, BLOCK), jnp.bfloat16)], axis=0)
        part = jnp.dot(vectors, p_ref[...], preferred_element_type=jnp.float32)
        far_sums_ref[at] += part[0:ACC, :]
        if both:
            part = lax.dot_general(side_vectors(side), p_ref[...], NT, preferred_element_type=jnp.float32)
            sums_ref[near] += part[0:ACC, :]

    @pl.loop(0, COLS)
    def _(near):
        @pl.when(near + 2 < COLS)
        def _():
            for copy in near_copies(near + 2):
                copy.start()

        for copy in near_copies(near):
            copy.wait()

        @pl.when(near == 0)
        def _():
            row_copy.wait()

        @pl.loop(0, count)
        def _(at):
            @pl.when(near == 0)
            def _():
                pltpu.make_async_copy(far_hbms[0], far_ref.at[at], far_sem.at[at]).wait()
                column_ref[at] = jnp.broadcast_to(side_norms(far_ref[at, BLOCK:PAYLOAD, :]), (128, BLOCK)).T

            flag = flags_ref[at * COLS + near]
            pl.when(flag == 1)(functools.partial(forward_only, at, near))
            pl.when(flag == 2)(functools.partial(backward, at, near, False))
            pl.when(flag == 3)(functools.partial(backward, at, near, True))

    old_copy.wait()
    sums_ref[...] += old_ref[...]
    out_copy = pltpu.make_async_copy(sums_ref, new_hbm, sem.at[0])
    out_copy.start()
    for at in range(count):
        degrees = far_sums_ref[at, EIGS:ACC, :]
        high = degrees.astype(jnp.bfloat16).astype(jnp.float32)
        sent = jnp.concatenate([far_sums_ref[at, 0:EIGS, :], high, degrees - high], axis=0)
        sent_refs[at][...] = sent.astype(jnp.bfloat16)
    out_copy.wait()


SUMS = jax.ShapeDtypeStruct((COLS, ACC, BLOCK), jnp.float32)
NORM = jax.ShapeDtypeStruct((COLS, BLOCK, 128), jnp.float32)
ROW = jax.ShapeDtypeStruct((COLS, 8, BLOCK), jnp.float32)
TOKEN = jax.ShapeDtypeStruct((8, 128), jnp.float32)
SENT_SHAPE = jax.ShapeDtypeStruct((SENT, BLOCK), jnp.bfloat16)


def block_of(shape):
    return pl.BlockSpec((1, *shape[1:]), lambda g, flags: (g, 0, 0))


def whole(shape):
    return pl.BlockSpec(shape, lambda g, flags: (0, 0))


def own_cells(flags, blocks, far):
    return pl.pallas_call(
        own_kernel,
        out_shape=[SUMS, NORM, ROW, TOKEN],
        grid_spec=pltpu.PrefetchScalarGridSpec(
            num_scalar_prefetch=1,
            grid=(COLS,),
            in_specs=[block_of(blocks.shape), whole(far.shape)],
            out_specs=[block_of(SUMS.shape), block_of(NORM.shape), block_of(ROW.shape), whole(TOKEN.shape)],
            scratch_shapes=[pltpu.VMEM((BLOCK, BLOCK), jnp.bfloat16)],
        ),
        compiler_params=pltpu.CompilerParams(vmem_limit_bytes=56 << 20),
        cost_estimate=estimate(1),
        name="cells_own",
    )(flags, blocks, far)


def estimate(count):
    return pl.CostEstimate(
        flops=count * COST * BLOCK * BLOCK * WIDTH,
        bytes_accessed=(12 + count) << 20,
        transcendentals=count * 4 * BLOCK * BLOCK,
    )


def cells(flags, blocks, near_v, fars, norms, rows, sums):
    count = len(fars)
    buffers = [
        ((COLS, BLOCK, WIDTH), jnp.bfloat16),
        ((COLS, EIGS, BLOCK), jnp.bfloat16),
        ((count, PAYLOAD, WIDTH), jnp.bfloat16),
        ((COLS, BLOCK, 128), jnp.float32),
        ((COLS, 8, BLOCK), jnp.float32),
        ((COLS, ACC, BLOCK), jnp.float32),
        ((COLS, ACC, BLOCK), jnp.float32),
        ((BLOCK, BLOCK), jnp.bfloat16),
        ((count, BLOCK, 128), jnp.float32),
        ((count, ACC, BLOCK), jnp.float32),
    ]
    in_place = pl.BlockSpec(memory_space=pltpu.HBM)
    result = pl.pallas_call(
        functools.partial(cells_kernel, count),
        out_shape=[SUMS] + [SENT_SHAPE] * count + [TOKEN],
        grid_spec=pltpu.PrefetchScalarGridSpec(
            num_scalar_prefetch=1,
            grid=(1,),
            in_specs=[in_place] * (5 + count),
            out_specs=[in_place] + [whole(SENT_SHAPE.shape)] * count + [whole(TOKEN.shape)],
            scratch_shapes=[pltpu.VMEM(*buffer) for buffer in buffers]
            + [pltpu.SemaphoreType.DMA(size) for size in ((3, COLS), (count,), (2,))],
        ),
        input_output_aliases={5 + count: 0},
        compiler_params=pltpu.CompilerParams(vmem_limit_bytes=56 << 20),
        cost_estimate=estimate(count),
        name="cells",
    )(flags, blocks, near_v, *fars, norms, rows, sums)
    return result[0], result[1:-1], result[-1]


def tie_kernel(*refs):
    pass


def tie(arrays, *tokens):
    return pl.pallas_call(
        tie_kernel,
        out_shape=[jax.ShapeDtypeStruct(array.shape, array.dtype) for array in arrays],
        in_specs=[pl.BlockSpec(memory_space=pltpu.HBM)] * (len(arrays) + len(tokens)),
        out_specs=[pl.BlockSpec(memory_space=pltpu.HBM)] * len(arrays),
        input_output_aliases={at: at for at in range(len(arrays))},
        name="tie",
    )(*arrays, *tokens)


def solve_kernel(gram_ref, smoothed_ref, out_ref):
    rows = lax.broadcasted_iota(jnp.int32, (EIGS, 2 * EIGS), 0)
    lanes = lax.broadcasted_iota(jnp.int32, (EIGS, 2 * EIGS), 1)
    eye = jnp.where(rows + EIGS == lanes, 1.0, 0.0)[:, EIGS:]
    work = jnp.concatenate([gram_ref[...], eye], axis=1)
    below = rows[0:8, :]
    tiles, done = [work[at : at + 8, :] for at in range(0, EIGS, 8)], []
    while tiles:
        for j in range(0, 8, 2):
            at = len(done) * 8 + j
            columns1 = [jnp.broadcast_to(tile[:, at : at + 1], tile.shape) for tile in tiles]
            columns2 = [jnp.broadcast_to(tile[:, at + 1 : at + 2], tile.shape) for tile in tiles]
            first, cross = columns1[0][j : j + 1, :], columns1[0][j + 1 : j + 2, :]
            second = columns2[0][j + 1 : j + 2, :]
            row1, row2 = tiles[0][j : j + 1, :], tiles[0][j + 1 : j + 2, :]
            scale = 1.0 / (first * second - cross * cross)
            scaled1 = (second * row1 - cross * row2) * scale
            scaled2 = (first * row2 - cross * row1) * scale
            ratio = cross / first
            columns1[0] = jnp.where(below > j + 1, columns1[0], 0.0)
            columns2[0] = jnp.where(below > j + 1, columns2[0], 0.0)
            tiles = [
                tile - (column1 * scaled1 + column2 * scaled2)
                for tile, column1, column2 in zip(tiles, columns1, columns2)
            ]
            tiles[0] = jnp.where(below == j, row1 * lax.rsqrt(first), tiles[0])
            last = (row2 - ratio * row1) * lax.rsqrt(second - ratio * cross)
            tiles[0] = jnp.where(below == j + 1, last, tiles[0])
        done.append(tiles.pop(0))
    inverse = jnp.concatenate(done, axis=0)[:, EIGS:]
    out_ref[...] = jnp.dot(
        inverse, smoothed_ref[...], precision=lax.Precision.HIGHEST, preferred_element_type=jnp.float32
    )


def solve(gram, smoothed):
    return pl.pallas_call(
        solve_kernel,
        out_shape=jax.ShapeDtypeStruct(smoothed.shape, jnp.float32),
        in_specs=[pl.BlockSpec(memory_space=pltpu.VMEM)] * 2,
        out_specs=pl.BlockSpec(memory_space=pltpu.VMEM),
        name="solve",
    )(gram, smoothed)


def per_device(embeddings, vectors, block_pairs):
    here_row = lax.axis_index("row")
    here_col = lax.axis_index("col")
    here_y, here_x = here_row // SIDE, here_row % SIDE
    blocks = embeddings.reshape(COLS, BLOCK, WIDTH)

    def move(array, dy, dx, keep=None):
        return lax.ppermute(array, "row", shift(dy, dx, keep))

    def turn(array, by):
        return lax.ppermute(array, "col", [(i, (i + by * CORES) % COLS) for i in range(COLS)])

    def swap(array):
        return lax.ppermute(array, "col", [(i, i ^ 1) for i in range(COLS)])

    far = {"own": make_payload(here_col[None], blocks, vectors)}
    far["a"] = move(far["own"], 0, 1)
    far["b"] = move(far["own"], 1, 0)
    far["c"] = move(far["own"], -1, -1)
    far_ids, works = [], []
    for (dy, dx), keep in STAGES.values():
        from_row = (here_y - dy) % SIDE * SIDE + (here_x - dx) % SIDE
        far_ids.append(from_row * COLS + here_col)
        works.append(jnp.broadcast_to(True if keep is None else keep(here_y, here_x), (COLS,)))
    far_ids = jnp.stack(far_ids)[:, None]
    near_ids = (here_row * COLS + jnp.arange(COLS, dtype=jnp.int32))[None, :]
    wanted = jnp.stack([near_ids * NBLOCKS + far_ids, far_ids * NBLOCKS + near_ids])
    listed = block_pairs[:, 0] * NBLOCKS + block_pairs[:, 1]
    found = jnp.any(wanted[..., None] == listed, axis=-1)
    both_ways = (jnp.arange(len(STAGES)) > 0)[:, None]
    flags = jnp.where(jnp.stack(works), found[0] + 2 * (found[1] & both_ways), 0).astype(jnp.int32)

    starts = {name: at for at, name in enumerate(STAGES)}

    def work(group, sums):
        at = starts[group[0]]
        return cells(
            flags[at : at + len(group)].reshape(-1),
            blocks,
            near_v,
            [far[name] for name in group],
            norms,
            rows,
            sums,
        )

    def give_back(group, parts):
        returned = []
        for name, part in zip(group, parts):
            back = [(to, source) for source, to in shift(*STAGES[name][0], STAGES[name][1])]
            returned.append(lax.ppermute(part, "row", back))
        return returned

    near_v = lax.all_to_all(jnp.broadcast_to(vectors, (COLS, EIGS, BLOCK)), "col", 0, 0)
    sums, norms, rows, token = own_cells(flags[0], blocks, far["own"])

    far["a"], far["b"], far["c"] = tie([far["a"], far["b"], far["c"]], token, near_v)
    far["h"] = move(far["b"], 1, 0)
    far["e"] = move(far["c"], 0, -1)
    far["d"] = move(far["a"], -1, 0)
    far["g"] = move(far["a"], 0, 1, left_half)
    group1, group2, group3 = ("a", "b"), ("c", "d", "e", "h"), ("f", "g", "k")
    sums, parts, token = work(group1, sums)

    far["h"], far["e"], *parts = tie([far["h"], far["e"], *parts], token, far["g"])
    far["f"] = move(far["h"], 0, 1)
    far["k"] = move(far["e"], -1, 0, top_half)
    returned = give_back(("a",), parts[0:1])
    later = parts[1:]
    sums, parts, token = work(group2, sums)

    far["f"], far["k"], *parts = tie([far["f"], far["k"], *later, *parts], *returned)
    returned += give_back(("b", *group2), parts)
    sums, parts, token = work(group3, sums)

    sums, *parts = tie([sums, *parts], *returned[1:])
    returned += give_back(group3, parts)

    layer, core = here_col // CORES, here_col % CORES
    halves = sums.reshape(SIDE, CORES, ACC, BLOCK)
    mine = lax.dynamic_index_in_dim(halves, core, 1, keepdims=False)
    kept = mine + swap(lax.dynamic_index_in_dim(halves, 1 - core, 1, keepdims=False))
    layers = [lax.dynamic_index_in_dim(kept, (layer - k) % SIDE, 0, keepdims=False) for k in range(SIDE)]
    summed = layers[0] + (turn(layers[1], 3) + turn(layers[2], 2) + turn(layers[3], 1))
    totals, degrees = summed[0:EIGS], summed[EIGS : EIGS + 1]
    for part in returned:
        part = part.astype(jnp.float32)
        totals, degrees = totals + part[0:EIGS], degrees + (part[EIGS : EIGS + 1] + part[ACC : ACC + 1])
    smoothed = totals / degrees
    gram = jnp.dot(
        smoothed, smoothed.T, precision=lax.Precision.HIGHEST, preferred_element_type=jnp.float32
    ) / (BLOCK * NBLOCKS)
    gram = gram + swap(gram)
    gram = gram + (turn(gram, 1) + turn(gram, 2) + turn(gram, 3))
    everyone = jnp.broadcast_to(gram, (SIDE * SIDE, EIGS, EIGS))
    gram = jnp.sum(lax.all_to_all(everyone, "row", 0, 0), axis=0)
    return solve(gram, smoothed)


def solution(mesh):
    return jax.shard_map(
        per_device,
        mesh=mesh,
        in_specs=(P("row", None), P(None, ("row", "col")), P()),
        out_specs=P(None, ("row", "col")),
        check_vma=False,
    )
```

```python
import functools
import math

import jax
import jax.numpy as jnp
from jax import lax
from jax.experimental import pallas as pl
from jax.experimental.pallas import tpu as pltpu
from jax.sharding import PartitionSpec as P

BLOCK = 512
WIDTH = 1024
EIGS = 64
NBLOCKS = 128
SIDE = 4
COLS = 8
CORES = 2
VROWS = BLOCK + EIGS // 2
PAYLOAD = VROWS + 16
ACC = EIGS + 8
SENT = EIGS + 16
SCALE = math.sqrt(math.log2(math.e) / math.sqrt(WIDTH))
COST = 8
NT = (((1,), (1,)), ((), ()))


def shift(dy, dx, keep=None):
    pairs = []
    for y in range(SIDE):
        for x in range(SIDE):
            to_y, to_x = (y + dy) % SIDE, (x + dx) % SIDE
            if keep is None or keep(to_y, to_x):
                pairs.append((y * SIDE + x, to_y * SIDE + to_x))
    return pairs


def left_half(y, x):
    return x < SIDE // 2


def top_half(y, x):
    return y < SIDE // 2


STAGES = {
    "own": ((0, 0), None),
    "a": ((0, 1), None),
    "b": ((1, 0), None),
    "c": ((-1, -1), None),
    "d": ((-1, 1), None),
    "e": ((-1, -2), None),
    "h": ((2, 0), top_half),
    "f": ((2, 1), None),
    "g": ((0, 2), left_half),
    "k": ((2, 2), top_half),
}


def row_norm(x):
    return lax.rsqrt(jnp.sum(x * x, axis=1, keepdims=True) * (1.0 / WIDTH) + 1e-06)


def payload_kernel(index_ref, x_ref, v_ref, out_ref):
    x = x_ref[0]
    out_ref[0:BLOCK, :] = x
    half = EIGS // 2
    out_ref[BLOCK:VROWS, 0:BLOCK] = v_ref[0:half, :]
    out_ref[BLOCK:VROWS, BLOCK : 2 * BLOCK] = v_ref[half:EIGS, :]
    norms = jnp.broadcast_to(row_norm(x.astype(jnp.float32)) * SCALE, (BLOCK, 128))
    rows = norms.T[0:16, :]
    high = rows.astype(jnp.bfloat16)
    low = (rows - high.astype(jnp.float32)).astype(jnp.bfloat16)
    out_ref[VROWS:PAYLOAD, 0:BLOCK] = high
    out_ref[VROWS:PAYLOAD, BLOCK : 2 * BLOCK] = low


def make_payload(here_col, blocks, vectors):
    return pl.pallas_call(
        payload_kernel,
        out_shape=jax.ShapeDtypeStruct((PAYLOAD, WIDTH), jnp.bfloat16),
        grid_spec=pltpu.PrefetchScalarGridSpec(
            num_scalar_prefetch=1,
            grid=(1,),
            in_specs=[
                pl.BlockSpec((1, BLOCK, WIDTH), lambda g, index: (index[0], 0, 0)),
                pl.BlockSpec((EIGS, BLOCK), lambda g, index: (0, 0)),
            ],
            out_specs=pl.BlockSpec((PAYLOAD, WIDTH), lambda g, index: (0, 0)),
        ),
        name="payload",
    )(here_col, blocks, vectors)


def side_vectors(side):
    half = EIGS // 2
    ones = jnp.ones((16, BLOCK), jnp.bfloat16)
    return jnp.concatenate([side[0:half, 0:BLOCK], side[0:half, BLOCK : 2 * BLOCK], ones], axis=0)


def side_norms(side):
    row = side[EIGS // 2 : EIGS // 2 + 1, :].astype(jnp.float32)
    return row[:, 0:BLOCK] + row[:, BLOCK : 2 * BLOCK]


def double(columns):
    return jnp.concatenate([columns, columns], axis=1)


def own_kernel(flags_ref, x_ref, far_ref, new_ref, norm_ref, row_ref, token_ref, p_ref):
    step = pl.program_id(0)
    new_ref[...] = jnp.zeros_like(new_ref)
    token_ref[...] = jnp.zeros_like(token_ref)
    norms = jnp.broadcast_to(row_norm(x_ref[0].astype(jnp.float32)) * SCALE, (BLOCK, 128))
    norm_ref[0] = norms
    row_ref[0] = norms.T[0:8, :]

    @pl.when(flags_ref[step] > 0)
    def _():
        side = far_ref[BLOCK:PAYLOAD, :]
        near, far = double(norm_ref[0]), side_norms(side)
        for at in range(0, BLOCK, 256):
            scores = lax.dot_general(
                x_ref[0], far_ref[at : at + 256, :], NT, preferred_element_type=jnp.float32
            )
            p_ref[:, at : at + 256] = jnp.exp2(scores * near * far[:, at : at + 256]).astype(jnp.bfloat16)
        part = lax.dot_general(side_vectors(side), p_ref[...], NT, preferred_element_type=jnp.float32)
        new_ref[0] = part[0:ACC, :]


def cells_kernel(count, flags_ref, x_hbm, v_hbm, *refs):
    far_hbms, (norm_hbm, row_hbm, old_hbm, new_hbm), refs = refs[:count], refs[count : count + 4], refs[count + 4 :]
    sent_refs, token_ref, refs = refs[:count], refs[count], refs[count + 1 :]
    x_ref, v_ref, far_ref, norm_ref, row_ref, old_ref, sums_ref, p_ref, column_ref, far_sums_ref = refs[:10]
    near_sem, far_sem, sem = refs[10:]

    def near_copies(near):
        pairs = ((x_hbm, x_ref), (norm_hbm, norm_ref), (v_hbm, v_ref))
        return [
            pltpu.make_async_copy(source.at[near], to.at[near], near_sem.at[at, near])
            for at, (source, to) in enumerate(pairs)
        ]

    far_copies = [pltpu.make_async_copy(far_hbms[at], far_ref.at[at], far_sem.at[at]) for at in range(count)]
    row_copy = pltpu.make_async_copy(row_hbm, row_ref, sem.at[0])
    old_copy = pltpu.make_async_copy(old_hbm, old_ref, sem.at[1])
    for copy in (far_copies[0], *near_copies(0), row_copy, *far_copies[1:], *near_copies(1), old_copy):
        copy.start()

    token_ref[...] = jnp.zeros_like(token_ref)
    far_sums_ref[...] = jnp.zeros_like(far_sums_ref)
    sums_ref[...] = jnp.zeros_like(sums_ref)

    def forward_only(at, near):
        rows, far = row_ref[near, 0:1, :], double(column_ref[at])
        for to in range(0, BLOCK, 256):
            scores = lax.dot_general(
                far_ref[at, 0:BLOCK, :], x_ref[near, to : to + 256, :], NT, preferred_element_type=jnp.float32
            )
            p_ref[:, to : to + 256] = jnp.exp2(scores * rows[:, to : to + 256] * far).astype(jnp.bfloat16)
        part = jnp.dot(side_vectors(far_ref[at, BLOCK:PAYLOAD, :]), p_ref[...], preferred_element_type=jnp.float32)
        sums_ref[near] += part[0:ACC, :]

    def backward(at, near, both):
        side = far_ref[at, BLOCK:PAYLOAD, :]
        columns, far = double(norm_ref[near]), side_norms(side)
        for to in range(0, BLOCK, 256):
            scores = lax.dot_general(
                x_ref[near], far_ref[at, to : to + 256, :], NT, preferred_element_type=jnp.float32
            )
            p_ref[:, to : to + 256] = jnp.exp2(scores * columns * far[:, to : to + 256]).astype(jnp.bfloat16)
        vectors = jnp.concatenate([v_ref[near], jnp.ones((16, BLOCK), jnp.bfloat16)], axis=0)
        part = jnp.dot(vectors, p_ref[...], preferred_element_type=jnp.float32)
        far_sums_ref[at] += part[0:ACC, :]
        if both:
            part = lax.dot_general(side_vectors(side), p_ref[...], NT, preferred_element_type=jnp.float32)
            sums_ref[near] += part[0:ACC, :]

    @pl.loop(0, COLS)
    def _(near):
        @pl.when(near + 2 < COLS)
        def _():
            for copy in near_copies(near + 2):
                copy.start()

        for copy in near_copies(near):
            copy.wait()

        @pl.when(near == 0)
        def _():
            row_copy.wait()

        @pl.loop(0, count)
        def _(at):
            @pl.when(near == 0)
            def _():
                pltpu.make_async_copy(far_hbms[0], far_ref.at[at], far_sem.at[at]).wait()
                column_ref[at] = jnp.broadcast_to(side_norms(far_ref[at, BLOCK:PAYLOAD, :]), (128, BLOCK)).T

            flag = flags_ref[at * COLS + near]
            pl.when(flag == 1)(functools.partial(forward_only, at, near))
            pl.when(flag == 2)(functools.partial(backward, at, near, False))
            pl.when(flag == 3)(functools.partial(backward, at, near, True))

    old_copy.wait()
    sums_ref[...] += old_ref[...]
    out_copy = pltpu.make_async_copy(sums_ref, new_hbm, sem.at[0])
    out_copy.start()
    for at in range(count):
        degrees = far_sums_ref[at, EIGS:ACC, :]
        high = degrees.astype(jnp.bfloat16).astype(jnp.float32)
        sent = jnp.concatenate([far_sums_ref[at, 0:EIGS, :], high, degrees - high], axis=0)
        sent_refs[at][...] = sent.astype(jnp.bfloat16)
    out_copy.wait()


SUMS = jax.ShapeDtypeStruct((COLS, ACC, BLOCK), jnp.float32)
NORM = jax.ShapeDtypeStruct((COLS, BLOCK, 128), jnp.float32)
ROW = jax.ShapeDtypeStruct((COLS, 8, BLOCK), jnp.float32)
TOKEN = jax.ShapeDtypeStruct((8, 128), jnp.float32)
SENT_SHAPE = jax.ShapeDtypeStruct((SENT, BLOCK), jnp.bfloat16)


def block_of(shape):
    return pl.BlockSpec((1, *shape[1:]), lambda g, flags: (g, 0, 0))


def whole(shape):
    return pl.BlockSpec(shape, lambda g, flags: (0, 0))


def own_cells(flags, blocks, far):
    return pl.pallas_call(
        own_kernel,
        out_shape=[SUMS, NORM, ROW, TOKEN],
        grid_spec=pltpu.PrefetchScalarGridSpec(
            num_scalar_prefetch=1,
            grid=(COLS,),
            in_specs=[block_of(blocks.shape), whole(far.shape)],
            out_specs=[block_of(SUMS.shape), block_of(NORM.shape), block_of(ROW.shape), whole(TOKEN.shape)],
            scratch_shapes=[pltpu.VMEM((BLOCK, BLOCK), jnp.bfloat16)],
        ),
        compiler_params=pltpu.CompilerParams(vmem_limit_bytes=56 << 20),
        cost_estimate=estimate(1),
        name="cells_own",
    )(flags, blocks, far)


def estimate(count):
    return pl.CostEstimate(
        flops=count * COST * BLOCK * BLOCK * WIDTH,
        bytes_accessed=(12 + count) << 20,
        transcendentals=count * 4 * BLOCK * BLOCK,
    )


def cells(flags, blocks, near_v, fars, norms, rows, sums):
    count = len(fars)
    buffers = [
        ((COLS, BLOCK, WIDTH), jnp.bfloat16),
        ((COLS, EIGS, BLOCK), jnp.bfloat16),
        ((count, PAYLOAD, WIDTH), jnp.bfloat16),
        ((COLS, BLOCK, 128), jnp.float32),
        ((COLS, 8, BLOCK), jnp.float32),
        ((COLS, ACC, BLOCK), jnp.float32),
        ((COLS, ACC, BLOCK), jnp.float32),
        ((BLOCK, BLOCK), jnp.bfloat16),
        ((count, BLOCK, 128), jnp.float32),
        ((count, ACC, BLOCK), jnp.float32),
    ]
    in_place = pl.BlockSpec(memory_space=pltpu.HBM)
    result = pl.pallas_call(
        functools.partial(cells_kernel, count),
        out_shape=[SUMS] + [SENT_SHAPE] * count + [TOKEN],
        grid_spec=pltpu.PrefetchScalarGridSpec(
            num_scalar_prefetch=1,
            grid=(1,),
            in_specs=[in_place] * (5 + count),
            out_specs=[in_place] + [whole(SENT_SHAPE.shape)] * count + [whole(TOKEN.shape)],
            scratch_shapes=[pltpu.VMEM(*buffer) for buffer in buffers]
            + [pltpu.SemaphoreType.DMA(size) for size in ((3, COLS), (count,), (2,))],
        ),
        input_output_aliases={5 + count: 0},
        compiler_params=pltpu.CompilerParams(vmem_limit_bytes=56 << 20),
        cost_estimate=estimate(count),
        name="cells",
    )(flags, blocks, near_v, *fars, norms, rows, sums)
    return result[0], result[1:-1], result[-1]


def tie_kernel(*refs):
    pass


def tie(arrays, *tokens):
    return pl.pallas_call(
        tie_kernel,
        out_shape=[jax.ShapeDtypeStruct(array.shape, array.dtype) for array in arrays],
        in_specs=[pl.BlockSpec(memory_space=pltpu.HBM)] * (len(arrays) + len(tokens)),
        out_specs=[pl.BlockSpec(memory_space=pltpu.HBM)] * len(arrays),
        input_output_aliases={at: at for at in range(len(arrays))},
        name="tie",
    )(*arrays, *tokens)


def solve_kernel(gram_ref, smoothed_ref, out_ref):
    rows = lax.broadcasted_iota(jnp.int32, (EIGS, 2 * EIGS), 0)
    lanes = lax.broadcasted_iota(jnp.int32, (EIGS, 2 * EIGS), 1)
    eye = jnp.where(rows + EIGS == lanes, 1.0, 0.0)[:, EIGS:]
    work = jnp.concatenate([gram_ref[...], eye], axis=1)
    below = rows[0:8, :]
    tiles, done = [work[at : at + 8, :] for at in range(0, EIGS, 8)], []
    while tiles:
        for j in range(0, 8, 2):
            at = len(done) * 8 + j
            columns1 = [jnp.broadcast_to(tile[:, at : at + 1], tile.shape) for tile in tiles]
            columns2 = [jnp.broadcast_to(tile[:, at + 1 : at + 2], tile.shape) for tile in tiles]
            first, cross = columns1[0][j : j + 1, :], columns1[0][j + 1 : j + 2, :]
            second = columns2[0][j + 1 : j + 2, :]
            row1, row2 = tiles[0][j : j + 1, :], tiles[0][j + 1 : j + 2, :]
            scale = 1.0 / (first * second - cross * cross)
            scaled1 = (second * row1 - cross * row2) * scale
            scaled2 = (first * row2 - cross * row1) * scale
            ratio = cross / first
            columns1[0] = jnp.where(below > j + 1, columns1[0], 0.0)
            columns2[0] = jnp.where(below > j + 1, columns2[0], 0.0)
            tiles = [
                tile - (column1 * scaled1 + column2 * scaled2)
                for tile, column1, column2 in zip(tiles, columns1, columns2)
            ]
            tiles[0] = jnp.where(below == j, row1 * lax.rsqrt(first), tiles[0])
            last = (row2 - ratio * row1) * lax.rsqrt(second - ratio * cross)
            tiles[0] = jnp.where(below == j + 1, last, tiles[0])
        done.append(tiles.pop(0))
    inverse = jnp.concatenate(done, axis=0)[:, EIGS:]
    out_ref[...] = jnp.dot(
        inverse, smoothed_ref[...], precision=lax.Precision.HIGHEST, preferred_element_type=jnp.float32
    )


def solve(gram, smoothed):
    return pl.pallas_call(
        solve_kernel,
        out_shape=jax.ShapeDtypeStruct(smoothed.shape, jnp.float32),
        in_specs=[pl.BlockSpec(memory_space=pltpu.VMEM)] * 2,
        out_specs=pl.BlockSpec(memory_space=pltpu.VMEM),
        name="solve",
    )(gram, smoothed)


def per_device(embeddings, vectors, block_pairs):
    here_row = lax.axis_index("row")
    here_col = lax.axis_index("col")
    here_y, here_x = here_row // SIDE, here_row % SIDE
    blocks = embeddings.reshape(COLS, BLOCK, WIDTH)

    def move(array, dy, dx, keep=None):
        return lax.ppermute(array, "row", shift(dy, dx, keep))

    def turn(array, by):
        return lax.ppermute(array, "col", [(i, (i + by * CORES) % COLS) for i in range(COLS)])

    def swap(array):
        return lax.ppermute(array, "col", [(i, i ^ 1) for i in range(COLS)])

    far = {"own": make_payload(here_col[None], blocks, vectors)}
    far["a"] = move(far["own"], 0, 1)
    far["b"] = move(far["own"], 1, 0)
    far["c"] = move(far["own"], -1, -1)
    far_ids, works = [], []
    for (dy, dx), keep in STAGES.values():
        from_row = (here_y - dy) % SIDE * SIDE + (here_x - dx) % SIDE
        far_ids.append(from_row * COLS + here_col)
        works.append(jnp.broadcast_to(True if keep is None else keep(here_y, here_x), (COLS,)))
    far_ids = jnp.stack(far_ids)[:, None]
    near_ids = (here_row * COLS + jnp.arange(COLS, dtype=jnp.int32))[None, :]
    wanted = jnp.stack([near_ids * NBLOCKS + far_ids, far_ids * NBLOCKS + near_ids])
    listed = block_pairs[:, 0] * NBLOCKS + block_pairs[:, 1]
    found = jnp.any(wanted[..., None] == listed, axis=-1)
    both_ways = (jnp.arange(len(STAGES)) > 0)[:, None]
    flags = jnp.where(jnp.stack(works), found[0] + 2 * (found[1] & both_ways), 0).astype(jnp.int32)

    starts = {name: at for at, name in enumerate(STAGES)}

    def work(group, sums):
        at = starts[group[0]]
        return cells(
            flags[at : at + len(group)].reshape(-1),
            blocks,
            near_v,
            [far[name] for name in group],
            norms,
            rows,
            sums,
        )

    def give_back(group, parts):
        returned = []
        for name, part in zip(group, parts):
            back = [(to, source) for source, to in shift(*STAGES[name][0], STAGES[name][1])]
            returned.append(lax.ppermute(part, "row", back))
        return returned

    near_v = lax.all_to_all(jnp.broadcast_to(vectors, (COLS, EIGS, BLOCK)), "col", 0, 0)
    sums, norms, rows, token = own_cells(flags[0], blocks, far["own"])

    far["a"], far["b"], far["c"] = tie([far["a"], far["b"], far["c"]], token, near_v)
    far["h"] = move(far["b"], 1, 0)
    far["e"] = move(far["c"], 0, -1)
    far["d"] = move(far["a"], -1, 0)
    far["g"] = move(far["a"], 0, 1, left_half)
    group1, group2, group3 = ("a", "b", "c"), ("d", "e", "h"), ("f", "g", "k")
    sums, parts, token = work(group1, sums)

    far["h"], far["e"], *parts = tie([far["h"], far["e"], *parts], token, far["d"], far["g"])
    far["f"] = move(far["h"], 0, 1)
    far["k"] = move(far["e"], -1, 0, top_half)
    returned = give_back(("a",), parts[0:1])
    later = parts[1:]
    sums, parts, token = work(group2, sums)

    ready = tie([*later, parts[0]], *returned, token)
    returned += give_back(("b", "c", "d"), ready)
    far["f"], far["k"], *parts = tie([far["f"], far["k"], *parts[1:]], ready[0])
    returned += give_back(("e", "h"), parts)
    sums, parts, token = work(group3, sums)

    sums, *parts = tie([sums, *parts], *returned[1:])
    returned += give_back(group3, parts)

    layer, core = here_col // CORES, here_col % CORES
    halves = sums.reshape(SIDE, CORES, ACC, BLOCK)
    mine = lax.dynamic_index_in_dim(halves, core, 1, keepdims=False)
    kept = mine + swap(lax.dynamic_index_in_dim(halves, 1 - core, 1, keepdims=False))
    layers = [lax.dynamic_index_in_dim(kept, (layer - k) % SIDE, 0, keepdims=False) for k in range(SIDE)]
    summed = layers[0] + (turn(layers[1], 3) + turn(layers[2], 2) + turn(layers[3], 1))
    totals, degrees = summed[0:EIGS], summed[EIGS : EIGS + 1]
    for part in returned:
        part = part.astype(jnp.float32)
        totals, degrees = totals + part[0:EIGS], degrees + (part[EIGS : EIGS + 1] + part[ACC : ACC + 1])
    smoothed = totals / degrees
    gram = jnp.dot(
        smoothed, smoothed.T, precision=lax.Precision.HIGHEST, preferred_element_type=jnp.float32
    ) / (BLOCK * NBLOCKS)
    gram = gram + swap(gram)
    gram = gram + (turn(gram, 1) + turn(gram, 2) + turn(gram, 3))
    everyone = jnp.broadcast_to(gram, (SIDE * SIDE, EIGS, EIGS))
    gram = jnp.sum(lax.all_to_all(everyone, "row", 0, 0), axis=0)
    return solve(gram, smoothed)


def solution(mesh):
    return jax.shard_map(
        per_device,
        mesh=mesh,
        in_specs=(P("row", None), P(None, ("row", "col")), P()),
        out_specs=P(None, ("row", "col")),
        check_vma=False,
    )
```

```python
import functools
import math

import jax
import jax.numpy as jnp
from jax import lax
from jax.experimental import pallas as pl
from jax.experimental.pallas import tpu as pltpu
from jax.sharding import PartitionSpec as P

BLOCK = 512
WIDTH = 1024
EIGS = 64
NBLOCKS = 128
SIDE = 4
COLS = 8
CORES = 2
VROWS = BLOCK + EIGS // 2
PAYLOAD = VROWS + 16
ACC = EIGS + 8
SENT = EIGS + 16
SCALE = math.sqrt(math.log2(math.e) / math.sqrt(WIDTH))
COST = 8
NT = (((1,), (1,)), ((), ()))


def shift(dy, dx, keep=None):
    pairs = []
    for y in range(SIDE):
        for x in range(SIDE):
            to_y, to_x = (y + dy) % SIDE, (x + dx) % SIDE
            if keep is None or keep(to_y, to_x):
                pairs.append((y * SIDE + x, to_y * SIDE + to_x))
    return pairs


def left_half(y, x):
    return x < SIDE // 2


def top_half(y, x):
    return y < SIDE // 2


STAGES = {
    "own": ((0, 0), None),
    "a": ((0, 1), None),
    "b": ((1, 0), None),
    "c": ((-1, -1), None),
    "d": ((-1, 1), None),
    "e": ((-1, -2), None),
    "h": ((2, 0), top_half),
    "f": ((2, 1), None),
    "g": ((0, 2), left_half),
    "k": ((2, 2), top_half),
}


def row_norm(x):
    return lax.rsqrt(jnp.sum(x * x, axis=1, keepdims=True) * (1.0 / WIDTH) + 1e-06)


def payload_kernel(index_ref, x_ref, v_ref, out_ref):
    x = x_ref[0]
    out_ref[0:BLOCK, :] = x
    half = EIGS // 2
    out_ref[BLOCK:VROWS, 0:BLOCK] = v_ref[0:half, :]
    out_ref[BLOCK:VROWS, BLOCK : 2 * BLOCK] = v_ref[half:EIGS, :]
    norms = jnp.broadcast_to(row_norm(x.astype(jnp.float32)) * SCALE, (BLOCK, 128))
    rows = norms.T[0:16, :]
    high = rows.astype(jnp.bfloat16)
    low = (rows - high.astype(jnp.float32)).astype(jnp.bfloat16)
    out_ref[VROWS:PAYLOAD, 0:BLOCK] = high
    out_ref[VROWS:PAYLOAD, BLOCK : 2 * BLOCK] = low


def make_payload(here_col, blocks, vectors):
    return pl.pallas_call(
        payload_kernel,
        out_shape=jax.ShapeDtypeStruct((PAYLOAD, WIDTH), jnp.bfloat16),
        grid_spec=pltpu.PrefetchScalarGridSpec(
            num_scalar_prefetch=1,
            grid=(1,),
            in_specs=[
                pl.BlockSpec((1, BLOCK, WIDTH), lambda g, index: (index[0], 0, 0)),
                pl.BlockSpec((EIGS, BLOCK), lambda g, index: (0, 0)),
            ],
            out_specs=pl.BlockSpec((PAYLOAD, WIDTH), lambda g, index: (0, 0)),
        ),
        name="payload",
    )(here_col, blocks, vectors)


def side_vectors(side):
    half = EIGS // 2
    ones = jnp.ones((16, BLOCK), jnp.bfloat16)
    return jnp.concatenate([side[0:half, 0:BLOCK], side[0:half, BLOCK : 2 * BLOCK], ones], axis=0)


def side_norms(side):
    row = side[EIGS // 2 : EIGS // 2 + 1, :].astype(jnp.float32)
    return row[:, 0:BLOCK] + row[:, BLOCK : 2 * BLOCK]


def double(columns):
    return jnp.concatenate([columns, columns], axis=1)


def own_kernel(flags_ref, x_ref, far_ref, new_ref, norm_ref, row_ref, token_ref, p_ref):
    step = pl.program_id(0)
    new_ref[...] = jnp.zeros_like(new_ref)
    token_ref[...] = jnp.zeros_like(token_ref)
    norms = jnp.broadcast_to(row_norm(x_ref[0].astype(jnp.float32)) * SCALE, (BLOCK, 128))
    norm_ref[0] = norms
    row_ref[0] = norms.T[0:8, :]

    @pl.when(flags_ref[step] > 0)
    def _():
        side = far_ref[BLOCK:PAYLOAD, :]
        near, far = double(norm_ref[0]), side_norms(side)
        for at in range(0, BLOCK, 256):
            scores = lax.dot_general(
                x_ref[0], far_ref[at : at + 256, :], NT, preferred_element_type=jnp.float32
            )
            p_ref[:, at : at + 256] = jnp.exp2(scores * near * far[:, at : at + 256]).astype(jnp.bfloat16)
        part = lax.dot_general(side_vectors(side), p_ref[...], NT, preferred_element_type=jnp.float32)
        new_ref[0] = part[0:ACC, :]


def cells_kernel(count, flags_ref, x_hbm, v_hbm, *refs):
    far_hbms, (norm_hbm, row_hbm, old_hbm, new_hbm), refs = refs[:count], refs[count : count + 4], refs[count + 4 :]
    sent_refs, token_ref, refs = refs[:count], refs[count], refs[count + 1 :]
    x_ref, v_ref, far_ref, norm_ref, row_ref, old_ref, sums_ref, p_ref, column_ref, far_sums_ref = refs[:10]
    near_sem, far_sem, sem = refs[10:]

    def near_copies(near):
        pairs = ((x_hbm, x_ref), (norm_hbm, norm_ref), (v_hbm, v_ref))
        return [
            pltpu.make_async_copy(source.at[near], to.at[near], near_sem.at[at, near])
            for at, (source, to) in enumerate(pairs)
        ]

    far_copies = [pltpu.make_async_copy(far_hbms[at], far_ref.at[at], far_sem.at[at]) for at in range(count)]
    row_copy = pltpu.make_async_copy(row_hbm, row_ref, sem.at[0])
    old_copy = pltpu.make_async_copy(old_hbm, old_ref, sem.at[1])
    for copy in (far_copies[0], *near_copies(0), row_copy, *far_copies[1:], *near_copies(1), old_copy):
        copy.start()

    token_ref[...] = jnp.zeros_like(token_ref)
    far_sums_ref[...] = jnp.zeros_like(far_sums_ref)
    sums_ref[...] = jnp.zeros_like(sums_ref)

    def forward_only(at, near):
        rows, far = row_ref[near, 0:1, :], double(column_ref[at])
        for to in range(0, BLOCK, 256):
            scores = lax.dot_general(
                far_ref[at, 0:BLOCK, :], x_ref[near, to : to + 256, :], NT, preferred_element_type=jnp.float32
            )
            p_ref[:, to : to + 256] = jnp.exp2(scores * rows[:, to : to + 256] * far).astype(jnp.bfloat16)
        part = jnp.dot(side_vectors(far_ref[at, BLOCK:PAYLOAD, :]), p_ref[...], preferred_element_type=jnp.float32)
        sums_ref[near] += part[0:ACC, :]

    def backward(at, near, both):
        side = far_ref[at, BLOCK:PAYLOAD, :]
        columns, far = double(norm_ref[near]), side_norms(side)
        for to in range(0, BLOCK, 256):
            scores = lax.dot_general(
                x_ref[near], far_ref[at, to : to + 256, :], NT, preferred_element_type=jnp.float32
            )
            p_ref[:, to : to + 256] = jnp.exp2(scores * columns * far[:, to : to + 256]).astype(jnp.bfloat16)
        vectors = jnp.concatenate([v_ref[near], jnp.ones((16, BLOCK), jnp.bfloat16)], axis=0)
        part = jnp.dot(vectors, p_ref[...], preferred_element_type=jnp.float32)
        far_sums_ref[at] += part[0:ACC, :]
        if both:
            part = lax.dot_general(side_vectors(side), p_ref[...], NT, preferred_element_type=jnp.float32)
            sums_ref[near] += part[0:ACC, :]

    @pl.loop(0, COLS)
    def _(near):
        @pl.when(near + 2 < COLS)
        def _():
            for copy in near_copies(near + 2):
                copy.start()

        for copy in near_copies(near):
            copy.wait()

        @pl.when(near == 0)
        def _():
            row_copy.wait()

        @pl.loop(0, count)
        def _(at):
            @pl.when(near == 0)
            def _():
                pltpu.make_async_copy(far_hbms[0], far_ref.at[at], far_sem.at[at]).wait()
                column_ref[at] = jnp.broadcast_to(side_norms(far_ref[at, BLOCK:PAYLOAD, :]), (128, BLOCK)).T

            flag = flags_ref[at * COLS + near]
            pl.when(flag == 1)(functools.partial(forward_only, at, near))
            pl.when(flag == 2)(functools.partial(backward, at, near, False))
            pl.when(flag == 3)(functools.partial(backward, at, near, True))

    old_copy.wait()
    sums_ref[...] += old_ref[...]
    out_copy = pltpu.make_async_copy(sums_ref, new_hbm, sem.at[0])
    out_copy.start()
    for at in range(count):
        degrees = far_sums_ref[at, EIGS:ACC, :]
        high = degrees.astype(jnp.bfloat16).astype(jnp.float32)
        sent = jnp.concatenate([far_sums_ref[at, 0:EIGS, :], high, degrees - high], axis=0)
        sent_refs[at][...] = sent.astype(jnp.bfloat16)
    out_copy.wait()


SUMS = jax.ShapeDtypeStruct((COLS, ACC, BLOCK), jnp.float32)
NORM = jax.ShapeDtypeStruct((COLS, BLOCK, 128), jnp.float32)
ROW = jax.ShapeDtypeStruct((COLS, 8, BLOCK), jnp.float32)
TOKEN = jax.ShapeDtypeStruct((8, 128), jnp.float32)
SENT_SHAPE = jax.ShapeDtypeStruct((SENT, BLOCK), jnp.bfloat16)


def block_of(shape):
    return pl.BlockSpec((1, *shape[1:]), lambda g, flags: (g, 0, 0))


def whole(shape):
    return pl.BlockSpec(shape, lambda g, flags: (0, 0))


def own_cells(flags, blocks, far):
    return pl.pallas_call(
        own_kernel,
        out_shape=[SUMS, NORM, ROW, TOKEN],
        grid_spec=pltpu.PrefetchScalarGridSpec(
            num_scalar_prefetch=1,
            grid=(COLS,),
            in_specs=[block_of(blocks.shape), whole(far.shape)],
            out_specs=[block_of(SUMS.shape), block_of(NORM.shape), block_of(ROW.shape), whole(TOKEN.shape)],
            scratch_shapes=[pltpu.VMEM((BLOCK, BLOCK), jnp.bfloat16)],
        ),
        compiler_params=pltpu.CompilerParams(vmem_limit_bytes=56 << 20),
        cost_estimate=estimate(1),
        name="cells_own",
    )(flags, blocks, far)


def estimate(count):
    return pl.CostEstimate(
        flops=count * COST * BLOCK * BLOCK * WIDTH,
        bytes_accessed=(12 + count) << 20,
        transcendentals=count * 4 * BLOCK * BLOCK,
    )


def cells(flags, blocks, near_v, fars, norms, rows, sums):
    count = len(fars)
    buffers = [
        ((COLS, BLOCK, WIDTH), jnp.bfloat16),
        ((COLS, EIGS, BLOCK), jnp.bfloat16),
        ((count, PAYLOAD, WIDTH), jnp.bfloat16),
        ((COLS, BLOCK, 128), jnp.float32),
        ((COLS, 8, BLOCK), jnp.float32),
        ((COLS, ACC, BLOCK), jnp.float32),
        ((COLS, ACC, BLOCK), jnp.float32),
        ((BLOCK, BLOCK), jnp.bfloat16),
        ((count, BLOCK, 128), jnp.float32),
        ((count, ACC, BLOCK), jnp.float32),
    ]
    in_place = pl.BlockSpec(memory_space=pltpu.HBM)
    result = pl.pallas_call(
        functools.partial(cells_kernel, count),
        out_shape=[SUMS] + [SENT_SHAPE] * count + [TOKEN],
        grid_spec=pltpu.PrefetchScalarGridSpec(
            num_scalar_prefetch=1,
            grid=(1,),
            in_specs=[in_place] * (5 + count),
            out_specs=[in_place] + [whole(SENT_SHAPE.shape)] * count + [whole(TOKEN.shape)],
            scratch_shapes=[pltpu.VMEM(*buffer) for buffer in buffers]
            + [pltpu.SemaphoreType.DMA(size) for size in ((3, COLS), (count,), (2,))],
        ),
        input_output_aliases={5 + count: 0},
        compiler_params=pltpu.CompilerParams(vmem_limit_bytes=56 << 20),
        cost_estimate=estimate(count),
        name="cells",
    )(flags, blocks, near_v, *fars, norms, rows, sums)
    return result[0], result[1:-1], result[-1]


def tie_kernel(*refs):
    pass


def tie(arrays, *tokens):
    return pl.pallas_call(
        tie_kernel,
        out_shape=[jax.ShapeDtypeStruct(array.shape, array.dtype) for array in arrays],
        in_specs=[pl.BlockSpec(memory_space=pltpu.HBM)] * (len(arrays) + len(tokens)),
        out_specs=[pl.BlockSpec(memory_space=pltpu.HBM)] * len(arrays),
        input_output_aliases={at: at for at in range(len(arrays))},
        name="tie",
    )(*arrays, *tokens)


def solve_kernel(gram_ref, smoothed_ref, out_ref):
    rows = lax.broadcasted_iota(jnp.int32, (EIGS, 2 * EIGS), 0)
    lanes = lax.broadcasted_iota(jnp.int32, (EIGS, 2 * EIGS), 1)
    eye = jnp.where(rows + EIGS == lanes, 1.0, 0.0)[:, EIGS:]
    work = jnp.concatenate([gram_ref[...], eye], axis=1)
    below = rows[0:8, :]
    tiles, done = [work[at : at + 8, :] for at in range(0, EIGS, 8)], []
    while tiles:
        for j in range(0, 8, 2):
            at = len(done) * 8 + j
            columns1 = [jnp.broadcast_to(tile[:, at : at + 1], tile.shape) for tile in tiles]
            columns2 = [jnp.broadcast_to(tile[:, at + 1 : at + 2], tile.shape) for tile in tiles]
            first, cross = columns1[0][j : j + 1, :], columns1[0][j + 1 : j + 2, :]
            second = columns2[0][j + 1 : j + 2, :]
            row1, row2 = tiles[0][j : j + 1, :], tiles[0][j + 1 : j + 2, :]
            scale = 1.0 / (first * second - cross * cross)
            scaled1 = (second * row1 - cross * row2) * scale
            scaled2 = (first * row2 - cross * row1) * scale
            ratio = cross / first
            columns1[0] = jnp.where(below > j + 1, columns1[0], 0.0)
            columns2[0] = jnp.where(below > j + 1, columns2[0], 0.0)
            tiles = [
                tile - (column1 * scaled1 + column2 * scaled2)
                for tile, column1, column2 in zip(tiles, columns1, columns2)
            ]
            tiles[0] = jnp.where(below == j, row1 * lax.rsqrt(first), tiles[0])
            last = (row2 - ratio * row1) * lax.rsqrt(second - ratio * cross)
            tiles[0] = jnp.where(below == j + 1, last, tiles[0])
        done.append(tiles.pop(0))
    inverse = jnp.concatenate(done, axis=0)[:, EIGS:]
    out_ref[...] = jnp.dot(
        inverse, smoothed_ref[...], precision=lax.Precision.HIGHEST, preferred_element_type=jnp.float32
    )


def solve(gram, smoothed):
    return pl.pallas_call(
        solve_kernel,
        out_shape=jax.ShapeDtypeStruct(smoothed.shape, jnp.float32),
        in_specs=[pl.BlockSpec(memory_space=pltpu.VMEM)] * 2,
        out_specs=pl.BlockSpec(memory_space=pltpu.VMEM),
        name="solve",
    )(gram, smoothed)


def per_device(embeddings, vectors, block_pairs):
    here_row = lax.axis_index("row")
    here_col = lax.axis_index("col")
    here_y, here_x = here_row // SIDE, here_row % SIDE
    blocks = embeddings.reshape(COLS, BLOCK, WIDTH)

    def move(array, dy, dx, keep=None):
        return lax.ppermute(array, "row", shift(dy, dx, keep))

    def turn(array, by):
        return lax.ppermute(array, "col", [(i, (i + by * CORES) % COLS) for i in range(COLS)])

    def swap(array):
        return lax.ppermute(array, "col", [(i, i ^ 1) for i in range(COLS)])

    far = {"own": make_payload(here_col[None], blocks, vectors)}
    far["a"] = move(far["own"], 0, 1)
    far["b"] = move(far["own"], 1, 0)
    far["c"] = move(far["own"], -1, -1)
    far_ids, works = [], []
    for (dy, dx), keep in STAGES.values():
        from_row = (here_y - dy) % SIDE * SIDE + (here_x - dx) % SIDE
        far_ids.append(from_row * COLS + here_col)
        works.append(jnp.broadcast_to(True if keep is None else keep(here_y, here_x), (COLS,)))
    far_ids = jnp.stack(far_ids)[:, None]
    near_ids = (here_row * COLS + jnp.arange(COLS, dtype=jnp.int32))[None, :]
    wanted = jnp.stack([near_ids * NBLOCKS + far_ids, far_ids * NBLOCKS + near_ids])
    listed = block_pairs[:, 0] * NBLOCKS + block_pairs[:, 1]
    found = jnp.any(wanted[..., None] == listed, axis=-1)
    both_ways = (jnp.arange(len(STAGES)) > 0)[:, None]
    flags = jnp.where(jnp.stack(works), found[0] + 2 * (found[1] & both_ways), 0).astype(jnp.int32)

    starts = {name: at for at, name in enumerate(STAGES)}

    def work(group, sums):
        at = starts[group[0]]
        return cells(
            flags[at : at + len(group)].reshape(-1),
            blocks,
            near_v,
            [far[name] for name in group],
            norms,
            rows,
            sums,
        )

    def give_back(group, parts):
        returned = []
        for name, part in zip(group, parts):
            back = [(to, source) for source, to in shift(*STAGES[name][0], STAGES[name][1])]
            returned.append(lax.ppermute(part, "row", back))
        return returned

    near_v = lax.all_to_all(jnp.broadcast_to(vectors, (COLS, EIGS, BLOCK)), "col", 0, 0)
    sums, norms, rows, token = own_cells(flags[0], blocks, far["own"])

    far["a"], far["b"], far["c"] = tie([far["a"], far["b"], far["c"]], token, near_v)
    far["h"] = move(far["b"], 1, 0)
    far["e"] = move(far["c"], 0, -1)
    far["d"] = move(far["a"], -1, 0)
    far["g"] = move(far["a"], 0, 1, left_half)
    group1, group2, group3 = ("a", "b", "c"), ("d", "e", "h"), ("f", "g", "k")
    sums, parts, token = work(group1, sums)

    far["h"], far["e"], *parts = tie([far["h"], far["e"], *parts], token, far["d"], far["g"])
    far["f"] = move(far["h"], 0, 1)
    far["k"] = move(far["e"], -1, 0, top_half)
    returned = give_back(("a",), parts[0:1])
    later = parts[1:]
    sums, parts, token = work(group2, sums)

    far["f"], far["k"], *parts = tie([far["f"], far["k"], *later, *parts], *returned)
    returned += give_back(("b", "c", *group2), parts)
    sums, parts, token = work(group3, sums)

    sums, *parts = tie([sums, *parts], *returned[1:])
    returned += give_back(group3, parts)

    high = lax.reduce_precision(sums, 8, 7)
    sent = jnp.concatenate([high, sums[:, EIGS:ACC] - high[:, EIGS:ACC]], axis=1).astype(jnp.bfloat16)
    summed = jnp.sum(lax.all_to_all(sent, "col", 0, 0).astype(jnp.float32), axis=0)
    totals, degrees = summed[0:EIGS], summed[EIGS : EIGS + 1] + summed[ACC : ACC + 1]
    for part in returned:
        part = part.astype(jnp.float32)
        totals, degrees = totals + part[0:EIGS], degrees + (part[EIGS : EIGS + 1] + part[ACC : ACC + 1])
    smoothed = totals / degrees
    gram = jnp.dot(
        smoothed, smoothed.T, precision=lax.Precision.HIGHEST, preferred_element_type=jnp.float32
    ) / (BLOCK * NBLOCKS)
    gram = gram + swap(gram)
    gram = gram + (turn(gram, 1) + turn(gram, 2) + turn(gram, 3))
    everyone = jnp.broadcast_to(gram, (SIDE * SIDE, EIGS, EIGS))
    gram = jnp.sum(lax.all_to_all(everyone, "row", 0, 0), axis=0)
    return solve(gram, smoothed)


def solution(mesh):
    return jax.shard_map(
        per_device,
        mesh=mesh,
        in_specs=(P("row", None), P(None, ("row", "col")), P()),
        out_specs=P(None, ("row", "col")),
        check_vma=False,
    )
```

```python
import functools
import math

import jax
import jax.numpy as jnp
from jax import lax
from jax.experimental import pallas as pl
from jax.experimental.pallas import tpu as pltpu
from jax.sharding import PartitionSpec as P

BLOCK = 512
WIDTH = 1024
EIGS = 64
NBLOCKS = 128
SIDE = 4
COLS = 8
CORES = 2
VROWS = BLOCK + EIGS // 2
PAYLOAD = VROWS + 16
ACC = EIGS + 8
SENT = EIGS + 16
SCALE = math.sqrt(math.log2(math.e) / math.sqrt(WIDTH))
COST = 8
NT = (((1,), (1,)), ((), ()))


def shift(dy, dx, keep=None):
    pairs = []
    for y in range(SIDE):
        for x in range(SIDE):
            to_y, to_x = (y + dy) % SIDE, (x + dx) % SIDE
            if keep is None or keep(to_y, to_x):
                pairs.append((y * SIDE + x, to_y * SIDE + to_x))
    return pairs


def left_half(y, x):
    return x < SIDE // 2


def top_half(y, x):
    return y < SIDE // 2


STAGES = {
    "own": ((0, 0), None),
    "a": ((0, 1), None),
    "b": ((1, 0), None),
    "c": ((-1, -1), None),
    "d": ((-1, 1), None),
    "e": ((-1, -2), None),
    "h": ((2, 0), top_half),
    "f": ((2, 1), None),
    "g": ((0, 2), left_half),
    "k": ((2, 2), top_half),
}


def row_norm(x):
    return lax.rsqrt(jnp.sum(x * x, axis=1, keepdims=True) * (1.0 / WIDTH) + 1e-06)


def payload_kernel(index_ref, x_ref, v_ref, out_ref):
    x = x_ref[0]
    out_ref[0:BLOCK, :] = x
    half = EIGS // 2
    out_ref[BLOCK:VROWS, 0:BLOCK] = v_ref[0:half, :]
    out_ref[BLOCK:VROWS, BLOCK : 2 * BLOCK] = v_ref[half:EIGS, :]
    norms = jnp.broadcast_to(row_norm(x.astype(jnp.float32)) * SCALE, (BLOCK, 128))
    rows = norms.T[0:16, :]
    high = rows.astype(jnp.bfloat16)
    low = (rows - high.astype(jnp.float32)).astype(jnp.bfloat16)
    out_ref[VROWS:PAYLOAD, 0:BLOCK] = high
    out_ref[VROWS:PAYLOAD, BLOCK : 2 * BLOCK] = low


def make_payload(here_col, blocks, vectors):
    return pl.pallas_call(
        payload_kernel,
        out_shape=jax.ShapeDtypeStruct((PAYLOAD, WIDTH), jnp.bfloat16),
        grid_spec=pltpu.PrefetchScalarGridSpec(
            num_scalar_prefetch=1,
            grid=(1,),
            in_specs=[
                pl.BlockSpec((1, BLOCK, WIDTH), lambda g, index: (index[0], 0, 0)),
                pl.BlockSpec((EIGS, BLOCK), lambda g, index: (0, 0)),
            ],
            out_specs=pl.BlockSpec((PAYLOAD, WIDTH), lambda g, index: (0, 0)),
        ),
        name="payload",
    )(here_col, blocks, vectors)


def side_vectors(side):
    half = EIGS // 2
    ones = jnp.ones((16, BLOCK), jnp.bfloat16)
    return jnp.concatenate([side[0:half, 0:BLOCK], side[0:half, BLOCK : 2 * BLOCK], ones], axis=0)


def side_norms(side):
    row = side[EIGS // 2 : EIGS // 2 + 1, :].astype(jnp.float32)
    return row[:, 0:BLOCK] + row[:, BLOCK : 2 * BLOCK]


def double(columns):
    return jnp.concatenate([columns, columns], axis=1)


def own_kernel(flags_ref, x_ref, far_ref, new_ref, norm_ref, row_ref, token_ref, p_ref):
    step = pl.program_id(0)
    new_ref[...] = jnp.zeros_like(new_ref)
    token_ref[...] = jnp.zeros_like(token_ref)
    norms = jnp.broadcast_to(row_norm(x_ref[0].astype(jnp.float32)) * SCALE, (BLOCK, 128))
    norm_ref[0] = norms
    row_ref[0] = norms.T[0:8, :]

    @pl.when(flags_ref[step] > 0)
    def _():
        side = far_ref[BLOCK:PAYLOAD, :]
        near, far = double(norm_ref[0]), side_norms(side)
        for at in range(0, BLOCK, 256):
            scores = lax.dot_general(
                x_ref[0], far_ref[at : at + 256, :], NT, preferred_element_type=jnp.float32
            )
            p_ref[:, at : at + 256] = jnp.exp2(scores * near * far[:, at : at + 256]).astype(jnp.bfloat16)
        part = lax.dot_general(side_vectors(side), p_ref[...], NT, preferred_element_type=jnp.float32)
        new_ref[0] = part[0:ACC, :]


def cells_kernel(count, flags_ref, x_hbm, v_hbm, *refs):
    far_hbms, (norm_hbm, row_hbm, old_hbm, new_hbm), refs = refs[:count], refs[count : count + 4], refs[count + 4 :]
    sent_refs, token_ref, refs = refs[:count], refs[count], refs[count + 1 :]
    x_ref, v_ref, far_ref, norm_ref, row_ref, old_ref, sums_ref, p_ref, column_ref, far_sums_ref = refs[:10]
    near_sem, far_sem, sem = refs[10:]

    def near_copies(near):
        pairs = ((x_hbm, x_ref), (norm_hbm, norm_ref), (v_hbm, v_ref))
        return [
            pltpu.make_async_copy(source.at[near], to.at[near], near_sem.at[at, near])
            for at, (source, to) in enumerate(pairs)
        ]

    far_copies = [pltpu.make_async_copy(far_hbms[at], far_ref.at[at], far_sem.at[at]) for at in range(count)]
    row_copy = pltpu.make_async_copy(row_hbm, row_ref, sem.at[0])
    old_copy = pltpu.make_async_copy(old_hbm, old_ref, sem.at[1])
    for copy in (far_copies[0], *near_copies(0), row_copy, *far_copies[1:], *near_copies(1), old_copy):
        copy.start()

    token_ref[...] = jnp.zeros_like(token_ref)
    far_sums_ref[...] = jnp.zeros_like(far_sums_ref)
    sums_ref[...] = jnp.zeros_like(sums_ref)

    def forward_only(at, near):
        rows, far = row_ref[near, 0:1, :], double(column_ref[at])
        for to in range(0, BLOCK, 256):
            scores = lax.dot_general(
                far_ref[at, 0:BLOCK, :], x_ref[near, to : to + 256, :], NT, preferred_element_type=jnp.float32
            )
            p_ref[:, to : to + 256] = jnp.exp2(scores * rows[:, to : to + 256] * far).astype(jnp.bfloat16)
        part = jnp.dot(side_vectors(far_ref[at, BLOCK:PAYLOAD, :]), p_ref[...], preferred_element_type=jnp.float32)
        sums_ref[near] += part[0:ACC, :]

    def backward(at, near, both):
        side = far_ref[at, BLOCK:PAYLOAD, :]
        columns, far = double(norm_ref[near]), side_norms(side)
        for to in range(0, BLOCK, 256):
            scores = lax.dot_general(
                x_ref[near], far_ref[at, to : to + 256, :], NT, preferred_element_type=jnp.float32
            )
            p_ref[:, to : to + 256] = jnp.exp2(scores * columns * far[:, to : to + 256]).astype(jnp.bfloat16)
        vectors = jnp.concatenate([v_ref[near], jnp.ones((16, BLOCK), jnp.bfloat16)], axis=0)
        part = jnp.dot(vectors, p_ref[...], preferred_element_type=jnp.float32)
        far_sums_ref[at] += part[0:ACC, :]
        if both:
            part = lax.dot_general(side_vectors(side), p_ref[...], NT, preferred_element_type=jnp.float32)
            sums_ref[near] += part[0:ACC, :]

    @pl.loop(0, COLS)
    def _(near):
        @pl.when(near + 2 < COLS)
        def _():
            for copy in near_copies(near + 2):
                copy.start()

        for copy in near_copies(near):
            copy.wait()

        @pl.when(near == 0)
        def _():
            row_copy.wait()

        @pl.loop(0, count)
        def _(at):
            @pl.when(near == 0)
            def _():
                pltpu.make_async_copy(far_hbms[0], far_ref.at[at], far_sem.at[at]).wait()
                column_ref[at] = jnp.broadcast_to(side_norms(far_ref[at, BLOCK:PAYLOAD, :]), (128, BLOCK)).T

            flag = flags_ref[at * COLS + near]
            pl.when(flag == 1)(functools.partial(forward_only, at, near))
            pl.when(flag == 2)(functools.partial(backward, at, near, False))
            pl.when(flag == 3)(functools.partial(backward, at, near, True))

    old_copy.wait()
    sums_ref[...] += old_ref[...]
    out_copy = pltpu.make_async_copy(sums_ref, new_hbm, sem.at[0])
    out_copy.start()
    for at in range(count):
        degrees = far_sums_ref[at, EIGS:ACC, :]
        high = degrees.astype(jnp.bfloat16).astype(jnp.float32)
        sent = jnp.concatenate([far_sums_ref[at, 0:EIGS, :], high, degrees - high], axis=0)
        sent_refs[at][...] = sent.astype(jnp.bfloat16)
    out_copy.wait()


SUMS = jax.ShapeDtypeStruct((COLS, ACC, BLOCK), jnp.float32)
NORM = jax.ShapeDtypeStruct((COLS, BLOCK, 128), jnp.float32)
ROW = jax.ShapeDtypeStruct((COLS, 8, BLOCK), jnp.float32)
TOKEN = jax.ShapeDtypeStruct((8, 128), jnp.float32)
SENT_SHAPE = jax.ShapeDtypeStruct((SENT, BLOCK), jnp.bfloat16)


def block_of(shape):
    return pl.BlockSpec((1, *shape[1:]), lambda g, flags: (g, 0, 0))


def whole(shape):
    return pl.BlockSpec(shape, lambda g, flags: (0, 0))


def own_cells(flags, blocks, far):
    return pl.pallas_call(
        own_kernel,
        out_shape=[SUMS, NORM, ROW, TOKEN],
        grid_spec=pltpu.PrefetchScalarGridSpec(
            num_scalar_prefetch=1,
            grid=(COLS,),
            in_specs=[block_of(blocks.shape), whole(far.shape)],
            out_specs=[block_of(SUMS.shape), block_of(NORM.shape), block_of(ROW.shape), whole(TOKEN.shape)],
            scratch_shapes=[pltpu.VMEM((BLOCK, BLOCK), jnp.bfloat16)],
        ),
        compiler_params=pltpu.CompilerParams(vmem_limit_bytes=56 << 20),
        cost_estimate=estimate(1),
        name="cells_own",
    )(flags, blocks, far)


def estimate(count):
    return pl.CostEstimate(
        flops=count * COST * BLOCK * BLOCK * WIDTH,
        bytes_accessed=(12 + count) << 20,
        transcendentals=count * 4 * BLOCK * BLOCK,
    )


def cells(flags, blocks, near_v, fars, norms, rows, sums):
    count = len(fars)
    buffers = [
        ((COLS, BLOCK, WIDTH), jnp.bfloat16),
        ((COLS, EIGS, BLOCK), jnp.bfloat16),
        ((count, PAYLOAD, WIDTH), jnp.bfloat16),
        ((COLS, BLOCK, 128), jnp.float32),
        ((COLS, 8, BLOCK), jnp.float32),
        ((COLS, ACC, BLOCK), jnp.float32),
        ((COLS, ACC, BLOCK), jnp.float32),
        ((BLOCK, BLOCK), jnp.bfloat16),
        ((count, BLOCK, 128), jnp.float32),
        ((count, ACC, BLOCK), jnp.float32),
    ]
    in_place = pl.BlockSpec(memory_space=pltpu.HBM)
    result = pl.pallas_call(
        functools.partial(cells_kernel, count),
        out_shape=[SUMS] + [SENT_SHAPE] * count + [TOKEN],
        grid_spec=pltpu.PrefetchScalarGridSpec(
            num_scalar_prefetch=1,
            grid=(1,),
            in_specs=[in_place] * (5 + count),
            out_specs=[in_place] + [whole(SENT_SHAPE.shape)] * count + [whole(TOKEN.shape)],
            scratch_shapes=[pltpu.VMEM(*buffer) for buffer in buffers]
            + [pltpu.SemaphoreType.DMA(size) for size in ((3, COLS), (count,), (2,))],
        ),
        input_output_aliases={5 + count: 0},
        compiler_params=pltpu.CompilerParams(vmem_limit_bytes=56 << 20),
        cost_estimate=estimate(count),
        name="cells",
    )(flags, blocks, near_v, *fars, norms, rows, sums)
    return result[0], result[1:-1], result[-1]


def tie_kernel(*refs):
    pass


def tie(arrays, *tokens):
    return pl.pallas_call(
        tie_kernel,
        out_shape=[jax.ShapeDtypeStruct(array.shape, array.dtype) for array in arrays],
        in_specs=[pl.BlockSpec(memory_space=pltpu.HBM)] * (len(arrays) + len(tokens)),
        out_specs=[pl.BlockSpec(memory_space=pltpu.HBM)] * len(arrays),
        input_output_aliases={at: at for at in range(len(arrays))},
        name="tie",
    )(*arrays, *tokens)


def solve_kernel(gram_ref, smoothed_ref, out_ref):
    rows = lax.broadcasted_iota(jnp.int32, (EIGS, 2 * EIGS), 0)
    lanes = lax.broadcasted_iota(jnp.int32, (EIGS, 2 * EIGS), 1)
    eye = jnp.where(rows + EIGS == lanes, 1.0, 0.0)[:, EIGS:]
    work = jnp.concatenate([gram_ref[...], eye], axis=1)
    below = rows[0:8, :]
    tiles, done = [work[at : at + 8, :] for at in range(0, EIGS, 8)], []
    while tiles:
        for j in range(0, 8, 2):
            at = len(done) * 8 + j
            columns1 = [jnp.broadcast_to(tile[:, at : at + 1], tile.shape) for tile in tiles]
            columns2 = [jnp.broadcast_to(tile[:, at + 1 : at + 2], tile.shape) for tile in tiles]
            first, cross = columns1[0][j : j + 1, :], columns1[0][j + 1 : j + 2, :]
            second = columns2[0][j + 1 : j + 2, :]
            row1, row2 = tiles[0][j : j + 1, :], tiles[0][j + 1 : j + 2, :]
            scale = 1.0 / (first * second - cross * cross)
            scaled1 = (second * row1 - cross * row2) * scale
            scaled2 = (first * row2 - cross * row1) * scale
            ratio = cross / first
            columns1[0] = jnp.where(below > j + 1, columns1[0], 0.0)
            columns2[0] = jnp.where(below > j + 1, columns2[0], 0.0)
            tiles = [
                tile - (column1 * scaled1 + column2 * scaled2)
                for tile, column1, column2 in zip(tiles, columns1, columns2)
            ]
            tiles[0] = jnp.where(below == j, row1 * lax.rsqrt(first), tiles[0])
            last = (row2 - ratio * row1) * lax.rsqrt(second - ratio * cross)
            tiles[0] = jnp.where(below == j + 1, last, tiles[0])
        done.append(tiles.pop(0))
    inverse = jnp.concatenate(done, axis=0)[:, EIGS:]
    out_ref[...] = jnp.dot(
        inverse, smoothed_ref[...], precision=lax.Precision.HIGHEST, preferred_element_type=jnp.float32
    )


def solve(gram, smoothed):
    return pl.pallas_call(
        solve_kernel,
        out_shape=jax.ShapeDtypeStruct(smoothed.shape, jnp.float32),
        in_specs=[pl.BlockSpec(memory_space=pltpu.VMEM)] * 2,
        out_specs=pl.BlockSpec(memory_space=pltpu.VMEM),
        name="solve",
    )(gram, smoothed)


def per_device(embeddings, vectors, block_pairs):
    here_row = lax.axis_index("row")
    here_col = lax.axis_index("col")
    here_y, here_x = here_row // SIDE, here_row % SIDE
    blocks = embeddings.reshape(COLS, BLOCK, WIDTH)

    def move(array, dy, dx, keep=None):
        return lax.ppermute(array, "row", shift(dy, dx, keep))

    def turn(array, by):
        return lax.ppermute(array, "col", [(i, (i + by * CORES) % COLS) for i in range(COLS)])

    def swap(array):
        return lax.ppermute(array, "col", [(i, i ^ 1) for i in range(COLS)])

    far = {"own": make_payload(here_col[None], blocks, vectors)}
    far["a"] = move(far["own"], 0, 1)
    far["b"] = move(far["own"], 1, 0)
    far["c"] = move(far["own"], -1, -1)
    far_ids, works = [], []
    for (dy, dx), keep in STAGES.values():
        from_row = (here_y - dy) % SIDE * SIDE + (here_x - dx) % SIDE
        far_ids.append(from_row * COLS + here_col)
        works.append(jnp.broadcast_to(True if keep is None else keep(here_y, here_x), (COLS,)))
    far_ids = jnp.stack(far_ids)[:, None]
    near_ids = (here_row * COLS + jnp.arange(COLS, dtype=jnp.int32))[None, :]
    wanted = jnp.stack([near_ids * NBLOCKS + far_ids, far_ids * NBLOCKS + near_ids])
    listed = block_pairs[:, 0] * NBLOCKS + block_pairs[:, 1]
    found = jnp.any(wanted[..., None] == listed, axis=-1)
    both_ways = (jnp.arange(len(STAGES)) > 0)[:, None]
    flags = jnp.where(jnp.stack(works), found[0] + 2 * (found[1] & both_ways), 0).astype(jnp.int32)

    starts = {name: at for at, name in enumerate(STAGES)}

    def work(group, sums):
        at = starts[group[0]]
        return cells(
            flags[at : at + len(group)].reshape(-1),
            blocks,
            near_v,
            [far[name] for name in group],
            norms,
            rows,
            sums,
        )

    def give_back(group, parts):
        returned = []
        for name, part in zip(group, parts):
            back = [(to, source) for source, to in shift(*STAGES[name][0], STAGES[name][1])]
            returned.append(lax.ppermute(part, "row", back))
        return returned

    near_v = lax.all_to_all(jnp.broadcast_to(vectors, (COLS, EIGS, BLOCK)), "col", 0, 0)
    sums, norms, rows, token = own_cells(flags[0], blocks, far["own"])

    far["a"], far["b"], far["c"] = tie([far["a"], far["b"], far["c"]], token, near_v)
    far["h"] = move(far["b"], 1, 0)
    far["e"] = move(far["c"], 0, -1)
    far["d"] = move(far["a"], -1, 0)
    far["g"] = move(far["a"], 0, 1, left_half)
    group1, group2, group3 = ("a", "b", "c"), ("d", "e", "h"), ("f", "g", "k")
    sums, parts, token = work(group1, sums)

    far["h"], far["e"], *parts = tie([far["h"], far["e"], *parts], token, far["g"])
    far["f"] = move(far["h"], 0, 1)
    far["k"] = move(far["e"], -1, 0, top_half)
    returned = give_back(("a",), parts[0:1])
    later = parts[1:]
    sums, parts, token = work(group2, sums)

    far["f"], far["k"], *parts = tie([far["f"], far["k"], *later, *parts], *returned)
    returned += give_back(("b", "c", *group2), parts)
    sums, parts, token = work(group3, sums)

    sums, *parts = tie([sums, *parts], *returned[1:])
    returned += give_back(group3, parts)

    layer, core = here_col // CORES, here_col % CORES
    halves = sums.reshape(SIDE, CORES, ACC, BLOCK)
    mine = lax.dynamic_index_in_dim(halves, core, 1, keepdims=False)
    kept = mine + swap(lax.dynamic_index_in_dim(halves, 1 - core, 1, keepdims=False))
    layers = [lax.dynamic_index_in_dim(kept, (layer - k) % SIDE, 0, keepdims=False) for k in range(SIDE)]
    summed = layers[0] + (turn(layers[1], 3) + turn(layers[2], 2) + turn(layers[3], 1))
    totals, degrees = summed[0:EIGS], summed[EIGS : EIGS + 1]
    for part in returned:
        part = part.astype(jnp.float32)
        totals, degrees = totals + part[0:EIGS], degrees + (part[EIGS : EIGS + 1] + part[ACC : ACC + 1])
    smoothed = totals / degrees
    gram = jnp.dot(
        smoothed, smoothed.T, precision=lax.Precision.HIGHEST, preferred_element_type=jnp.float32
    ) / (BLOCK * NBLOCKS)
    gram = gram + swap(gram)
    gram = gram + (turn(gram, 1) + turn(gram, 2) + turn(gram, 3))
    everyone = jnp.broadcast_to(gram, (SIDE * SIDE, EIGS, EIGS))
    gram = jnp.sum(lax.all_to_all(everyone, "row", 0, 0), axis=0)
    return solve(gram, smoothed)


def solution(mesh):
    return jax.shard_map(
        per_device,
        mesh=mesh,
        in_specs=(P("row", None), P(None, ("row", "col")), P()),
        out_specs=P(None, ("row", "col")),
        check_vma=False,
    )
```

```python
import functools
import math

import jax
import jax.numpy as jnp
from jax import lax
from jax.experimental import pallas as pl
from jax.experimental.pallas import tpu as pltpu
from jax.sharding import PartitionSpec as P

BLOCK = 512
WIDTH = 1024
EIGS = 64
NBLOCKS = 128
SIDE = 4
COLS = 8
CORES = 2
VROWS = BLOCK + EIGS // 2
PAYLOAD = VROWS + 16
ACC = EIGS + 8
SENT = EIGS + 16
SCALE = math.sqrt(math.log2(math.e) / math.sqrt(WIDTH))
COST = 8
NT = (((1,), (1,)), ((), ()))


def shift(dy, dx, keep=None):
    pairs = []
    for y in range(SIDE):
        for x in range(SIDE):
            to_y, to_x = (y + dy) % SIDE, (x + dx) % SIDE
            if keep is None or keep(to_y, to_x):
                pairs.append((y * SIDE + x, to_y * SIDE + to_x))
    return pairs


def left_half(y, x):
    return x < SIDE // 2


def top_half(y, x):
    return y < SIDE // 2


STAGES = {
    "own": ((0, 0), None),
    "a": ((0, 1), None),
    "b": ((1, 0), None),
    "c": ((-1, -1), None),
    "d": ((-1, 1), None),
    "e": ((-1, -2), None),
    "h": ((2, 0), top_half),
    "f": ((2, 1), None),
    "g": ((0, 2), left_half),
    "k": ((2, 2), top_half),
}


def row_norm(x):
    return lax.rsqrt(jnp.sum(x * x, axis=1, keepdims=True) * (1.0 / WIDTH) + 1e-06)


def payload_kernel(index_ref, x_ref, v_ref, out_ref):
    x = x_ref[0]
    out_ref[0:BLOCK, :] = x
    half = EIGS // 2
    out_ref[BLOCK:VROWS, 0:BLOCK] = v_ref[0:half, :]
    out_ref[BLOCK:VROWS, BLOCK : 2 * BLOCK] = v_ref[half:EIGS, :]
    norms = jnp.broadcast_to(row_norm(x.astype(jnp.float32)) * SCALE, (BLOCK, 128))
    rows = norms.T[0:16, :]
    high = rows.astype(jnp.bfloat16)
    low = (rows - high.astype(jnp.float32)).astype(jnp.bfloat16)
    out_ref[VROWS:PAYLOAD, 0:BLOCK] = high
    out_ref[VROWS:PAYLOAD, BLOCK : 2 * BLOCK] = low


def make_payload(here_col, blocks, vectors):
    return pl.pallas_call(
        payload_kernel,
        out_shape=jax.ShapeDtypeStruct((PAYLOAD, WIDTH), jnp.bfloat16),
        grid_spec=pltpu.PrefetchScalarGridSpec(
            num_scalar_prefetch=1,
            grid=(1,),
            in_specs=[
                pl.BlockSpec((1, BLOCK, WIDTH), lambda g, index: (index[0], 0, 0)),
                pl.BlockSpec((EIGS, BLOCK), lambda g, index: (0, 0)),
            ],
            out_specs=pl.BlockSpec((PAYLOAD, WIDTH), lambda g, index: (0, 0)),
        ),
        name="payload",
    )(here_col, blocks, vectors)


def side_vectors(side):
    half = EIGS // 2
    ones = jnp.ones((16, BLOCK), jnp.bfloat16)
    return jnp.concatenate([side[0:half, 0:BLOCK], side[0:half, BLOCK : 2 * BLOCK], ones], axis=0)


def side_norms(side):
    row = side[EIGS // 2 : EIGS // 2 + 1, :].astype(jnp.float32)
    return row[:, 0:BLOCK] + row[:, BLOCK : 2 * BLOCK]


def double(columns):
    return jnp.concatenate([columns, columns], axis=1)


def own_kernel(flags_ref, x_ref, far_ref, new_ref, norm_ref, row_ref, token_ref, p_ref):
    step = pl.program_id(0)
    new_ref[...] = jnp.zeros_like(new_ref)
    token_ref[...] = jnp.zeros_like(token_ref)
    norms = jnp.broadcast_to(row_norm(x_ref[0].astype(jnp.float32)) * SCALE, (BLOCK, 128))
    norm_ref[0] = norms
    row_ref[0] = norms.T[0:8, :]

    @pl.when(flags_ref[step] > 0)
    def _():
        side = far_ref[BLOCK:PAYLOAD, :]
        near, far = double(norm_ref[0]), side_norms(side)
        for at in range(0, BLOCK, 256):
            scores = lax.dot_general(
                x_ref[0], far_ref[at : at + 256, :], NT, preferred_element_type=jnp.float32
            )
            p_ref[:, at : at + 256] = jnp.exp2(scores * near * far[:, at : at + 256]).astype(jnp.bfloat16)
        part = lax.dot_general(side_vectors(side), p_ref[...], NT, preferred_element_type=jnp.float32)
        new_ref[0] = part[0:ACC, :]


def cells_kernel(count, flags_ref, x_hbm, v_hbm, *refs):
    far_hbms, (norm_hbm, row_hbm, old_hbm, new_hbm), refs = refs[:count], refs[count : count + 4], refs[count + 4 :]
    sent_refs, token_ref, refs = refs[:count], refs[count], refs[count + 1 :]
    x_ref, v_ref, far_ref, norm_ref, row_ref, old_ref, sums_ref, p_ref, column_ref, far_sums_ref = refs[:10]
    near_sem, far_sem, sem = refs[10:]

    def near_copies(near):
        pairs = ((x_hbm, x_ref), (norm_hbm, norm_ref), (v_hbm, v_ref))
        return [
            pltpu.make_async_copy(source.at[near], to.at[near], near_sem.at[at, near])
            for at, (source, to) in enumerate(pairs)
        ]

    far_copies = [pltpu.make_async_copy(far_hbms[at], far_ref.at[at], far_sem.at[at]) for at in range(count)]
    row_copy = pltpu.make_async_copy(row_hbm, row_ref, sem.at[0])
    old_copy = pltpu.make_async_copy(old_hbm, old_ref, sem.at[1])
    for copy in (far_copies[0], *near_copies(0), row_copy, *far_copies[1:], *near_copies(1), old_copy):
        copy.start()

    token_ref[...] = jnp.zeros_like(token_ref)
    far_sums_ref[...] = jnp.zeros_like(far_sums_ref)
    sums_ref[...] = jnp.zeros_like(sums_ref)

    def forward_only(at, near):
        rows, far = row_ref[near, 0:1, :], double(column_ref[at])
        for to in range(0, BLOCK, 256):
            scores = lax.dot_general(
                far_ref[at, 0:BLOCK, :], x_ref[near, to : to + 256, :], NT, preferred_element_type=jnp.float32
            )
            p_ref[:, to : to + 256] = jnp.exp2(scores * rows[:, to : to + 256] * far).astype(jnp.bfloat16)
        part = jnp.dot(side_vectors(far_ref[at, BLOCK:PAYLOAD, :]), p_ref[...], preferred_element_type=jnp.float32)
        sums_ref[near] += part[0:ACC, :]

    def backward(at, near, both):
        side = far_ref[at, BLOCK:PAYLOAD, :]
        columns, far = double(norm_ref[near]), side_norms(side)
        for to in range(0, BLOCK, 256):
            scores = lax.dot_general(
                x_ref[near], far_ref[at, to : to + 256, :], NT, preferred_element_type=jnp.float32
            )
            p_ref[:, to : to + 256] = jnp.exp2(scores * columns * far[:, to : to + 256]).astype(jnp.bfloat16)
        vectors = jnp.concatenate([v_ref[near], jnp.ones((16, BLOCK), jnp.bfloat16)], axis=0)
        part = jnp.dot(vectors, p_ref[...], preferred_element_type=jnp.float32)
        far_sums_ref[at] += part[0:ACC, :]
        if both:
            part = lax.dot_general(side_vectors(side), p_ref[...], NT, preferred_element_type=jnp.float32)
            sums_ref[near] += part[0:ACC, :]

    @pl.loop(0, COLS)
    def _(near):
        @pl.when(near + 2 < COLS)
        def _():
            for copy in near_copies(near + 2):
                copy.start()

        for copy in near_copies(near):
            copy.wait()

        @pl.when(near == 0)
        def _():
            row_copy.wait()

        @pl.loop(0, count)
        def _(at):
            @pl.when(near == 0)
            def _():
                pltpu.make_async_copy(far_hbms[0], far_ref.at[at], far_sem.at[at]).wait()
                column_ref[at] = jnp.broadcast_to(side_norms(far_ref[at, BLOCK:PAYLOAD, :]), (128, BLOCK)).T

            flag = flags_ref[at * COLS + near]
            pl.when(flag == 1)(functools.partial(forward_only, at, near))
            pl.when(flag == 2)(functools.partial(backward, at, near, False))
            pl.when(flag == 3)(functools.partial(backward, at, near, True))

    old_copy.wait()
    sums_ref[...] += old_ref[...]
    out_copy = pltpu.make_async_copy(sums_ref, new_hbm, sem.at[0])
    out_copy.start()
    for at in range(count):
        degrees = far_sums_ref[at, EIGS:ACC, :]
        high = degrees.astype(jnp.bfloat16).astype(jnp.float32)
        sent = jnp.concatenate([far_sums_ref[at, 0:EIGS, :], high, degrees - high], axis=0)
        sent_refs[at][...] = sent.astype(jnp.bfloat16)
    out_copy.wait()


SUMS = jax.ShapeDtypeStruct((COLS, ACC, BLOCK), jnp.float32)
NORM = jax.ShapeDtypeStruct((COLS, BLOCK, 128), jnp.float32)
ROW = jax.ShapeDtypeStruct((COLS, 8, BLOCK), jnp.float32)
TOKEN = jax.ShapeDtypeStruct((8, 128), jnp.float32)
SENT_SHAPE = jax.ShapeDtypeStruct((SENT, BLOCK), jnp.bfloat16)


def block_of(shape):
    return pl.BlockSpec((1, *shape[1:]), lambda g, flags: (g, 0, 0))


def whole(shape):
    return pl.BlockSpec(shape, lambda g, flags: (0, 0))


def own_cells(flags, blocks, far):
    return pl.pallas_call(
        own_kernel,
        out_shape=[SUMS, NORM, ROW, TOKEN],
        grid_spec=pltpu.PrefetchScalarGridSpec(
            num_scalar_prefetch=1,
            grid=(COLS,),
            in_specs=[block_of(blocks.shape), whole(far.shape)],
            out_specs=[block_of(SUMS.shape), block_of(NORM.shape), block_of(ROW.shape), whole(TOKEN.shape)],
            scratch_shapes=[pltpu.VMEM((BLOCK, BLOCK), jnp.bfloat16)],
        ),
        compiler_params=pltpu.CompilerParams(vmem_limit_bytes=56 << 20),
        cost_estimate=estimate(1),
        name="cells_own",
    )(flags, blocks, far)


def estimate(count):
    return pl.CostEstimate(
        flops=count * COST * BLOCK * BLOCK * WIDTH,
        bytes_accessed=(12 + count) << 20,
        transcendentals=count * 4 * BLOCK * BLOCK,
    )


def cells(flags, blocks, near_v, fars, norms, rows, sums):
    count = len(fars)
    buffers = [
        ((COLS, BLOCK, WIDTH), jnp.bfloat16),
        ((COLS, EIGS, BLOCK), jnp.bfloat16),
        ((count, PAYLOAD, WIDTH), jnp.bfloat16),
        ((COLS, BLOCK, 128), jnp.float32),
        ((COLS, 8, BLOCK), jnp.float32),
        ((COLS, ACC, BLOCK), jnp.float32),
        ((COLS, ACC, BLOCK), jnp.float32),
        ((BLOCK, BLOCK), jnp.bfloat16),
        ((count, BLOCK, 128), jnp.float32),
        ((count, ACC, BLOCK), jnp.float32),
    ]
    in_place = pl.BlockSpec(memory_space=pltpu.HBM)
    result = pl.pallas_call(
        functools.partial(cells_kernel, count),
        out_shape=[SUMS] + [SENT_SHAPE] * count + [TOKEN],
        grid_spec=pltpu.PrefetchScalarGridSpec(
            num_scalar_prefetch=1,
            grid=(1,),
            in_specs=[in_place] * (5 + count),
            out_specs=[in_place] + [whole(SENT_SHAPE.shape)] * count + [whole(TOKEN.shape)],
            scratch_shapes=[pltpu.VMEM(*buffer) for buffer in buffers]
            + [pltpu.SemaphoreType.DMA(size) for size in ((3, COLS), (count,), (2,))],
        ),
        input_output_aliases={5 + count: 0},
        compiler_params=pltpu.CompilerParams(vmem_limit_bytes=56 << 20),
        cost_estimate=estimate(count),
        name="cells",
    )(flags, blocks, near_v, *fars, norms, rows, sums)
    return result[0], result[1:-1], result[-1]


def tie_kernel(*refs):
    pass


def tie(arrays, *tokens):
    return pl.pallas_call(
        tie_kernel,
        out_shape=[jax.ShapeDtypeStruct(array.shape, array.dtype) for array in arrays],
        in_specs=[pl.BlockSpec(memory_space=pltpu.HBM)] * (len(arrays) + len(tokens)),
        out_specs=[pl.BlockSpec(memory_space=pltpu.HBM)] * len(arrays),
        input_output_aliases={at: at for at in range(len(arrays))},
        name="tie",
    )(*arrays, *tokens)


def solve_kernel(gram_ref, smoothed_ref, out_ref):
    rows = lax.broadcasted_iota(jnp.int32, (EIGS, 2 * EIGS), 0)
    lanes = lax.broadcasted_iota(jnp.int32, (EIGS, 2 * EIGS), 1)
    eye = jnp.where(rows + EIGS == lanes, 1.0, 0.0)[:, EIGS:]
    work = jnp.concatenate([gram_ref[...], eye], axis=1)
    below = rows[0:8, :]
    tiles, done = [work[at : at + 8, :] for at in range(0, EIGS, 8)], []
    while tiles:
        for j in range(0, 8, 2):
            at = len(done) * 8 + j
            columns1 = [jnp.broadcast_to(tile[:, at : at + 1], tile.shape) for tile in tiles]
            columns2 = [jnp.broadcast_to(tile[:, at + 1 : at + 2], tile.shape) for tile in tiles]
            first, cross = columns1[0][j : j + 1, :], columns1[0][j + 1 : j + 2, :]
            second = columns2[0][j + 1 : j + 2, :]
            row1, row2 = tiles[0][j : j + 1, :], tiles[0][j + 1 : j + 2, :]
            scale = 1.0 / (first * second - cross * cross)
            scaled1 = (second * row1 - cross * row2) * scale
            scaled2 = (first * row2 - cross * row1) * scale
            ratio = cross / first
            columns1[0] = jnp.where(below > j + 1, columns1[0], 0.0)
            columns2[0] = jnp.where(below > j + 1, columns2[0], 0.0)
            tiles = [
                tile - (column1 * scaled1 + column2 * scaled2)
                for tile, column1, column2 in zip(tiles, columns1, columns2)
            ]
            tiles[0] = jnp.where(below == j, row1 * lax.rsqrt(first), tiles[0])
            last = (row2 - ratio * row1) * lax.rsqrt(second - ratio * cross)
            tiles[0] = jnp.where(below == j + 1, last, tiles[0])
        done.append(tiles.pop(0))
    inverse = jnp.concatenate(done, axis=0)[:, EIGS:]
    out_ref[...] = jnp.dot(
        inverse, smoothed_ref[...], precision=lax.Precision.HIGHEST, preferred_element_type=jnp.float32
    )


def solve(gram, smoothed):
    return pl.pallas_call(
        solve_kernel,
        out_shape=jax.ShapeDtypeStruct(smoothed.shape, jnp.float32),
        in_specs=[pl.BlockSpec(memory_space=pltpu.VMEM)] * 2,
        out_specs=pl.BlockSpec(memory_space=pltpu.VMEM),
        name="solve",
    )(gram, smoothed)


def per_device(embeddings, vectors, block_pairs):
    here_row = lax.axis_index("row")
    here_col = lax.axis_index("col")
    here_y, here_x = here_row // SIDE, here_row % SIDE
    blocks = embeddings.reshape(COLS, BLOCK, WIDTH)

    def move(array, dy, dx, keep=None):
        return lax.ppermute(array, "row", shift(dy, dx, keep))

    def turn(array, by):
        return lax.ppermute(array, "col", [(i, (i + by * CORES) % COLS) for i in range(COLS)])

    def swap(array):
        return lax.ppermute(array, "col", [(i, i ^ 1) for i in range(COLS)])

    far = {"own": make_payload(here_col[None], blocks, vectors)}
    far["a"] = move(far["own"], 0, 1)
    far["b"] = move(far["own"], 1, 0)
    far["c"] = move(far["own"], -1, -1)
    far_ids, works = [], []
    for (dy, dx), keep in STAGES.values():
        from_row = (here_y - dy) % SIDE * SIDE + (here_x - dx) % SIDE
        far_ids.append(from_row * COLS + here_col)
        works.append(jnp.broadcast_to(True if keep is None else keep(here_y, here_x), (COLS,)))
    far_ids = jnp.stack(far_ids)[:, None]
    near_ids = (here_row * COLS + jnp.arange(COLS, dtype=jnp.int32))[None, :]
    wanted = jnp.stack([near_ids * NBLOCKS + far_ids, far_ids * NBLOCKS + near_ids])
    listed = block_pairs[:, 0] * NBLOCKS + block_pairs[:, 1]
    found = jnp.any(wanted[..., None] == listed, axis=-1)
    both_ways = (jnp.arange(len(STAGES)) > 0)[:, None]
    flags = jnp.where(jnp.stack(works), found[0] + 2 * (found[1] & both_ways), 0).astype(jnp.int32)

    starts = {name: at for at, name in enumerate(STAGES)}

    def work(group, sums):
        at = starts[group[0]]
        return cells(
            flags[at : at + len(group)].reshape(-1),
            blocks,
            near_v,
            [far[name] for name in group],
            norms,
            rows,
            sums,
        )

    def give_back(group, parts):
        returned = []
        for name, part in zip(group, parts):
            back = [(to, source) for source, to in shift(*STAGES[name][0], STAGES[name][1])]
            returned.append(lax.ppermute(part, "row", back))
        return returned

    near_v = lax.all_to_all(jnp.broadcast_to(vectors, (COLS, EIGS, BLOCK)), "col", 0, 0)
    sums, norms, rows, token = own_cells(flags[0], blocks, far["own"])

    far["a"], far["b"], far["c"] = tie([far["a"], far["b"], far["c"]], token, near_v)
    far["h"] = move(far["b"], 1, 0)
    far["e"] = move(far["c"], 0, -1)
    far["d"] = move(far["a"], -1, 0)
    far["g"] = move(far["a"], 0, 1, left_half)
    group1, group2, group3 = ("a", "b", "c"), ("d", "e", "h"), ("f", "g", "k")
    sums, parts, token = work(group1, sums)

    far["h"], far["e"], *parts = tie([far["h"], far["e"], *parts], token, far["g"])
    far["f"] = move(far["h"], 0, 1)
    far["k"] = move(far["e"], -1, 0, top_half)
    returned = give_back(("a",), parts[0:1])
    later = parts[1:]
    sums, parts, token = work(group2, sums)

    ready = tie([*later, parts[0]], *returned, token)
    returned += give_back(("b", "c", "d"), ready)
    far["f"], far["k"], *parts = tie([far["f"], far["k"], *parts[1:]], ready[0])
    returned += give_back(("e", "h"), parts)
    sums, parts, token = work(group3, sums)

    sums, *parts = tie([sums, *parts], *returned[1:])
    returned += give_back(group3, parts)

    layer, core = here_col // CORES, here_col % CORES
    halves = sums.reshape(SIDE, CORES, ACC, BLOCK)
    mine = lax.dynamic_index_in_dim(halves, core, 1, keepdims=False)
    kept = mine + swap(lax.dynamic_index_in_dim(halves, 1 - core, 1, keepdims=False))
    layers = [lax.dynamic_index_in_dim(kept, (layer - k) % SIDE, 0, keepdims=False) for k in range(SIDE)]
    summed = layers[0] + (turn(layers[1], 3) + turn(layers[2], 2) + turn(layers[3], 1))
    totals, degrees = summed[0:EIGS], summed[EIGS : EIGS + 1]
    for part in returned:
        part = part.astype(jnp.float32)
        totals, degrees = totals + part[0:EIGS], degrees + (part[EIGS : EIGS + 1] + part[ACC : ACC + 1])
    smoothed = totals / degrees
    gram = jnp.dot(
        smoothed, smoothed.T, precision=lax.Precision.HIGHEST, preferred_element_type=jnp.float32
    ) / (BLOCK * NBLOCKS)
    gram = gram + swap(gram)
    gram = gram + (turn(gram, 1) + turn(gram, 2) + turn(gram, 3))
    everyone = jnp.broadcast_to(gram, (SIDE * SIDE, EIGS, EIGS))
    gram = jnp.sum(lax.all_to_all(everyone, "row", 0, 0), axis=0)
    return solve(gram, smoothed)


def solution(mesh):
    return jax.shard_map(
        per_device,
        mesh=mesh,
        in_specs=(P("row", None), P(None, ("row", "col")), P()),
        out_specs=P(None, ("row", "col")),
        check_vma=False,
    )
```
